32 devices in a mesh: dp: 8 (over y, x, core), tensor: 4 (over z).
Axes of the slice: x: 2, y: 2, z: 4, core: 2. Of those that a mesh axis runs over, the one named last changes fastest.
Arguments:
- tokens: bfloat16 [8192, 768], P(('dp', 'tensor')), may hold values from -60 to 60
- encoder: bfloat16 [4096, 768], P(('dp', 'tensor')), may hold values from -6 to 6
- segments: int32 [8, 1024], P('dp'), may hold values from 0 to 5, never falling along the last dimension, each value on 1 to 800 neighbouring positions
- rel_bucket: int32 [1024], replicated, may hold values from 0 to 31
- out_grad: bfloat16 [8192, 768], P(('dp', 'tensor')), may hold values from -6 to 6
- self_q: bfloat16 [768, 768], P('dp', 'tensor'), may hold values from -0.109375 to 0.109375
- self_k: bfloat16 [768, 768], P('dp', 'tensor'), may hold values from -0.109375 to 0.109375
- self_v: bfloat16 [768, 768], P('dp', 'tensor'), may hold values from -0.21875 to 0.21875
- self_o: bfloat16 [768, 768], P('tensor', 'dp'), may hold values from -0.875 to 0.875
- cross_q: bfloat16 [768, 768], P('dp', 'tensor'), may hold values from -0.109375 to 0.109375
- cross_k: bfloat16 [768, 768], P('dp', 'tensor'), may hold values from -0.109375 to 0.109375
- cross_v: bfloat16 [768, 768], P('dp', 'tensor'), may hold values from -0.21875 to 0.21875
- cross_o: bfloat16 [768, 768], P('tensor', 'dp'), may hold values from -0.875 to 0.875
- ffn_gate: bfloat16 [768, 2048], P('dp', 'tensor'), may hold values from -0.21875 to 0.21875
- ffn_up: bfloat16 [768, 2048], P('dp', 'tensor'), may hold values from -0.21875 to 0.21875
- ffn_down: bfloat16 [2048, 768], P('tensor', 'dp'), may hold values from -0.125 to 0.125
- bias_table: bfloat16 [32, 12], P(None, 'tensor'), may hold values from -3 to 3
- norm_gains: bfloat16 [3, 768], P(None, 'dp'), may hold values from 0.5 to 1.5
Outputs:
- layer_out: bfloat16 [8192, 768], P(('dp', 'tensor'))
- tokens_grad: float32 [8192, 768], P(('dp', 'tensor'))
- encoder_grad: float32 [4096, 768], P(('dp', 'tensor'))
- self_q_grad: float32 [768, 768], P('dp', 'tensor')
- self_k_grad: float32 [768, 768], P('dp', 'tensor')
- self_v_grad: float32 [768, 768], P('dp', 'tensor')
- self_o_grad: float32 [768, 768], P('tensor', 'dp')
- cross_q_grad: float32 [768, 768], P('dp', 'tensor')
- cross_k_grad: float32 [768, 768], P('dp', 'tensor')
- cross_v_grad: float32 [768, 768], P('dp', 'tensor')
- cross_o_grad: float32 [768, 768], P('tensor', 'dp')
- ffn_gate_grad: float32 [768, 2048], P('dp', 'tensor')
- ffn_up_grad: float32 [768, 2048], P('dp', 'tensor')
- ffn_down_grad: float32 [2048, 768], P('tensor', 'dp')
- bias_table_grad: float32 [32, 12], P(None, 'tensor')
- norm_gains_grad: float32 [3, 768], P(None, 'dp')
The draws below stay inside these ranges and needn't reach their ends.
Inputs may be any that keep to these rules, and one draw needn't show every extreme that they name: `segments`: within each sequence the numbers never fall; every document holds at most 800 tokens and some holds exactly 800.
All inputs are finite; a program needn't handle non-finite values.
Results may differ from the reference program's by a relative error of at most 0.04.
Values may be sent and summed in bfloat16 or wider, within the bound.
A program may use at most 192 MiB of HBM per device.

```python
import math
import jax
import jax.numpy as jnp
import numpy as np
from jax import lax

D = 768
HEADS = 12
DK = 64
FF = 2048
NB = 32
LEN = 1024
ENC = 512
MOST = 800
DOCS = 6
BATCH = 8
TOKENS = 8192
ENC_TOKENS = 4096


def draw_tokens(key, part):
    first, second, third = jax.random.split(key, 3)
    row_scale = jnp.exp(jax.random.uniform(first, (TOKENS, 1), jnp.float32, 0.0, math.log(10.0))) / 4.0
    column_scale = jnp.exp(jax.random.uniform(second, (1, D), jnp.float32, 0.0, math.log(10.0))) / 4.0
    base = jax.random.normal(third, (TOKENS, D), jnp.float32)
    return (base * row_scale * column_scale).astype(jnp.bfloat16)


def touch_ends(entries, own_key, smallest, top_value):
    longest = entries.shape.index(max(entries.shape))
    spots = []
    for shift in (0, 1):
        where = [jax.random.randint(jax.random.fold_in(own_key, axis), (), 0, length) for axis, length in enumerate(entries.shape)]
        where[longest] = (where[longest] + shift) % entries.shape[longest]
        spots.append(tuple(where))
    return entries.at[spots[0]].set(smallest).at[spots[1]].set(top_value)


def shard_levels(key, shape, pieces, low, largest):
    factor_of = 1.0
    for dim, blocks in pieces:
        heights = jax.random.uniform(jax.random.fold_in(jax.random.fold_in(key, 6), dim), (blocks,), jnp.float32, low / len(pieces), largest / len(pieces))
        factor_of = factor_of * jnp.repeat(jnp.exp(heights), shape[dim] // blocks).reshape((-1,) + (1,) * (len(shape) - 1 - dim))
    return factor_of


def profile(number_of, total, limit, slope):
    portions = [(1 << 20) // math.isqrt(rank ** slope) + 1 for rank in range(2, number_of + 1)]
    spare, counts = total - limit - (number_of - 1), [1] * (number_of - 1)
    while spare > 0:
        free = [i for i in range(number_of - 1) if counts[i] < limit]
        pool, budget = sum([portions[i] for i in free]), spare
        for i in free:
            extra = min(limit - counts[i], max(1, budget * portions[i] // pool), spare)
            counts[i] = counts[i] + extra
            spare = spare - extra
    return np.array([limit] + counts)


def ragged_sizes(stream_key, amount, total, limit, slope):
    if amount == 2:
        one = jax.random.randint(stream_key, (), max(1, total - limit), min(limit, total - 1) + 1)
        return jnp.stack([one, total - one])
    lengths = jnp.asarray(profile(amount, total, limit, slope), jnp.int32)
    pairs = (amount - 1) // 2
    giver, taker = lengths[1:1 + 2 * pairs:2], lengths[2:2 + 2 * pairs:2]
    slack = jnp.minimum(giver - 1, limit - taker)
    moved = jax.random.randint(jax.random.fold_in(stream_key, 1), (pairs,), 0, 1 << 20) % (slack + 1)
    lengths = lengths.at[1:1 + 2 * pairs:2].set(giver - moved).at[2:2 + 2 * pairs:2].set(taker + moved)
    return lengths[jax.random.permutation(jax.random.fold_in(stream_key, 2), amount)]


def noise(key, shape, deviation, limit, pieces=(), held_as=jnp.bfloat16):
    level = shard_levels(key, shape, pieces, -0.22, 0.18) if pieces else 1.0
    drawn = jax.random.normal(key, shape, jnp.float32) * deviation * level
    return jnp.minimum(jnp.maximum(drawn, -limit), limit).astype(held_as)


def setup_inputs(seed: int = 0) -> dict:
    key_list = jax.random.split(jax.random.key(seed), 19)
    return {
        "tokens": draw_tokens(jax.random.fold_in(key_list[18], 71), 0),
        "encoder": noise(key_list[1], (ENC_TOKENS, D), 1.0, 6.0, ((0, 32),)),
        "segments": jax.vmap(lambda own: jnp.searchsorted(jnp.cumsum(ragged_sizes(own, DOCS, LEN, MOST, 1)), jnp.arange(LEN), side="right"))(jax.random.split(key_list[2], BATCH)).reshape((BATCH, LEN)).astype(jnp.int32),
        "rel_bucket": touch_ends(jax.random.randint(key_list[3], (LEN,), 0, NB), jax.random.fold_in(key_list[3], 1), 0, NB - 1).astype(jnp.int32),
        "out_grad": noise(key_list[4], (TOKENS, D), 1.0, 6.0, ((0, 32),)),
        "self_q": noise(key_list[5], (D, HEADS * DK), (4 * D) ** -0.5, 0.109375, ((0, 8), (1, 4))),
        "self_k": noise(key_list[6], (D, HEADS * DK), (4 * D) ** -0.5, 0.109375, ((0, 8), (1, 4))),
        "self_v": noise(key_list[7], (D, HEADS * DK), D ** -0.5, 0.21875, ((0, 8), (1, 4))),
        "self_o": noise(key_list[8], (HEADS * DK, D), (HEADS * DK // 16) ** -0.5, 0.875, ((0, 4), (1, 8))),
        "cross_q": noise(key_list[9], (D, HEADS * DK), (4 * D) ** -0.5, 0.109375, ((0, 8), (1, 4))),
        "cross_k": noise(key_list[10], (D, HEADS * DK), (4 * D) ** -0.5, 0.109375, ((0, 8), (1, 4))),
        "cross_v": noise(key_list[11], (D, HEADS * DK), D ** -0.5, 0.21875, ((0, 8), (1, 4))),
        "cross_o": noise(key_list[12], (HEADS * DK, D), (HEADS * DK // 16) ** -0.5, 0.875, ((0, 4), (1, 8))),
        "ffn_gate": noise(key_list[13], (D, FF), D ** -0.5, 0.21875, ((0, 8), (1, 4))),
        "ffn_up": noise(key_list[14], (D, FF), D ** -0.5, 0.21875, ((0, 8), (1, 4))),
        "ffn_down": noise(key_list[15], (FF, D), FF ** -0.5, 0.125, ((0, 4), (1, 8))),
        "bias_table": noise(key_list[16], (NB, HEADS), 1.0, 3.0, ((1, 4),)),
        "norm_gains": jnp.clip(1.0 + 0.1 * jax.random.normal(key_list[17], (3, D), jnp.float32), 0.5, 1.5).astype(jnp.bfloat16),
    }


EPS = 1e-06
MASKED = -1e+30
HIGHEST = lax.Precision.HIGHEST

@jax.custom_vjp
def low(v):
    return lax.optimization_barrier(v.astype(jnp.bfloat16)).astype(jnp.float32)

@jax.custom_vjp
def low_back(v):
    return v

def low_keep(v):
    return (low(v), None)

def low_pass(kept, grad):
    return (grad,)

def back_keep(v):
    return (v, None)

def back_low(kept, grad):
    return (low(grad),)
low.defvjp(low_keep, low_pass)
low_back.defvjp(back_keep, back_low)

def rms_norm(rows, gain):
    scale = lax.rsqrt(lax.optimization_barrier(jnp.mean(rows * rows, axis=-1, keepdims=True)) + EPS)
    return rows * scale * gain

def matmul(left, right):
    return jnp.dot(left, right, precision=HIGHEST, preferred_element_type=jnp.float32)

def self_attention(query, keys, values, segment_ids, bucket, table):
    block = min(512, LEN)
    count = LEN // block
    columns = jnp.arange(LEN, dtype=jnp.int32)
    table_t = table.T

    def one_block(start):
        rows = start + jnp.arange(block, dtype=jnp.int32)
        part = lax.dynamic_slice_in_dim(query, start, block, 0)
        row_ids = lax.dynamic_slice_in_dim(segment_ids, start, block, 0)
        distance = rows[:, None] - columns[None, :]
        valid = (distance >= 0) & (row_ids[:, None] == segment_ids[None, :])
        bucket_index = jnp.take(bucket, jnp.clip(distance, 0, LEN - 1), axis=0)
        scores = jnp.einsum('qhd,khd->hqk', part, keys, precision=HIGHEST)
        scores = low_back(scores + jnp.take(table_t, bucket_index, axis=1))
        probs = jax.nn.softmax(jnp.where(valid[None], scores, MASKED), axis=-1)
        return jnp.einsum('hqk,khd->qhd', low(probs), values, precision=HIGHEST)
    starts = jnp.arange(count, dtype=jnp.int32) * block
    return lax.map(jax.checkpoint(one_block), starts).reshape(LEN, HEADS * DK)

def cross_attention(query, keys, values):
    block = min(512, LEN)
    count = LEN // block

    def one_block(start):
        part = lax.dynamic_slice_in_dim(query, start, block, 0)
        scores = low_back(jnp.einsum('qhd,khd->hqk', part, keys, precision=HIGHEST))
        probs = jax.nn.softmax(scores, axis=-1)
        return jnp.einsum('hqk,khd->qhd', low(probs), values, precision=HIGHEST)
    starts = jnp.arange(count, dtype=jnp.int32) * block
    return lax.map(jax.checkpoint(one_block), starts).reshape(LEN, HEADS * DK)

def split_heads(value):
    return value.reshape(value.shape[0], HEADS, DK)

def one_sequence(rows, states, segment_ids, bucket, self_q, self_k, self_v, self_o, cross_q, cross_k, cross_v, cross_o, ffn_gate, ffn_up, ffn_down, table, gains):
    normed_self = low(rms_norm(rows, gains[0]))
    query = split_heads(low_back(low(matmul(normed_self, self_q))))
    keys = split_heads(low_back(low(matmul(normed_self, self_k))))
    values = split_heads(low_back(low(matmul(normed_self, self_v))))
    attended = low_back(low(self_attention(query, keys, values, segment_ids, bucket, table)))
    hidden_one = rows + low_back(matmul(attended, self_o))
    normed_cross = low(rms_norm(hidden_one, gains[1]))
    query_cross = split_heads(low_back(low(matmul(normed_cross, cross_q))))
    keys_cross = split_heads(low_back(low(matmul(states, cross_k))))
    values_cross = split_heads(low_back(low(matmul(states, cross_v))))
    attended_cross = low_back(low(cross_attention(query_cross, keys_cross, values_cross)))
    hidden_two = hidden_one + low_back(matmul(attended_cross, cross_o))
    normed_ffn = low(rms_norm(hidden_two, gains[2]))
    gate = low_back(matmul(normed_ffn, ffn_gate))
    upper = low_back(matmul(normed_ffn, ffn_up))
    inner = low(jax.nn.gelu(gate, approximate=True) * upper)
    return hidden_two + low_back(matmul(inner, ffn_down))

def reference(tokens, encoder, segments, rel_bucket, out_grad, self_q, self_k, self_v, self_o, cross_q, cross_k, cross_v, cross_o, ffn_gate, ffn_up, ffn_down, bias_table, norm_gains):
    floats = tuple((a.astype(jnp.float32) for a in (tokens, encoder, self_q, self_k, self_v, self_o, cross_q, cross_k, cross_v, cross_o, ffn_gate, ffn_up, ffn_down, bias_table, norm_gains)))

    def forward(rows_all, states_all, sq, sk, sv, so, cq, ck, cv, co, fg, fu, fd, table, gains):

        def one(item):
            rows, states, segment_ids = item
            return one_sequence(rows, states, segment_ids, rel_bucket, sq, sk, sv, so, cq, ck, cv, co, fg, fu, fd, table, gains)
        outputs = lax.map(one, (rows_all.reshape(BATCH, LEN, D), states_all.reshape(BATCH, ENC, D), segments))
        return outputs.reshape(TOKENS, D)
    result, pull = jax.vjp(forward, *floats)
    grads = pull(out_grad.astype(jnp.float32))
    return (result.astype(jnp.bfloat16), grads[0], grads[1], grads[2], grads[3], grads[4], grads[5], grads[6], grads[7], grads[8], grads[9], grads[10], grads[11], grads[12], grads[13], grads[14])
```

```python
from functools import partial

import jax
import jax.numpy as jnp
from jax import lax
from jax.experimental import pallas as pl
from jax.experimental.pallas import tpu as pltpu
from jax.sharding import PartitionSpec as P

DK = 64
EPS = 1e-06
MASKED = -1e30
BF = jnp.bfloat16
F32 = jnp.float32
MESH = pl.DeviceIdType.MESH
VMEM = pl.BlockSpec(memory_space=pltpu.VMEM)
ANY = pl.BlockSpec(memory_space=pl.ANY)
LIMIT = 62 * 1024 * 1024
STEP = 256


def dot(a, b):
    return jnp.dot(a, b, preferred_element_type=F32)


def dot_nt(a, b):
    return lax.dot_general(a, b, (((1,), (1,)), ((), ())), preferred_element_type=F32)


def dot_tn(a, b):
    return lax.dot_general(a, b, (((0,), (0,)), ((), ())), preferred_element_type=F32)


def norm_scale(x):
    return lax.rsqrt(jnp.mean(x * x, axis=-1, keepdims=True) + EPS)


def norm_back(x, r, g, u):
    w = u * g
    inner = jnp.mean(w * x, axis=-1, keepdims=True)
    return r * w - x * (r * r * r * inner), jnp.sum(u * (x * r), axis=0, keepdims=True)


def flip(index, bit):
    size = 1 << bit
    return index + size - 2 * size * lax.rem(index // size, 2)


def flip_all(index, mask):
    bit = 0
    while mask:
        if mask & 1:
            index = flip(index, bit)
        mask >>= 1
        bit += 1
    return index


def subsets(bits):
    out = [0]
    for b in bits:
        out = out + [m | (1 << b) for m in out]
    return out


def bit_orders(count):
    upper = list(range(1, count))
    return [upper + [0], upper[::-1] + [0]]


class Sems:
    def __init__(self, ref):
        self.ref = ref
        self.used = 0

    def take(self):
        self.used += 1
        return self.ref.at[self.used - 1]


def wait_bytes(ref, sem):
    pltpu.make_async_copy(ref, ref, sem).wait()


def enter(nt, nd):
    me_t, me_d = lax.axis_index("tensor"), lax.axis_index("dp")
    bar = pltpu.get_barrier_semaphore()
    bits = nd.bit_length() - 1
    for b in range(bits):
        pl.semaphore_signal(bar, 1, device_id={"dp": flip(me_d, b)}, device_id_type=MESH)

    @pl.when(me_t > 0)
    def _():
        pl.semaphore_signal(bar, 1, device_id={"tensor": me_t - 1}, device_id_type=MESH)

    @pl.when(me_t < nt - 1)
    def _():
        pl.semaphore_signal(bar, 1, device_id={"tensor": me_t + 1}, device_id_type=MESH)

    pl.semaphore_wait(bar, bits + (me_t + nt - 1) // nt + (2 * nt - 2 - me_t) // nt)
    return me_t, me_d


def run_jobs(jobs, after):
    last = max(start + len(stages) for start, stages in jobs)
    for tick in range(last):
        for start, stages in jobs:
            if 0 <= tick - start < len(stages):
                stages[tick - start]()
    for fn in after:
        fn()


def line_gather(nt, me, own, slot, sends, recvs, after):
    sem = {(s, j): (sends.take(), recvs.take()) for s in (1, -1) for j in range(1, nt)}

    def send(side, j):
        block = me - side * (j - 1)
        target = me + side
        ok = (block >= 0) & (block < nt) & (target >= 0) & (target < nt)
        src = own if j == 1 else slot(jnp.clip(block, 0, nt - 1))
        dst = slot(jnp.clip(block, 0, nt - 1))
        ss, rs = sem[side, j]

        @pl.when(ok)
        def _():
            pltpu.make_async_remote_copy(
                src, dst, ss, rs, device_id={"tensor": target}, device_id_type=MESH
            ).start()

        def done():
            @pl.when(ok)
            def _():
                wait_bytes(own, ss)

        after.append(done)

    def arrive(side, j):
        block = me - side * j

        @pl.when((block >= 0) & (block < nt))
        def _():
            wait_bytes(own, sem[side, j][1])

    def stage(j):
        def run():
            for side in (1, -1):
                if j > 0:
                    arrive(side, j)
                if j < nt - 1:
                    send(side, j + 1)

        return run

    return [stage(j) for j in range(nt)]


def cube_gather(nd, me, order, own, slot, slots, sends, recvs, after):
    count = len(order)
    sem = [(sends.take(), recvs.take()) for _ in range(count)]

    def start(k):
        bit = order[k]
        for m in subsets(order[:k]):
            block = flip_all(me, m)
            src = own if (m == 0 and own is not None) else slot(block)
            pltpu.make_async_remote_copy(
                src, slot(block), sem[k][0], sem[k][1], device_id={"dp": flip(me, bit)}, device_id_type=MESH
            ).start()

        def done():
            wait_bytes(slots(1 << k), sem[k][0])

        after.append(done)

    def stage(k):
        def run():
            if k > 0:
                wait_bytes(slots(1 << (k - 1)), sem[k - 1][1])
            if k < count:
                start(k)

        return run

    return [stage(k) for k in range(count + 1)]


def gather_kernel(
    nt, nd, tok_ref, enc_ref, wa_ref, wb_ref, tok_out, enc_out, wa_out, wb_out, ssem, rsem, lsem
):
    me_t, me_d = enter(nt, nd)
    bits = nd.bit_length() - 1
    sends, recvs, after = Sems(ssem), Sems(rsem), []
    locals_ = [
        (tok_ref, tok_out.at[me_t]),
        (enc_ref, enc_out.at[me_t]),
        (wa_ref, wa_out.at[me_d]),
        (wb_ref, wb_out.at[me_t, me_d]),
    ]
    for n, (src, dst) in enumerate(locals_):
        pltpu.make_async_copy(src, dst, lsem.at[n]).start()
    orders = bit_orders(bits)
    cols = wb_ref.shape[1]
    chunks = cols // STEP
    half = STEP // 2
    jobs = []
    jobs.append(
        (0, cube_gather(nd, me_d, orders[0], wa_ref, lambda d: wa_out.at[d], lambda n: wa_out.at[pl.ds(0, n)], sends, recvs, after))
    )

    def chunk_job(c):
        first = c * STEP
        z = line_gather(
            nt,
            me_t,
            wb_ref.at[:, pl.ds(first, STEP)],
            lambda t: wb_out.at[t, me_d, :, pl.ds(first, STEP)],
            sends,
            recvs,
            after,
        )
        cubes = []
        for n in range(2):
            at = first + n * half
            cubes.append(
                cube_gather(
                    nd,
                    me_d,
                    orders[n],
                    None,
                    lambda d, at=at: wb_out.at[:, d, :, pl.ds(at, half)],
                    lambda k, at=at: wb_out.at[:, pl.ds(0, k), :, pl.ds(at, half)],
                    sends,
                    recvs,
                    after,
                )
            )

        def meet():
            z[-1]()
            for q in cubes:
                q[0]()

        def both(k):
            def run():
                for q in cubes:
                    q[k]()

            return run

        return z[:-1] + [meet] + [both(k) for k in range(1, bits + 1)]

    tok_job = line_gather(nt, me_t, tok_ref, lambda t: tok_out.at[t], sends, recvs, after)
    enc_job = line_gather(nt, me_t, enc_ref, lambda t: enc_out.at[t], sends, recvs, after)
    for c in range(chunks):
        jobs.append((c, chunk_job(c)))
    jobs.append((2, tok_job))
    jobs.append((5, enc_job))
    pltpu.make_async_copy(wb_ref, wb_out.at[me_t, me_d], lsem.at[3]).wait()
    for n in range(3):
        src, dst = locals_[n]
        after.append(lambda n=n, src=src, dst=dst: pltpu.make_async_copy(src, dst, lsem.at[n]).wait())
    run_jobs(jobs, after)


def gather_all(nt, nd, tok, enc, wa, wb):
    bits = nd.bit_length() - 1
    chunks = wb.shape[1] // STEP
    total = (chunks + 2) * 2 * (nt - 1) + (2 * chunks + 1) * bits
    return pl.pallas_call(
        partial(gather_kernel, nt, nd),
        out_shape=(
            jax.ShapeDtypeStruct((nt,) + tok.shape, BF),
            jax.ShapeDtypeStruct((nt,) + enc.shape, BF),
            jax.ShapeDtypeStruct((nd,) + wa.shape, BF),
            jax.ShapeDtypeStruct((nt, nd) + wb.shape, BF),
        ),
        in_specs=[VMEM] * 4,
        out_specs=(ANY,) * 4,
        scratch_shapes=[
            pltpu.SemaphoreType.DMA((total,)),
            pltpu.SemaphoreType.DMA((total,)),
            pltpu.SemaphoreType.DMA((4,)),
        ],
        compiler_params=pltpu.CompilerParams(collective_id=0, has_side_effects=True),
        name="gather_all",
    )(tok, enc, wa, wb)


def exchange_kernel(nt, x_ref, o_ref, ssem, rsem, lsem):
    me = lax.axis_index("tensor")
    bar = pltpu.get_barrier_semaphore()
    for k in range(1, nt):
        pl.semaphore_signal(bar, 1, device_id={"tensor": lax.rem(me + k, nt)}, device_id_type=MESH)
    pl.semaphore_wait(bar, nt - 1)
    local = pltpu.make_async_copy(x_ref.at[me], o_ref.at[me], lsem)
    local.start()
    copies = []
    for k in range(1, nt):
        peer = lax.rem(me + k, nt)
        copy = pltpu.make_async_remote_copy(
            x_ref.at[peer], o_ref.at[me], ssem.at[k], rsem.at[k], device_id={"tensor": peer}, device_id_type=MESH
        )
        copy.start()
        copies.append(copy)
    local.wait()
    for copy in copies:
        copy.wait()


def exchange(nt, x, ident):
    return pl.pallas_call(
        partial(exchange_kernel, nt),
        out_shape=jax.ShapeDtypeStruct(x.shape, x.dtype),
        in_specs=[VMEM],
        out_specs=VMEM,
        scratch_shapes=[
            pltpu.SemaphoreType.DMA((nt,)),
            pltpu.SemaphoreType.DMA((nt,)),
            pltpu.SemaphoreType.DMA,
        ],
        compiler_params=pltpu.CompilerParams(collective_id=ident, has_side_effects=True),
        name="exchange",
    )(x)


def cube_scatter(nd, me, order, value, recv, sends, recvs, after):
    count = len(order)
    sem = [(sends.take(), recvs.take()) for _ in range(count)]

    def start(k):
        bit = order[k]
        peer = flip(me, bit)
        for j, m in enumerate(subsets(order[k + 1 :])):
            pltpu.make_async_remote_copy(
                value(flip_all(peer, m)),
                recv[k].at[j],
                sem[k][0],
                sem[k][1],
                device_id={"dp": peer},
                device_id_type=MESH,
            ).start()

        def done():
            wait_bytes(recv[k], sem[k][0])

        after.append(done)

    def land(k):
        wait_bytes(recv[k], sem[k][1])
        for j, m in enumerate(subsets(order[k + 1 :])):
            ref = value(flip_all(me, m))
            got = recv[k].at[j]
            if len(ref.shape) == 2:
                ref[...] = (ref[...].astype(F32) + got[...].astype(F32)).astype(BF)
            else:
                for t in range(ref.shape[0]):
                    ref[t] = (ref[t].astype(F32) + got[t].astype(F32)).astype(BF)

    def stage(k):
        def run():
            if k > 0:
                land(k - 1)
            if k < count:
                start(k)

        return run

    return [stage(k) for k in range(count + 1)]


def line_scatter(nt, me, value, recv, finish, sends, recvs, after):
    sem = {(s, b): (sends.take(), recvs.take()) for s in (0, 1) for b in range(nt)}

    def hop(z):
        def run():
            for side, here in ((0, z), (1, nt - 1 - z)):
                goal = here + 1 if side == 0 else here - 1
                blocks = range(here + 1, nt) if side == 0 else range(here - 1, -1, -1)

                @pl.when(me == here)
                def _(side=side, goal=goal, blocks=blocks):
                    for b in blocks:
                        ref = value(b)
                        if z > 0:
                            got = recv.at[side, b]
                            wait_bytes(got, sem[side, b][1])
                            ref[...] = (ref[...].astype(F32) + got[...].astype(F32)).astype(BF)
                        pltpu.make_async_remote_copy(
                            ref,
                            recv.at[side, b],
                            sem[side, b][0],
                            sem[side, b][1],
                            device_id={"tensor": goal},
                            device_id_type=MESH,
                        ).start()

        return run

    def last():
        for here in range(nt):

            @pl.when(me == here)
            def _(here=here):
                if here > 0:
                    wait_bytes(recv.at[0, here], sem[0, here][1])
                if here < nt - 1:
                    wait_bytes(recv.at[1, here], sem[1, here][1])
                total = value(here)[...].astype(F32)
                if here > 0:
                    total = total + recv[0, here].astype(F32)
                if here < nt - 1:
                    total = total + recv[1, here].astype(F32)
                finish(total)

    def done():
        for here in range(nt):

            @pl.when(me == here)
            def _(here=here):
                for b in range(here + 1, nt):
                    wait_bytes(recv.at[0, b], sem[0, b][0])
                for b in range(here):
                    wait_bytes(recv.at[1, b], sem[1, b][0])

    after.append(done)
    return [hop(z) for z in range(nt - 1)] + [last]


def scatter_kernel(
    nt,
    nd,
    g_ref,
    a_ref,
    u_ref,
    e_ref,
    gg_ref,
    tt_ref,
    g_out,
    a_out,
    u_out,
    e_out,
    *scratch,
):
    bits = nd.bit_length() - 1
    gv, uz, ez, gz = scratch[:4]
    arecv = scratch[4 : 4 + bits]
    grecv = scratch[4 + bits : 4 + 2 * bits]
    ssem, rsem, lsem = scratch[4 + 2 * bits :]
    cols = g_ref.shape[3]
    chunks = cols // STEP
    half = STEP // 2
    for c in range(chunks):
        at = pl.ds(c * STEP, STEP)
        pltpu.make_async_copy(g_ref.at[:, :, :, at], gv.at[:, :, :, at], lsem.at[c]).start()
    me_t, me_d = enter(nt, nd)
    sends, recvs, after = Sems(ssem), Sems(rsem), []
    orders = [[0] + o[:-1][::-1] for o in bit_orders(bits)]
    heads = tt_ref.shape[0]
    wide = a_ref.shape[2]
    for d in range(nd):
        a_ref[d, :heads, wide - 128 :] = tt_ref[...].astype(BF)
    jobs = []

    def a_done():
        a_out[...] = a_ref[me_d].astype(F32)

    a_job = cube_scatter(nd, me_d, orders[0], lambda d: a_ref.at[d], arecv, sends, recvs, after) + [a_done]

    def chunk_job(c):
        first = c * STEP
        cubes = []
        for n in range(2):
            at = first + n * half
            cubes.append(
                cube_scatter(
                    nd,
                    me_d,
                    orders[n],
                    lambda d, at=at: gv.at[:, d, :, pl.ds(at, half)],
                    [r.at[2 * c + n] for r in grecv],
                    sends,
                    recvs,
                    after,
                )
            )

        def finish(total):
            g_out[:, first : first + STEP] = total

        z = line_scatter(
            nt,
            me_t,
            lambda b: gv.at[b, me_d, :, pl.ds(first, STEP)],
            gz.at[c],
            finish,
            sends,
            recvs,
            after,
        )

        def begin():
            at = pl.ds(first, STEP)
            pltpu.make_async_copy(g_ref.at[:, :, :, at], gv.at[:, :, :, at], lsem.at[c]).wait()
            if c == chunks - 1:
                for t in range(nt):
                    for d in range(nd):
                        gv[t, d, :, cols - 128 :] = gv[t, d, :, cols - 128 :] + gg_ref[d]
            for q in cubes:
                q[0]()

        def both(k):
            def run():
                for q in cubes:
                    q[k]()

            return run

        def meet():
            for q in cubes:
                q[bits]()
            z[0]()

        return [begin] + [both(k) for k in range(1, bits)] + [meet] + z[1:]

    def u_finish(total):
        u_out[...] = total

    def e_finish(total):
        e_out[...] = total

    jobs.append((0, a_job))
    jobs.append((0, line_scatter(nt, me_t, lambda b: u_ref.at[b], uz, u_finish, sends, recvs, after)))
    jobs.append((1, line_scatter(nt, me_t, lambda b: e_ref.at[b], ez, e_finish, sends, recvs, after)))
    for c in range(chunks):
        jobs.append((c, chunk_job(c)))
    run_jobs(jobs, after)


def scatter_all(nt, nd, g, a, u, e, gg, tt):
    bits = nd.bit_length() - 1
    rows, cols = g.shape[2:]
    wide = a.shape[2]
    chunks = cols // STEP
    total = (chunks + 2) * 2 * nt + (2 * chunks + 1) * bits
    return pl.pallas_call(
        partial(scatter_kernel, nt, nd),
        out_shape=(
            jax.ShapeDtypeStruct((rows, cols), F32),
            jax.ShapeDtypeStruct((rows, wide), F32),
            jax.ShapeDtypeStruct(u.shape[1:], F32),
            jax.ShapeDtypeStruct(e.shape[1:], F32),
        ),
        in_specs=[ANY] + [VMEM] * 5,
        out_specs=(VMEM,) * 4,
        scratch_shapes=[
            pltpu.VMEM((nt, nd, rows, cols), BF),
            pltpu.VMEM((2,) + u.shape, BF),
            pltpu.VMEM((2,) + e.shape, BF),
            pltpu.VMEM((chunks, 2, nt, rows, STEP), BF),
        ]
        + [pltpu.VMEM((1 << (bits - 1 - k), rows, wide), BF) for k in range(bits)]
        + [pltpu.VMEM((2 * chunks, 1 << (bits - 1 - k), nt, rows, STEP // 2), BF) for k in range(bits)]
        + [
            pltpu.SemaphoreType.DMA((total,)),
            pltpu.SemaphoreType.DMA((total,)),
            pltpu.SemaphoreType.DMA((chunks,)),
        ],
        compiler_params=pltpu.CompilerParams(collective_id=1, has_side_effects=True, vmem_limit_bytes=LIMIT),
        name="scatter_all",
    )(g, a, u, e, gg, tt)


def build_strips(strip, line, heads):
    block = strip.shape[1]
    width = strip.shape[2]
    row = lax.broadcasted_iota(jnp.int32, (8, width), 0)
    for h in range(heads):
        x = jnp.broadcast_to(line[h : h + 1, :], (8, width))
        for b in range(3):
            x = jnp.where((row >> b) % 2 == 1, pltpu.roll(x, 1 << b, 1), x)
        strip[h, 0:8, :] = x
        n = 8
        while n < block:
            strip[h, n : 2 * n, :] = pltpu.roll(strip[h, 0:n, :], n, 1)
            n *= 2


def bias_lines(bl_ref, tab_ref):
    width = bl_ref.shape[1]
    buckets = tab_ref.shape[1]
    hot = bl_ref[...] == lax.broadcasted_iota(jnp.int32, (buckets, width), 0)
    line = dot(tab_ref[...], hot.astype(F32).astype(BF))
    return jnp.where(bl_ref[...] >= 0, line, MASKED), hot


def self_forward_kernel(
    heads, tok_ref, wa_ref, g_ref, segc_ref, segr_ref, bl_ref, tab_ref, qkv_ref, attn_ref, lse_ref, strip, qs, ks, vs, os
):
    nt, block = tok_ref.shape[:2]
    hw = heads * DK
    line, _ = bias_lines(bl_ref, tab_ref)
    build_strips(strip, line, heads)
    for i in range(nt):
        x = tok_ref[i].astype(F32)
        n = (x * norm_scale(x) * g_ref[...]).astype(BF)
        y = dot(n, wa_ref[:, : 3 * hw]).astype(BF)
        qkv_ref[i] = y
        for h in range(heads):
            for which, ref in enumerate((qs, ks, vs)):
                at = which * hw + h * DK
                ref[h, i * block : (i + 1) * block, :] = y[:, at : at + DK]

    def head(h, carry):
        for i in range(nt):
            mine = slice(i * block, (i + 1) * block)
            seen = (i + 1) * block
            s = dot_nt(qs[h, mine, :], ks[h, :seen, :])
            s = s + strip[h, :, (nt - 1 - i) * block : (nt - 1 - i) * block + seen]
            s = jnp.where(segc_ref[mine, :] == segr_ref[:, :seen], s, MASKED)
            top = jnp.max(s, axis=-1, keepdims=True)
            p = jnp.exp(s - top)
            total = jnp.sum(p, axis=-1, keepdims=True)
            o = dot(p.astype(BF), vs[h, :seen, :]) / total
            os[h, mine, :] = o
            lse_ref[h, mine, :] = top + jnp.log(total)
        return carry

    lax.fori_loop(0, heads, head, 0)
    for i in range(nt):
        mine = slice(i * block, (i + 1) * block)
        attn_ref[i] = jnp.concatenate([os[h, mine, :] for h in range(heads)], axis=1).astype(BF)


def self_forward(heads, tok, wa, g, segc, segr, bl, tab):
    nt, block, width = tok.shape
    length = nt * block
    hw = heads * DK
    return pl.pallas_call(
        partial(self_forward_kernel, heads),
        out_shape=(
            jax.ShapeDtypeStruct((nt, block, 3 * hw), BF),
            jax.ShapeDtypeStruct((nt, block, hw), BF),
            jax.ShapeDtypeStruct((heads, length, 1), F32),
        ),
        in_specs=[VMEM] * 7,
        out_specs=(VMEM,) * 3,
        scratch_shapes=[pltpu.VMEM((heads, block, length + block), F32)]
        + [pltpu.VMEM((heads, length, DK), BF)] * 3
        + [pltpu.VMEM((heads, length, DK), F32)],
        compiler_params=pltpu.CompilerParams(vmem_limit_bytes=LIMIT),
        name="self_forward",
    )(tok, wa, g, segc, segr, bl, tab)


def self_backward_kernel(
    heads,
    tok_ref,
    wa_ref,
    g_ref,
    segc_ref,
    segr_ref,
    bl_ref,
    tab_ref,
    qkv_ref,
    attn_ref,
    lse_ref,
    dattn_ref,
    u_ref,
    ga_ref,
    gain_ref,
    table_ref,
    strip,
    dstrip,
    qs,
    ks,
    vs,
    das,
    delta,
    dq,
    dkt,
    dvt,
    norms,
    dqkv,
):
    nt, block = tok_ref.shape[:2]
    hw = heads * DK
    length = nt * block
    line, hot = bias_lines(bl_ref, tab_ref)
    build_strips(strip, line, heads)
    for i in range(nt):
        mine = slice(i * block, (i + 1) * block)
        y = qkv_ref[i]
        da = dattn_ref[i]
        prod = da.astype(F32) * attn_ref[i].astype(F32)
        for h in range(heads):
            part = slice(h * DK, (h + 1) * DK)
            for which, ref in enumerate((qs, ks, vs)):
                at = which * hw + h * DK
                ref[h, mine, :] = y[:, at : at + DK]
            das[h, mine, :] = da[:, part]
            delta[h, mine, :] = jnp.sum(prod[:, part], axis=1, keepdims=True)
    dstrip[...] = jnp.zeros_like(dstrip)
    dkt[...] = jnp.zeros_like(dkt)
    dvt[...] = jnp.zeros_like(dvt)

    def head(h, carry):
        for i in range(nt):
            mine = slice(i * block, (i + 1) * block)
            seen = (i + 1) * block
            off = (nt - 1 - i) * block
            q = qs[h, mine, :]
            da = das[h, mine, :]
            s = dot_nt(q, ks[h, :seen, :])
            s = s + strip[h, :, off : off + seen]
            s = jnp.where(segc_ref[mine, :] == segr_ref[:, :seen], s, MASKED)
            p = jnp.exp(s - lse_ref[h, mine, :])
            dp = dot_nt(da, vs[h, :seen, :])
            ds = p * (dp - delta[h, mine, :])
            low = ds.astype(BF)
            dq[h, mine, :] = dot(low, ks[h, :seen, :])
            dkt[h, :, :seen] += dot_tn(q, low)
            dvt[h, :, :seen] += dot_tn(da, p.astype(BF))
            dstrip[h, :, off : off + seen] += ds
        return carry

    lax.fori_loop(0, heads, head, 0)
    lines = []
    for h in range(heads):
        n = block // 2
        while n >= 8:
            dstrip[h, 0:n, :] = dstrip[h, 0:n, :] + pltpu.roll(dstrip[h, n : 2 * n, :], length + block - n, 1)
            n //= 2
        x = dstrip[h, 0:8, :]
        row = lax.broadcasted_iota(jnp.int32, x.shape, 0)
        for b in range(3):
            x = jnp.where((row >> b) % 2 == 1, pltpu.roll(x, length + block - (1 << b), 1), x)
        lines.append(jnp.sum(x, axis=0, keepdims=True))
    lines = jnp.concatenate(lines + [jnp.zeros((8 - heads, length + block), F32)], axis=0)
    table = lax.dot_general(
        lines,
        hot.astype(F32),
        (((1,), (1,)), ((), ())),
        precision=lax.Precision.HIGHEST,
        preferred_element_type=F32,
    )
    table_ref[...] = jnp.concatenate([table, jnp.zeros((8, 128 - table.shape[1]), F32)], axis=1)
    gain = jnp.zeros(gain_ref.shape, F32)
    for i in range(nt):
        mine = slice(i * block, (i + 1) * block)
        pieces = [dq[h, mine, :] for h in range(heads)]
        pieces += [dkt[h, :, mine].T for h in range(heads)]
        pieces += [dvt[h, :, mine].T for h in range(heads)]
        low = jnp.concatenate(pieces, axis=1).astype(BF)
        dqkv[mine, :] = low
        x = tok_ref[i].astype(F32)
        hat = x * norm_scale(x)
        norms[mine, :] = (hat * g_ref[...]).astype(BF)
        u = dot_nt(low, wa_ref[:, : 3 * hw])
        gain = gain + jnp.sum(u * hat, axis=0, keepdims=True)
        u_ref[i] = u.astype(BF)
    gain_ref[...] = gain
    ga_ref[:, : 3 * hw] = dot_tn(norms[...], dqkv[...]).astype(BF)
    ga_ref[:, 3 * hw :] = jnp.zeros((ga_ref.shape[0], ga_ref.shape[1] - 3 * hw), BF)


def self_backward(heads, tok, wa, g, segc, segr, bl, tab, qkv, attn, lse, dattn):
    nt, block, width = tok.shape
    length = nt * block
    hw = heads * DK
    return pl.pallas_call(
        partial(self_backward_kernel, heads),
        out_shape=(
            jax.ShapeDtypeStruct((nt, block, width), BF),
            jax.ShapeDtypeStruct(wa.shape, BF),
            jax.ShapeDtypeStruct((1, width), F32),
            jax.ShapeDtypeStruct((8, 128), F32),
        ),
        in_specs=[VMEM] * 11,
        out_specs=(VMEM,) * 4,
        scratch_shapes=[pltpu.VMEM((heads, block, length + block), F32)] * 2
        + [pltpu.VMEM((heads, length, DK), BF)] * 4
        + [pltpu.VMEM((heads, length, 1), F32), pltpu.VMEM((heads, length, DK), F32)]
        + [pltpu.VMEM((heads, DK, length), F32)] * 2
        + [pltpu.VMEM((length, width), BF), pltpu.VMEM((length, 3 * hw), BF)],
        compiler_params=pltpu.CompilerParams(vmem_limit_bytes=LIMIT),
        name="self_backward",
    )(tok, wa, g, segc, segr, bl, tab, qkv, attn, lse, dattn)


def middle_kernel(
    heads,
    ff,
    tok_ref,
    enc_ref,
    attn_ref,
    og_ref,
    gains_ref,
    w_hbm,
    layer_ref,
    one_ref,
    denc_ref,
    gain_ref,
    dattn_ref,
    g_hbm,
    w,
    g,
    h1_ref,
    h2_ref,
    n1_ref,
    n2_ref,
    acc_ref,
    dn_ref,
    g2_ref,
    denc,
    qc,
    kv,
    ac,
    oc,
    lse,
    dkv,
    insem,
    outsem,
):
    nt = w.shape[0]
    hw = heads * DK
    cols = w.shape[2]
    f0, f1, f2 = 0, ff, 2 * ff
    kv0 = 3 * ff
    q0 = kv0 + 2 * hw
    c0 = q0 + hw
    s0 = c0 + hw
    end = s0 + hw
    ffn = pl.ds(0, 3 * ff)
    att = pl.ds(3 * ff, cols - 3 * ff)
    loads = [pltpu.make_async_copy(w_hbm.at[t, :, att], w.at[t, :, att], insem.at[0, t]) for t in range(nt)]
    loads += [pltpu.make_async_copy(w_hbm.at[t, :, ffn], w.at[t, :, ffn], insem.at[1, t]) for t in range(nt)]
    for copy in loads:
        copy.start()

    def load_wait(which, t):
        at = att if which == 0 else ffn
        pltpu.make_async_copy(w_hbm.at[t, :, at], w.at[t, :, at], insem.at[which, t]).wait()

    def store(which, t):
        at = att if which == 0 else ffn
        return pltpu.make_async_copy(g.at[t, :, at], g_hbm.at[t, :, at], outsem.at[which, t])

    acc_ref[...] = tok_ref[...].astype(F32)

    def self_out(t, carry):
        load_wait(0, t)
        acc_ref[...] += dot_nt(attn_ref[t], w[t, :, s0:end])
        return carry

    lax.fori_loop(0, nt, self_out, 0)
    h1 = acc_ref[...]
    h1_ref[...] = h1
    n1_ref[...] = (h1 * norm_scale(h1) * gains_ref[1:2, :]).astype(BF)

    def cross(t, carry):
        q = dot(n1_ref[...], w[t, :, q0:c0]).astype(BF)
        both = dot(enc_ref[...], w[t, :, kv0:q0]).astype(BF)
        qc[t] = q
        kv[t] = both
        outs = []
        for h in range(heads):
            part = slice(h * DK, (h + 1) * DK)
            s = dot_nt(q[:, part], both[:, part])
            top = jnp.max(s, axis=-1, keepdims=True)
            p = jnp.exp(s - top)
            total = jnp.sum(p, axis=-1, keepdims=True)
            lse[t, h] = top + jnp.log(total)
            outs.append(dot(p.astype(BF), both[:, hw + h * DK : hw + (h + 1) * DK]) / total)
        a = jnp.concatenate(outs, axis=1).astype(BF)
        ac[t] = a
        acc_ref[...] += dot_nt(a, w[t, :, c0:s0])
        return carry

    lax.fori_loop(0, nt, cross, 0)
    h2 = acc_ref[...]
    h2_ref[...] = h2
    n2_ref[...] = (h2 * norm_scale(h2) * gains_ref[2:3, :]).astype(BF)
    dn_ref[...] = jnp.zeros_like(dn_ref)

    def units(t, carry):
        load_wait(1, t)
        n2 = n2_ref[...]
        og = og_ref[...]
        gate = dot(n2, w[t, :, f0:f1])
        up = dot(n2, w[t, :, f1:f2])
        dinner = dot(og, w[t, :, f2 : 3 * ff])
        sq = gate * gate
        th = jnp.tanh(0.7978845608028654 * (gate + 0.044715 * (gate * sq)))
        cdf = 0.5 * (1.0 + th)
        act = gate * cdf
        slope = cdf + gate * (0.5 * (1.0 - th * th)) * (0.7978845608028654 * (1.0 + 0.134145 * sq))
        inner = (act * up).astype(BF)
        dgate = (dinner * up * slope).astype(BF)
        dup = (dinner * act).astype(BF)
        acc_ref[...] += dot_nt(inner, w[t, :, f2 : 3 * ff])
        dn_ref[...] += dot_nt(dgate, w[t, :, f0:f1]) + dot_nt(dup, w[t, :, f1:f2])
        g[t, :, f0:f1] = dot_tn(n2, dgate).astype(BF)
        g[t, :, f1:f2] = dot_tn(n2, dup).astype(BF)
        g[t, :, f2 : 3 * ff] = dot_tn(og, inner).astype(BF)
        store(1, t).start()
        return carry

    lax.fori_loop(0, nt, units, 0)
    layer_ref[...] = acc_ref[...].astype(BF)
    h2 = h2_ref[...]
    back, gain2 = norm_back(h2, norm_scale(h2), gains_ref[2:3, :], dn_ref[...])
    g2 = og_ref[...].astype(F32) + back
    acc_ref[...] = g2
    g2_ref[...] = g2.astype(BF)
    dn_ref[...] = jnp.zeros_like(dn_ref)
    denc[...] = jnp.zeros_like(denc)

    def cross_back(t, carry):
        g2 = g2_ref[...]
        a = ac[t]
        da = dot(g2, w[t, :, c0:s0]).astype(BF)
        g[t, :, c0:s0] = dot_tn(g2, a).astype(BF)
        prod = da.astype(F32) * a.astype(F32)
        q = qc[t]
        both = kv[t]
        dqs = []
        for h in range(heads):
            part = slice(h * DK, (h + 1) * DK)
            qh, kh = q[:, part], both[:, part]
            vh, dah = both[:, hw + h * DK : hw + (h + 1) * DK], da[:, part]
            p = jnp.exp(dot_nt(qh, kh) - lse[t, h])
            delta = jnp.sum(prod[:, part], axis=1, keepdims=True)
            ds = (p * (dot_nt(dah, vh) - delta)).astype(BF)
            dqs.append(dot(ds, kh))
            dkv[h * DK : (h + 1) * DK, :] = dot_tn(qh, ds)
            dkv[hw + h * DK : hw + (h + 1) * DK, :] = dot_tn(dah, p.astype(BF))
        dq = jnp.concatenate(dqs, axis=1).astype(BF)
        dboth = dkv[...].astype(BF)
        g[t, :, q0:c0] = dot_tn(n1_ref[...], dq).astype(BF)
        g[t, :, kv0:q0] = lax.dot_general(
            enc_ref[...], dboth, (((0,), (1,)), ((), ())), preferred_element_type=F32
        ).astype(BF)
        dn_ref[...] += dot_nt(dq, w[t, :, q0:c0])
        denc[...] += lax.dot_general(
            dboth, w[t, :, kv0:q0], (((0,), (1,)), ((), ())), preferred_element_type=F32
        )
        return carry

    lax.fori_loop(0, nt, cross_back, 0)
    denc_ref[...] = denc[...].astype(BF)
    h1 = h1_ref[...]
    back, gain1 = norm_back(h1, norm_scale(h1), gains_ref[1:2, :], dn_ref[...])
    g1 = acc_ref[...] + back
    one_ref[...] = g1
    g2_ref[...] = g1.astype(BF)
    gain_ref[...] = jnp.concatenate([gain1, gain2, jnp.zeros((6, gain1.shape[1]), F32)], axis=0)

    def self_out_back(t, carry):
        low = g2_ref[...]
        dattn_ref[t] = dot(low, w[t, :, s0:end]).astype(BF)
        tail = dot_tn(low, attn_ref[t])
        g[t, :, s0:cols] = jnp.concatenate([tail, jnp.zeros((tail.shape[0], cols - end), F32)], axis=1).astype(BF)
        store(0, t).start()
        return carry

    lax.fori_loop(0, nt, self_out_back, 0)
    for t in range(nt):
        store(1, t).wait()
        store(0, t).wait()


def middle(heads, ff, tok, enc, attn, og, gains, w):
    nt, _, cols = w.shape
    rows, width = tok.shape
    states = enc.shape[0]
    hw = heads * DK
    return pl.pallas_call(
        partial(middle_kernel, heads, ff),
        out_shape=(
            jax.ShapeDtypeStruct((rows, width), BF),
            jax.ShapeDtypeStruct((rows, width), F32),
            jax.ShapeDtypeStruct((states, width), BF),
            jax.ShapeDtypeStruct((8, width), F32),
            jax.ShapeDtypeStruct((nt, rows, hw), BF),
            jax.ShapeDtypeStruct(w.shape, BF),
        ),
        in_specs=[VMEM] * 5 + [ANY],
        out_specs=(VMEM,) * 5 + (ANY,),
        scratch_shapes=[
            pltpu.VMEM(w.shape, BF),
            pltpu.VMEM(w.shape, BF),
            pltpu.VMEM((rows, width), F32),
            pltpu.VMEM((rows, width), F32),
            pltpu.VMEM((rows, width), BF),
            pltpu.VMEM((rows, width), BF),
            pltpu.VMEM((rows, width), F32),
            pltpu.VMEM((rows, width), F32),
            pltpu.VMEM((rows, width), BF),
            pltpu.VMEM((states, width), F32),
            pltpu.VMEM((nt, rows, hw), BF),
            pltpu.VMEM((nt, states, 2 * hw), BF),
            pltpu.VMEM((nt, rows, hw), BF),
            pltpu.VMEM((8, 128), F32),
            pltpu.VMEM((nt, heads, rows, 1), F32),
            pltpu.VMEM((2 * hw, states), F32),
            pltpu.SemaphoreType.DMA((2, nt)),
            pltpu.SemaphoreType.DMA((2, nt)),
        ],
        compiler_params=pltpu.CompilerParams(vmem_limit_bytes=LIMIT),
        name="middle",
    )(tok, enc, attn, og, gains, w)


def per_device(
    tokens,
    encoder,
    segments,
    rel_bucket,
    out_grad,
    self_q,
    self_k,
    self_v,
    self_o,
    cross_q,
    cross_k,
    cross_v,
    cross_o,
    ffn_gate,
    ffn_up,
    ffn_down,
    bias_table,
    norm_gains,
):
    nt, nd = lax.axis_size("tensor"), lax.axis_size("dp")
    part, hw = self_q.shape
    ff = ffn_gate.shape[1]
    heads = hw // DK
    rows, width = tokens.shape
    length = rows * nt
    buckets = bias_table.shape[0]
    wa = jnp.concatenate([self_q, self_k, self_v, jnp.pad(norm_gains.T, ((0, 0), (0, 128 - norm_gains.shape[0])))], axis=1)
    wb = jnp.concatenate([ffn_gate, ffn_up, ffn_down.T, cross_k, cross_v, cross_q, cross_o.T, self_o.T], axis=1)
    used = wb.shape[1]
    cols = -(-(used + 3) // STEP) * STEP
    wb = jnp.pad(wb, ((0, 0), (0, cols - used)))
    tok_all, enc_all, wa_all, wb_all = gather_all(nt, nd, tokens, encoder, wa, wb)
    wa_full = wa_all.reshape(nd * part, wa.shape[1])
    wb_full = wb_all.reshape(nt, nd * part, cols)
    gains = jnp.pad(wa_full[:, 3 * hw : 3 * hw + 3].T.astype(F32), ((0, 5), (0, 0)))
    top = (nt - 1) * rows
    blank = jnp.full((length - 1 - top,), -1, jnp.int32)
    bl = jnp.concatenate(
        [rel_bucket[: top + 1][::-1], blank, jnp.full((1,), -1, jnp.int32), rel_bucket[top + 1 : length][::-1]]
    )[None, :]
    tab = jnp.pad(bias_table.T, ((0, 8 - heads), (0, 0)))
    segr = segments
    segc = segments.T
    g0 = gains[0:1]
    qkv, attn, lse = self_forward(heads, tok_all, wa_full, g0, segc, segr, bl, tab)
    mine = exchange(nt, attn, 2)
    layer_out, grad_one, denc, gain12, dmine, gb = middle(
        heads, ff, tokens, enc_all.reshape(nt * encoder.shape[0], width), mine, out_grad, gains, wb_full
    )
    dattn = exchange(nt, dmine, 3)
    u, ga, gain0, table = self_backward(
        heads, tok_all, wa_full, g0, segc, segr, bl, tab, qkv, attn, lse, dattn
    )
    gg = jnp.concatenate([gain0, gain12[0:2]], axis=0).T.astype(BF)
    lane = used - (cols - 128)
    gg = jnp.pad(gg, ((0, 0), (lane, 128 - lane - 3))).reshape(nd, part, 128)
    gsum, asum, usum, esum = scatter_all(
        nt,
        nd,
        gb.reshape(nt, nd, part, cols),
        ga.reshape(nd, part, wa.shape[1]),
        u,
        denc.reshape((nt,) + encoder.shape),
        gg,
        table,
    )
    x = tokens.astype(F32)
    back, _ = norm_back(x, norm_scale(x), g0, usum)
    tokens_grad = grad_one + back
    at = 3 * ff
    ck, cv, cq, co, so = (gsum[:, at + n * hw : at + (n + 1) * hw] for n in range(5))
    return (
        layer_out,
        tokens_grad,
        esum,
        asum[:, :hw],
        asum[:, hw : 2 * hw],
        asum[:, 2 * hw : 3 * hw],
        so.T,
        cq,
        ck,
        cv,
        co.T,
        gsum[:, :ff],
        gsum[:, ff : 2 * ff],
        gsum[:, 2 * ff : 3 * ff].T,
        asum[:heads, 3 * hw : 3 * hw + buckets].T,
        gsum[:, used : used + 3].T,
    )


def solution(mesh):
    rows = P(("dp", "tensor"), None)
    left = P("dp", "tensor")
    right = P("tensor", "dp")
    return jax.shard_map(
        per_device,
        mesh=mesh,
        in_specs=(rows, rows, P("dp", None), P(), rows, left, left, left, right, left, left, left, right, left, left, right)
        + (P(None, "tensor"), P(None, "dp")),
        out_specs=(rows, rows, rows, left, left, left, right, left, left, left, right, left, left, right)
        + (P(None, "tensor"), P(None, "dp")),
        check_vma=False,
    )
```

```python
from functools import partial

import jax
import jax.numpy as jnp
from jax import lax
from jax.experimental import pallas as pl
from jax.experimental.pallas import tpu as pltpu
from jax.sharding import PartitionSpec as P

DK = 64
EPS = 1e-06
MASKED = -1e30
BF = jnp.bfloat16
F32 = jnp.float32
MESH = pl.DeviceIdType.MESH
VMEM = pl.BlockSpec(memory_space=pltpu.VMEM)
ANY = pl.BlockSpec(memory_space=pl.ANY)
LIMIT = 62 * 1024 * 1024
STEP = 256
SPACE = 2
PIECE = 32
TOK0 = 2
TOKR = 1
ROWR = 1


def dot(a, b):
    return jnp.dot(a, b, preferred_element_type=F32)


def dot_nt(a, b):
    return lax.dot_general(a, b, (((1,), (1,)), ((), ())), preferred_element_type=F32)


def dot_tn(a, b):
    return lax.dot_general(a, b, (((0,), (0,)), ((), ())), preferred_element_type=F32)


def norm_scale(x):
    return lax.rsqrt(jnp.mean(x * x, axis=-1, keepdims=True) + EPS)


def norm_back(x, r, g, u):
    w = u * g
    inner = jnp.mean(w * x, axis=-1, keepdims=True)
    return r * w - x * (r * r * r * inner), jnp.sum(u * (x * r), axis=0, keepdims=True)


def flip(index, bit):
    size = 1 << bit
    return index + size - 2 * size * lax.rem(index // size, 2)


def flip_all(index, mask):
    bit = 0
    while mask:
        if mask & 1:
            index = flip(index, bit)
        mask >>= 1
        bit += 1
    return index


def subsets(bits):
    out = [0]
    for b in bits:
        out = out + [m | (1 << b) for m in out]
    return out


def bit_orders(count):
    upper = list(range(1, count))
    return [upper + [0], upper[::-1] + [0]]


class Sems:
    def __init__(self, ref):
        self.ref = ref
        self.used = 0

    def take(self):
        self.used += 1
        return self.ref.at[self.used - 1]


def wait_bytes(ref, sem):
    pltpu.make_async_copy(ref, ref, sem).wait()


def enter(nt, nd):
    me_t, me_d = lax.axis_index("tensor"), lax.axis_index("dp")
    bar = pltpu.get_barrier_semaphore()
    bits = nd.bit_length() - 1
    for b in range(bits):
        pl.semaphore_signal(bar, 1, device_id={"dp": flip(me_d, b)}, device_id_type=MESH)

    @pl.when(me_t > 0)
    def _():
        pl.semaphore_signal(bar, 1, device_id={"tensor": me_t - 1}, device_id_type=MESH)

    @pl.when(me_t < nt - 1)
    def _():
        pl.semaphore_signal(bar, 1, device_id={"tensor": me_t + 1}, device_id_type=MESH)

    pl.semaphore_wait(bar, bits + (me_t + nt - 1) // nt + (2 * nt - 2 - me_t) // nt)
    return me_t, me_d


def run_jobs(jobs, after):
    events = []
    for number, (start, stages, ticks) in enumerate(jobs):
        for tick, stage in zip(ticks, stages, strict=True):
            events.append((start + tick, start, number, stage))
    for event in sorted(events, key=lambda e: e[:3]):
        event[3]()
    for fn in after:
        fn()


def line_gather(nt, me, own, slot, sends, recvs, after):
    sem = {(s, j): (sends.take(), recvs.take()) for s in (1, -1) for j in range(1, nt)}

    def send(side, j):
        block = me - side * (j - 1)
        target = me + side
        ok = (block >= 0) & (block < nt) & (target >= 0) & (target < nt)
        src = own if j == 1 else slot(jnp.clip(block, 0, nt - 1))
        dst = slot(jnp.clip(block, 0, nt - 1))
        ss, rs = sem[side, j]

        @pl.when(ok)
        def _():
            pltpu.make_async_remote_copy(
                src, dst, ss, rs, device_id={"tensor": target}, device_id_type=MESH
            ).start()

        def done():
            @pl.when(ok)
            def _():
                wait_bytes(own, ss)

        after.append(done)

    def arrive(side, j):
        block = me - side * j

        @pl.when((block >= 0) & (block < nt))
        def _():
            wait_bytes(own, sem[side, j][1])

    def stage(j):
        def run():
            for side in (1, -1):
                if j > 0:
                    arrive(side, j)
                if j < nt - 1:
                    send(side, j + 1)

        return run

    return [stage(j) for j in range(nt)]


def cube_gather(nd, me, order, own, slot, slots, sends, recvs, after):
    count = len(order)
    sem = [(sends.take(), recvs.take()) for _ in range(count)]

    def start(k):
        bit = order[k]
        for m in subsets(order[:k]):
            block = flip_all(me, m)
            src = own if (m == 0 and own is not None) else slot(block)
            pltpu.make_async_remote_copy(
                src, slot(block), sem[k][0], sem[k][1], device_id={"dp": flip(me, bit)}, device_id_type=MESH
            ).start()

        def done():
            wait_bytes(slots(1 << k), sem[k][0])

        after.append(done)

    def stage(k):
        def run():
            if k > 0:
                wait_bytes(slots(1 << (k - 1)), sem[k - 1][1])
            if k < count:
                start(k)

        return run

    return [stage(k) for k in range(count + 1)]


def gather_kernel(
    nt, nd, tok_ref, enc_ref, wa_ref, wb_ref, tok_out, enc_out, wa_out, wb_out, ssem, rsem, lsem
):
    me_t, me_d = enter(nt, nd)
    bits = nd.bit_length() - 1
    sends, recvs, after = Sems(ssem), Sems(rsem), []
    locals_ = [
        (tok_ref, tok_out.at[me_t]),
        (enc_ref, enc_out.at[me_t]),
        (wa_ref, wa_out.at[me_d]),
        (wb_ref, wb_out.at[me_t, me_d]),
    ]
    for n, (src, dst) in enumerate(locals_):
        pltpu.make_async_copy(src, dst, lsem.at[n]).start()
    orders = bit_orders(bits)
    cols = wb_ref.shape[1]
    chunks = cols // STEP
    half = STEP // 2
    jobs = []
    jobs.append(
        (
            0,
            cube_gather(nd, me_d, orders[0], wa_ref, lambda d: wa_out.at[d], lambda n: wa_out.at[pl.ds(0, n)], sends, recvs, after),
            [SPACE * k for k in range(bits + 1)],
        )
    )

    def chunk_job(c):
        first = c * STEP
        z = line_gather(
            nt,
            me_t,
            wb_ref.at[:, pl.ds(first, STEP)],
            lambda t: wb_out.at[t, me_d, :, pl.ds(first, STEP)],
            sends,
            recvs,
            after,
        )
        cubes = []
        for n in range(2):
            at = first + n * half
            cubes.append(
                cube_gather(
                    nd,
                    me_d,
                    orders[n],
                    None,
                    lambda d, at=at: wb_out.at[:, d, :, pl.ds(at, half)],
                    lambda k, at=at: wb_out.at[:, pl.ds(0, k), :, pl.ds(at, half)],
                    sends,
                    recvs,
                    after,
                )
            )

        def meet():
            z[-1]()
            for q in cubes:
                q[0]()

        def both(k):
            def run():
                for q in cubes:
                    q[k]()

            return run

        return z[:-1] + [meet] + [both(k) for k in range(1, bits + 1)]


    def row_job(ref, out, n):
        at = pl.ds(n * PIECE, PIECE)
        return line_gather(nt, me_t, ref.at[at], lambda t: out.at[t, at], sends, recvs, after)

    ticks = list(range(nt)) + [nt - 1 + SPACE * k for k in range(1, bits + 1)]
    for c in range(chunks):
        jobs.append((c, chunk_job(c), ticks))
    number = TOK0
    for ref, out in ((tok_ref, tok_out), (enc_ref, enc_out)):
        for n in range(ref.shape[0] // PIECE):
            jobs.append((number // TOKR, row_job(ref, out, n), list(range(nt))))
            number += 1
    pltpu.make_async_copy(wb_ref, wb_out.at[me_t, me_d], lsem.at[3]).wait()
    for n in range(3):
        src, dst = locals_[n]
        after.append(lambda n=n, src=src, dst=dst: pltpu.make_async_copy(src, dst, lsem.at[n]).wait())
    run_jobs(jobs, after)


def gather_all(nt, nd, tok, enc, wa, wb):
    bits = nd.bit_length() - 1
    chunks = wb.shape[1] // STEP
    lines = chunks + (tok.shape[0] + enc.shape[0]) // PIECE
    total = lines * 2 * (nt - 1) + (2 * chunks + 1) * bits
    return pl.pallas_call(
        partial(gather_kernel, nt, nd),
        out_shape=(
            jax.ShapeDtypeStruct((nt,) + tok.shape, BF),
            jax.ShapeDtypeStruct((nt,) + enc.shape, BF),
            jax.ShapeDtypeStruct((nd,) + wa.shape, BF),
            jax.ShapeDtypeStruct((nt, nd) + wb.shape, BF),
        ),
        in_specs=[VMEM] * 4,
        out_specs=(ANY,) * 4,
        scratch_shapes=[
            pltpu.SemaphoreType.DMA((total,)),
            pltpu.SemaphoreType.DMA((total,)),
            pltpu.SemaphoreType.DMA((4,)),
        ],
        compiler_params=pltpu.CompilerParams(collective_id=0, has_side_effects=True),
        name="gather_all",
    )(tok, enc, wa, wb)


def exchange_kernel(nt, x_ref, o_ref, ssem, rsem, lsem):
    me = lax.axis_index("tensor")
    bar = pltpu.get_barrier_semaphore()
    for k in range(1, nt):
        pl.semaphore_signal(bar, 1, device_id={"tensor": lax.rem(me + k, nt)}, device_id_type=MESH)
    pl.semaphore_wait(bar, nt - 1)
    local = pltpu.make_async_copy(x_ref.at[me], o_ref.at[me], lsem)
    local.start()
    copies = []
    for k in range(1, nt):
        peer = lax.rem(me + k, nt)
        copy = pltpu.make_async_remote_copy(
            x_ref.at[peer], o_ref.at[me], ssem.at[k], rsem.at[k], device_id={"tensor": peer}, device_id_type=MESH
        )
        copy.start()
        copies.append(copy)
    local.wait()
    for copy in copies:
        copy.wait()


def exchange(nt, x, ident):
    return pl.pallas_call(
        partial(exchange_kernel, nt),
        out_shape=jax.ShapeDtypeStruct(x.shape, x.dtype),
        in_specs=[VMEM],
        out_specs=VMEM,
        scratch_shapes=[
            pltpu.SemaphoreType.DMA((nt,)),
            pltpu.SemaphoreType.DMA((nt,)),
            pltpu.SemaphoreType.DMA,
        ],
        compiler_params=pltpu.CompilerParams(collective_id=ident, has_side_effects=True),
        name="exchange",
    )(x)


def cube_scatter(nd, me, order, value, recv, sends, recvs, after):
    count = len(order)
    sem = [(sends.take(), recvs.take()) for _ in range(count)]

    def start(k):
        bit = order[k]
        peer = flip(me, bit)
        for j, m in enumerate(subsets(order[k + 1 :])):
            pltpu.make_async_remote_copy(
                value(flip_all(peer, m)),
                recv[k].at[j],
                sem[k][0],
                sem[k][1],
                device_id={"dp": peer},
                device_id_type=MESH,
            ).start()

        def done():
            wait_bytes(recv[k], sem[k][0])

        after.append(done)

    def land(k):
        wait_bytes(recv[k], sem[k][1])
        for j, m in enumerate(subsets(order[k + 1 :])):
            ref = value(flip_all(me, m))
            got = recv[k].at[j]
            if len(ref.shape) == 2:
                ref[...] = (ref[...].astype(F32) + got[...].astype(F32)).astype(BF)
            else:
                for t in range(ref.shape[0]):
                    ref[t] = (ref[t].astype(F32) + got[t].astype(F32)).astype(BF)

    def stage(k):
        def run():
            if k > 0:
                land(k - 1)
            if k < count:
                start(k)

        return run

    return [stage(k) for k in range(count + 1)]


def line_scatter(nt, me, value, recv, finish, sends, recvs, after):
    sem = {(s, b): (sends.take(), recvs.take()) for s in (0, 1) for b in range(nt)}

    def hop(z):
        def run():
            for side, here in ((0, z), (1, nt - 1 - z)):
                goal = here + 1 if side == 0 else here - 1
                blocks = range(here + 1, nt) if side == 0 else range(here - 1, -1, -1)

                @pl.when(me == here)
                def _(side=side, goal=goal, blocks=blocks):
                    for b in blocks:
                        ref = value(b)
                        if z > 0:
                            got = recv.at[side, b]
                            wait_bytes(got, sem[side, b][1])
                            ref[...] = (ref[...].astype(F32) + got[...].astype(F32)).astype(BF)
                        pltpu.make_async_remote_copy(
                            ref,
                            recv.at[side, b],
                            sem[side, b][0],
                            sem[side, b][1],
                            device_id={"tensor": goal},
                            device_id_type=MESH,
                        ).start()

        return run

    def last():
        for here in range(nt):

            @pl.when(me == here)
            def _(here=here):
                if here > 0:
                    wait_bytes(recv.at[0, here], sem[0, here][1])
                if here < nt - 1:
                    wait_bytes(recv.at[1, here], sem[1, here][1])
                total = value(here)[...].astype(F32)
                if here > 0:
                    total = total + recv.at[0, here][...].astype(F32)
                if here < nt - 1:
                    total = total + recv.at[1, here][...].astype(F32)
                finish(total)

    def done():
        for here in range(nt):

            @pl.when(me == here)
            def _(here=here):
                for b in range(here + 1, nt):
                    wait_bytes(recv.at[0, b], sem[0, b][0])
                for b in range(here):
                    wait_bytes(recv.at[1, b], sem[1, b][0])

    after.append(done)
    return [hop(z) for z in range(nt - 1)] + [last]


def scatter_kernel(
    nt,
    nd,
    g_ref,
    a_ref,
    u_ref,
    e_ref,
    gg_ref,
    tt_ref,
    g_out,
    a_out,
    u_out,
    e_out,
    *scratch,
):
    bits = nd.bit_length() - 1
    gv, uz, ez, gz = scratch[:4]
    arecv = scratch[4 : 4 + bits]
    grecv = scratch[4 + bits : 4 + 2 * bits]
    ssem, rsem, lsem = scratch[4 + 2 * bits :]
    cols = g_ref.shape[3]
    chunks = cols // STEP
    half = STEP // 2
    for c in range(chunks):
        at = pl.ds(c * STEP, STEP)
        pltpu.make_async_copy(g_ref.at[:, :, :, at], gv.at[:, :, :, at], lsem.at[c]).start()
    me_t, me_d = enter(nt, nd)
    sends, recvs, after = Sems(ssem), Sems(rsem), []
    orders = [[0] + o[:-1][::-1] for o in bit_orders(bits)]
    heads = tt_ref.shape[0]
    wide = a_ref.shape[2]
    for d in range(nd):
        a_ref[d, :heads, wide - 128 :] = tt_ref[...].astype(BF)
    jobs = []

    def a_done():
        a_out[...] = a_ref[me_d].astype(F32)

    a_job = cube_scatter(nd, me_d, orders[0], lambda d: a_ref.at[d], arecv, sends, recvs, after) + [a_done]

    def chunk_job(c):
        first = c * STEP
        cubes = []
        for n in range(2):
            at = first + n * half
            cubes.append(
                cube_scatter(
                    nd,
                    me_d,
                    orders[n],
                    lambda d, at=at: gv.at[:, d, :, pl.ds(at, half)],
                    [r.at[2 * c + n] for r in grecv],
                    sends,
                    recvs,
                    after,
                )
            )

        def finish(total):
            g_out[:, first : first + STEP] = total

        z = line_scatter(
            nt,
            me_t,
            lambda b: gv.at[b, me_d, :, pl.ds(first, STEP)],
            gz.at[c],
            finish,
            sends,
            recvs,
            after,
        )

        def begin():
            at = pl.ds(first, STEP)
            pltpu.make_async_copy(g_ref.at[:, :, :, at], gv.at[:, :, :, at], lsem.at[c]).wait()
            if c == chunks - 1:
                for t in range(nt):
                    for d in range(nd):
                        gv[t, d, :, cols - 128 :] = gv[t, d, :, cols - 128 :] + gg_ref[d]
            for q in cubes:
                q[0]()

        def both(k):
            def run():
                for q in cubes:
                    q[k]()

            return run

        def meet():
            for q in cubes:
                q[bits]()
            z[0]()

        return [begin] + [both(k) for k in range(1, bits)] + [meet] + z[1:]

    def row_job(ref, recv, out, n):
        at = pl.ds(n * PIECE, PIECE)

        def finish(total):
            out[at, :] = total

        return line_scatter(nt, me_t, lambda b: ref.at[b, at], recv.at[:, :, at], finish, sends, recvs, after)

    ticks = [SPACE * k for k in range(bits)] + [SPACE * bits + k for k in range(nt)]
    jobs.append((0, a_job, [SPACE * k for k in range(bits + 1)] + [SPACE * bits]))
    for c in range(chunks):
        jobs.append((c, chunk_job(c), ticks))
    number = 0
    for ref, recv, out in ((u_ref, uz, u_out), (e_ref, ez, e_out)):
        for n in range(out.shape[0] // PIECE):
            jobs.append((number // ROWR, row_job(ref, recv, out, n), list(range(nt))))
            number += 1
    run_jobs(jobs, after)


def scatter_all(nt, nd, g, a, u, e, gg, tt):
    bits = nd.bit_length() - 1
    rows, cols = g.shape[2:]
    wide = a.shape[2]
    chunks = cols // STEP
    lines = chunks + (u.shape[1] + e.shape[1]) // PIECE
    total = lines * 2 * nt + (2 * chunks + 1) * bits
    return pl.pallas_call(
        partial(scatter_kernel, nt, nd),
        out_shape=(
            jax.ShapeDtypeStruct((rows, cols), F32),
            jax.ShapeDtypeStruct((rows, wide), F32),
            jax.ShapeDtypeStruct(u.shape[1:], F32),
            jax.ShapeDtypeStruct(e.shape[1:], F32),
        ),
        in_specs=[ANY] + [VMEM] * 5,
        out_specs=(VMEM,) * 4,
        scratch_shapes=[
            pltpu.VMEM((nt, nd, rows, cols), BF),
            pltpu.VMEM((2,) + u.shape, BF),
            pltpu.VMEM((2,) + e.shape, BF),
            pltpu.VMEM((chunks, 2, nt, rows, STEP), BF),
        ]
        + [pltpu.VMEM((1 << (bits - 1 - k), rows, wide), BF) for k in range(bits)]
        + [pltpu.VMEM((2 * chunks, 1 << (bits - 1 - k), nt, rows, STEP // 2), BF) for k in range(bits)]
        + [
            pltpu.SemaphoreType.DMA((total,)),
            pltpu.SemaphoreType.DMA((total,)),
            pltpu.SemaphoreType.DMA((chunks,)),
        ],
        compiler_params=pltpu.CompilerParams(collective_id=1, has_side_effects=True, vmem_limit_bytes=LIMIT),
        name="scatter_all",
    )(g, a, u, e, gg, tt)


def build_strips(strip, line, heads):
    block = strip.shape[1]
    width = strip.shape[2]
    row = lax.broadcasted_iota(jnp.int32, (8, width), 0)
    for h in range(heads):
        x = jnp.broadcast_to(line[h : h + 1, :], (8, width))
        for b in range(3):
            x = jnp.where((row >> b) % 2 == 1, pltpu.roll(x, 1 << b, 1), x)
        strip[h, 0:8, :] = x
        n = 8
        while n < block:
            strip[h, n : 2 * n, :] = pltpu.roll(strip[h, 0:n, :], n, 1)
            n *= 2


def bias_lines(bl_ref, tab_ref):
    width = bl_ref.shape[1]
    buckets = tab_ref.shape[1]
    hot = bl_ref[...] == lax.broadcasted_iota(jnp.int32, (buckets, width), 0)
    line = dot(tab_ref[...], hot.astype(F32).astype(BF))
    return jnp.where(bl_ref[...] >= 0, line, MASKED), hot


def self_forward_kernel(
    heads, tok_ref, wa_ref, g_ref, segc_ref, segr_ref, bl_ref, tab_ref, qkv_ref, attn_ref, lse_ref, strip, qs, ks, vs, os
):
    nt, block = tok_ref.shape[:2]
    hw = heads * DK
    line, _ = bias_lines(bl_ref, tab_ref)
    build_strips(strip, line, heads)
    for i in range(nt):
        x = tok_ref[i].astype(F32)
        n = (x * norm_scale(x) * g_ref[...]).astype(BF)
        y = dot(n, wa_ref[:, : 3 * hw]).astype(BF)
        qkv_ref[i] = y
        for h in range(heads):
            for which, ref in enumerate((qs, ks, vs)):
                at = which * hw + h * DK
                ref[h, i * block : (i + 1) * block, :] = y[:, at : at + DK]

    def head(h, carry):
        for i in range(nt):
            mine = slice(i * block, (i + 1) * block)
            seen = (i + 1) * block
            s = dot_nt(qs[h, mine, :], ks[h, :seen, :])
            s = s + strip[h, :, (nt - 1 - i) * block : (nt - 1 - i) * block + seen]
            s = jnp.where(segc_ref[mine, :] == segr_ref[:, :seen], s, MASKED)
            top = jnp.max(s, axis=-1, keepdims=True)
            p = jnp.exp(s - top)
            total = jnp.sum(p, axis=-1, keepdims=True)
            o = dot(p.astype(BF), vs[h, :seen, :]) / total
            os[h, mine, :] = o
            lse_ref[h, mine, :] = top + jnp.log(total)
        return carry

    lax.fori_loop(0, heads, head, 0)
    for i in range(nt):
        mine = slice(i * block, (i + 1) * block)
        attn_ref[i] = jnp.concatenate([os[h, mine, :] for h in range(heads)], axis=1).astype(BF)


def self_forward(heads, tok, wa, g, segc, segr, bl, tab):
    nt, block, width = tok.shape
    length = nt * block
    hw = heads * DK
    return pl.pallas_call(
        partial(self_forward_kernel, heads),
        out_shape=(
            jax.ShapeDtypeStruct((nt, block, 3 * hw), BF),
            jax.ShapeDtypeStruct((nt, block, hw), BF),
            jax.ShapeDtypeStruct((heads, length, 1), F32),
        ),
        in_specs=[VMEM] * 7,
        out_specs=(VMEM,) * 3,
        scratch_shapes=[pltpu.VMEM((heads, block, length + block), F32)]
        + [pltpu.VMEM((heads, length, DK), BF)] * 3
        + [pltpu.VMEM((heads, length, DK), F32)],
        compiler_params=pltpu.CompilerParams(vmem_limit_bytes=LIMIT),
        name="self_forward",
    )(tok, wa, g, segc, segr, bl, tab)


def self_backward_kernel(
    heads,
    tok_ref,
    wa_ref,
    g_ref,
    segc_ref,
    segr_ref,
    bl_ref,
    tab_ref,
    qkv_ref,
    attn_ref,
    lse_ref,
    dattn_ref,
    u_ref,
    ga_ref,
    gain_ref,
    table_ref,
    strip,
    dstrip,
    qs,
    ks,
    vs,
    das,
    delta,
    dq,
    dkt,
    dvt,
    norms,
    dqkv,
):
    nt, block = tok_ref.shape[:2]
    hw = heads * DK
    length = nt * block
    line, hot = bias_lines(bl_ref, tab_ref)
    build_strips(strip, line, heads)
    for i in range(nt):
        mine = slice(i * block, (i + 1) * block)
        y = qkv_ref[i]
        da = dattn_ref[i]
        prod = da.astype(F32) * attn_ref[i].astype(F32)
        for h in range(heads):
            part = slice(h * DK, (h + 1) * DK)
            for which, ref in enumerate((qs, ks, vs)):
                at = which * hw + h * DK
                ref[h, mine, :] = y[:, at : at + DK]
            das[h, mine, :] = da[:, part]
            delta[h, mine, :] = jnp.sum(prod[:, part], axis=1, keepdims=True)
    dstrip[...] = jnp.zeros_like(dstrip)
    dkt[...] = jnp.zeros_like(dkt)
    dvt[...] = jnp.zeros_like(dvt)

    def head(h, carry):
        for i in range(nt):
            mine = slice(i * block, (i + 1) * block)
            seen = (i + 1) * block
            off = (nt - 1 - i) * block
            q = qs[h, mine, :]
            da = das[h, mine, :]
            s = dot_nt(q, ks[h, :seen, :])
            s = s + strip[h, :, off : off + seen]
            s = jnp.where(segc_ref[mine, :] == segr_ref[:, :seen], s, MASKED)
            p = jnp.exp(s - lse_ref[h, mine, :])
            dp = dot_nt(da, vs[h, :seen, :])
            ds = p * (dp - delta[h, mine, :])
            low = ds.astype(BF)
            dq[h, mine, :] = dot(low, ks[h, :seen, :])
            dkt[h, :, :seen] += dot_tn(q, low)
            dvt[h, :, :seen] += dot_tn(da, p.astype(BF))
            dstrip[h, :, off : off + seen] += ds
        return carry

    lax.fori_loop(0, heads, head, 0)
    lines = []
    for h in range(heads):
        n = block // 2
        while n >= 8:
            dstrip[h, 0:n, :] = dstrip[h, 0:n, :] + pltpu.roll(dstrip[h, n : 2 * n, :], length + block - n, 1)
            n //= 2
        x = dstrip[h, 0:8, :]
        row = lax.broadcasted_iota(jnp.int32, x.shape, 0)
        for b in range(3):
            x = jnp.where((row >> b) % 2 == 1, pltpu.roll(x, length + block - (1 << b), 1), x)
        lines.append(jnp.sum(x, axis=0, keepdims=True))
    lines = jnp.concatenate(lines + [jnp.zeros((8 - heads, length + block), F32)], axis=0)
    table = lax.dot_general(
        lines,
        hot.astype(F32),
        (((1,), (1,)), ((), ())),
        precision=lax.Precision.HIGHEST,
        preferred_element_type=F32,
    )
    table_ref[...] = jnp.concatenate([table, jnp.zeros((8, 128 - table.shape[1]), F32)], axis=1)
    gain = jnp.zeros(gain_ref.shape, F32)
    for i in range(nt):
        mine = slice(i * block, (i + 1) * block)
        pieces = [dq[h, mine, :] for h in range(heads)]
        pieces += [dkt[h, :, mine].T for h in range(heads)]
        pieces += [dvt[h, :, mine].T for h in range(heads)]
        low = jnp.concatenate(pieces, axis=1).astype(BF)
        dqkv[mine, :] = low
        x = tok_ref[i].astype(F32)
        hat = x * norm_scale(x)
        norms[mine, :] = (hat * g_ref[...]).astype(BF)
        u = dot_nt(low, wa_ref[:, : 3 * hw])
        gain = gain + jnp.sum(u * hat, axis=0, keepdims=True)
        u_ref[i] = u.astype(BF)
    gain_ref[...] = gain
    ga_ref[:, : 3 * hw] = dot_tn(norms[...], dqkv[...]).astype(BF)
    ga_ref[:, 3 * hw :] = jnp.zeros((ga_ref.shape[0], ga_ref.shape[1] - 3 * hw), BF)


def self_backward(heads, tok, wa, g, segc, segr, bl, tab, qkv, attn, lse, dattn):
    nt, block, width = tok.shape
    length = nt * block
    hw = heads * DK
    return pl.pallas_call(
        partial(self_backward_kernel, heads),
        out_shape=(
            jax.ShapeDtypeStruct((nt, block, width), BF),
            jax.ShapeDtypeStruct(wa.shape, BF),
            jax.ShapeDtypeStruct((1, width), F32),
            jax.ShapeDtypeStruct((8, 128), F32),
        ),
        in_specs=[VMEM] * 11,
        out_specs=(VMEM,) * 4,
        scratch_shapes=[pltpu.VMEM((heads, block, length + block), F32)] * 2
        + [pltpu.VMEM((heads, length, DK), BF)] * 4
        + [pltpu.VMEM((heads, length, 1), F32), pltpu.VMEM((heads, length, DK), F32)]
        + [pltpu.VMEM((heads, DK, length), F32)] * 2
        + [pltpu.VMEM((length, width), BF), pltpu.VMEM((length, 3 * hw), BF)],
        compiler_params=pltpu.CompilerParams(vmem_limit_bytes=LIMIT),
        name="self_backward",
    )(tok, wa, g, segc, segr, bl, tab, qkv, attn, lse, dattn)


def middle_kernel(
    heads,
    ff,
    tok_ref,
    enc_ref,
    attn_ref,
    og_ref,
    gains_ref,
    w_hbm,
    layer_ref,
    one_ref,
    denc_ref,
    gain_ref,
    dattn_ref,
    g_hbm,
    w,
    g,
    h1_ref,
    h2_ref,
    n1_ref,
    n2_ref,
    acc_ref,
    dn_ref,
    g2_ref,
    denc,
    qc,
    kv,
    ac,
    oc,
    lse,
    dkv,
    insem,
    outsem,
):
    nt = w.shape[0]
    hw = heads * DK
    cols = w.shape[2]
    f0, f1, f2 = 0, ff, 2 * ff
    kv0 = 3 * ff
    q0 = kv0 + 2 * hw
    c0 = q0 + hw
    s0 = c0 + hw
    end = s0 + hw
    ffn = pl.ds(0, 3 * ff)
    att = pl.ds(3 * ff, cols - 3 * ff)
    loads = [pltpu.make_async_copy(w_hbm.at[t, :, att], w.at[t, :, att], insem.at[0, t]) for t in range(nt)]
    loads += [pltpu.make_async_copy(w_hbm.at[t, :, ffn], w.at[t, :, ffn], insem.at[1, t]) for t in range(nt)]
    for copy in loads:
        copy.start()

    def load_wait(which, t):
        at = att if which == 0 else ffn
        pltpu.make_async_copy(w_hbm.at[t, :, at], w.at[t, :, at], insem.at[which, t]).wait()

    def store(which, t):
        at = att if which == 0 else ffn
        return pltpu.make_async_copy(g.at[t, :, at], g_hbm.at[t, :, at], outsem.at[which, t])

    acc_ref[...] = tok_ref[...].astype(F32)

    def self_out(t, carry):
        load_wait(0, t)
        acc_ref[...] += dot_nt(attn_ref[t], w[t, :, s0:end])
        return carry

    lax.fori_loop(0, nt, self_out, 0)
    h1 = acc_ref[...]
    h1_ref[...] = h1
    n1_ref[...] = (h1 * norm_scale(h1) * gains_ref[1:2, :]).astype(BF)

    def cross(t, carry):
        q = dot(n1_ref[...], w[t, :, q0:c0]).astype(BF)
        both = dot(enc_ref[...], w[t, :, kv0:q0]).astype(BF)
        qc[t] = q
        kv[t] = both
        outs = []
        for h in range(heads):
            part = slice(h * DK, (h + 1) * DK)
            s = dot_nt(q[:, part], both[:, part])
            top = jnp.max(s, axis=-1, keepdims=True)
            p = jnp.exp(s - top)
            total = jnp.sum(p, axis=-1, keepdims=True)
            lse[t, h] = top + jnp.log(total)
            outs.append(dot(p.astype(BF), both[:, hw + h * DK : hw + (h + 1) * DK]) / total)
        a = jnp.concatenate(outs, axis=1).astype(BF)
        ac[t] = a
        acc_ref[...] += dot_nt(a, w[t, :, c0:s0])
        return carry

    lax.fori_loop(0, nt, cross, 0)
    h2 = acc_ref[...]
    h2_ref[...] = h2
    n2_ref[...] = (h2 * norm_scale(h2) * gains_ref[2:3, :]).astype(BF)
    dn_ref[...] = jnp.zeros_like(dn_ref)

    def units(t, carry):
        load_wait(1, t)
        n2 = n2_ref[...]
        og = og_ref[...]
        gate = dot(n2, w[t, :, f0:f1])
        up = dot(n2, w[t, :, f1:f2])
        dinner = dot(og, w[t, :, f2 : 3 * ff])
        sq = gate * gate
        th = jnp.tanh(0.7978845608028654 * (gate + 0.044715 * (gate * sq)))
        cdf = 0.5 * (1.0 + th)
        act = gate * cdf
        slope = cdf + gate * (0.5 * (1.0 - th * th)) * (0.7978845608028654 * (1.0 + 0.134145 * sq))
        inner = (act * up).astype(BF)
        dgate = (dinner * up * slope).astype(BF)
        dup = (dinner * act).astype(BF)
        acc_ref[...] += dot_nt(inner, w[t, :, f2 : 3 * ff])
        dn_ref[...] += dot_nt(dgate, w[t, :, f0:f1]) + dot_nt(dup, w[t, :, f1:f2])
        g[t, :, f0:f1] = dot_tn(n2, dgate).astype(BF)
        g[t, :, f1:f2] = dot_tn(n2, dup).astype(BF)
        g[t, :, f2 : 3 * ff] = dot_tn(og, inner).astype(BF)
        store(1, t).start()
        return carry

    lax.fori_loop(0, nt, units, 0)
    layer_ref[...] = acc_ref[...].astype(BF)
    h2 = h2_ref[...]
    back, gain2 = norm_back(h2, norm_scale(h2), gains_ref[2:3, :], dn_ref[...])
    g2 = og_ref[...].astype(F32) + back
    acc_ref[...] = g2
    g2_ref[...] = g2.astype(BF)
    dn_ref[...] = jnp.zeros_like(dn_ref)
    denc[...] = jnp.zeros_like(denc)

    def cross_back(t, carry):
        g2 = g2_ref[...]
        a = ac[t]
        da = dot(g2, w[t, :, c0:s0]).astype(BF)
        g[t, :, c0:s0] = dot_tn(g2, a).astype(BF)
        prod = da.astype(F32) * a.astype(F32)
        q = qc[t]
        both = kv[t]
        dqs = []
        for h in range(heads):
            part = slice(h * DK, (h + 1) * DK)
            qh, kh = q[:, part], both[:, part]
            vh, dah = both[:, hw + h * DK : hw + (h + 1) * DK], da[:, part]
            p = jnp.exp(dot_nt(qh, kh) - lse[t, h])
            delta = jnp.sum(prod[:, part], axis=1, keepdims=True)
            ds = (p * (dot_nt(dah, vh) - delta)).astype(BF)
            dqs.append(dot(ds, kh))
            dkv[h * DK : (h + 1) * DK, :] = dot_tn(qh, ds)
            dkv[hw + h * DK : hw + (h + 1) * DK, :] = dot_tn(dah, p.astype(BF))
        dq = jnp.concatenate(dqs, axis=1).astype(BF)
        dboth = dkv[...].astype(BF)
        g[t, :, q0:c0] = dot_tn(n1_ref[...], dq).astype(BF)
        g[t, :, kv0:q0] = lax.dot_general(
            enc_ref[...], dboth, (((0,), (1,)), ((), ())), preferred_element_type=F32
        ).astype(BF)
        dn_ref[...] += dot_nt(dq, w[t, :, q0:c0])
        denc[...] += lax.dot_general(
            dboth, w[t, :, kv0:q0], (((0,), (1,)), ((), ())), preferred_element_type=F32
        )
        return carry

    lax.fori_loop(0, nt, cross_back, 0)
    denc_ref[...] = denc[...].astype(BF)
    h1 = h1_ref[...]
    back, gain1 = norm_back(h1, norm_scale(h1), gains_ref[1:2, :], dn_ref[...])
    g1 = acc_ref[...] + back
    one_ref[...] = g1
    g2_ref[...] = g1.astype(BF)
    gain_ref[...] = jnp.concatenate([gain1, gain2, jnp.zeros((6, gain1.shape[1]), F32)], axis=0)

    def self_out_back(t, carry):
        low = g2_ref[...]
        dattn_ref[t] = dot(low, w[t, :, s0:end]).astype(BF)
        tail = dot_tn(low, attn_ref[t])
        g[t, :, s0:cols] = jnp.concatenate([tail, jnp.zeros((tail.shape[0], cols - end), F32)], axis=1).astype(BF)
        store(0, t).start()
        return carry

    lax.fori_loop(0, nt, self_out_back, 0)
    for t in range(nt):
        store(1, t).wait()
        store(0, t).wait()


def middle(heads, ff, tok, enc, attn, og, gains, w):
    nt, _, cols = w.shape
    rows, width = tok.shape
    states = enc.shape[0]
    hw = heads * DK
    return pl.pallas_call(
        partial(middle_kernel, heads, ff),
        out_shape=(
            jax.ShapeDtypeStruct((rows, width), BF),
            jax.ShapeDtypeStruct((rows, width), F32),
            jax.ShapeDtypeStruct((states, width), BF),
            jax.ShapeDtypeStruct((8, width), F32),
            jax.ShapeDtypeStruct((nt, rows, hw), BF),
            jax.ShapeDtypeStruct(w.shape, BF),
        ),
        in_specs=[VMEM] * 5 + [ANY],
        out_specs=(VMEM,) * 5 + (ANY,),
        scratch_shapes=[
            pltpu.VMEM(w.shape, BF),
            pltpu.VMEM(w.shape, BF),
            pltpu.VMEM((rows, width), F32),
            pltpu.VMEM((rows, width), F32),
            pltpu.VMEM((rows, width), BF),
            pltpu.VMEM((rows, width), BF),
            pltpu.VMEM((rows, width), F32),
            pltpu.VMEM((rows, width), F32),
            pltpu.VMEM((rows, width), BF),
            pltpu.VMEM((states, width), F32),
            pltpu.VMEM((nt, rows, hw), BF),
            pltpu.VMEM((nt, states, 2 * hw), BF),
            pltpu.VMEM((nt, rows, hw), BF),
            pltpu.VMEM((8, 128), F32),
            pltpu.VMEM((nt, heads, rows, 1), F32),
            pltpu.VMEM((2 * hw, states), F32),
            pltpu.SemaphoreType.DMA((2, nt)),
            pltpu.SemaphoreType.DMA((2, nt)),
        ],
        compiler_params=pltpu.CompilerParams(vmem_limit_bytes=LIMIT),
        name="middle",
    )(tok, enc, attn, og, gains, w)


def per_device(
    tokens,
    encoder,
    segments,
    rel_bucket,
    out_grad,
    self_q,
    self_k,
    self_v,
    self_o,
    cross_q,
    cross_k,
    cross_v,
    cross_o,
    ffn_gate,
    ffn_up,
    ffn_down,
    bias_table,
    norm_gains,
):
    nt, nd = lax.axis_size("tensor"), lax.axis_size("dp")
    part, hw = self_q.shape
    ff = ffn_gate.shape[1]
    heads = hw // DK
    rows, width = tokens.shape
    length = rows * nt
    buckets = bias_table.shape[0]
    wa = jnp.concatenate([self_q, self_k, self_v, jnp.pad(norm_gains.T, ((0, 0), (0, 128 - norm_gains.shape[0])))], axis=1)
    wb = jnp.concatenate([ffn_gate, ffn_up, ffn_down.T, cross_k, cross_v, cross_q, cross_o.T, self_o.T], axis=1)
    used = wb.shape[1]
    cols = -(-(used + 3) // STEP) * STEP
    wb = jnp.pad(wb, ((0, 0), (0, cols - used)))
    tok_all, enc_all, wa_all, wb_all = gather_all(nt, nd, tokens, encoder, wa, wb)
    wa_full = wa_all.reshape(nd * part, wa.shape[1])
    wb_full = wb_all.reshape(nt, nd * part, cols)
    gains = jnp.pad(wa_full[:, 3 * hw : 3 * hw + 3].T.astype(F32), ((0, 5), (0, 0)))
    top = (nt - 1) * rows
    blank = jnp.full((length - 1 - top,), -1, jnp.int32)
    bl = jnp.concatenate(
        [rel_bucket[: top + 1][::-1], blank, jnp.full((1,), -1, jnp.int32), rel_bucket[top + 1 : length][::-1]]
    )[None, :]
    tab = jnp.pad(bias_table.T, ((0, 8 - heads), (0, 0)))
    segr = segments
    segc = segments.T
    g0 = gains[0:1]
    qkv, attn, lse = self_forward(heads, tok_all, wa_full, g0, segc, segr, bl, tab)
    mine = exchange(nt, attn, 2)
    layer_out, grad_one, denc, gain12, dmine, gb = middle(
        heads, ff, tokens, enc_all.reshape(nt * encoder.shape[0], width), mine, out_grad, gains, wb_full
    )
    dattn = exchange(nt, dmine, 3)
    u, ga, gain0, table = self_backward(
        heads, tok_all, wa_full, g0, segc, segr, bl, tab, qkv, attn, lse, dattn
    )
    gg = jnp.concatenate([gain0, gain12[0:2]], axis=0).T.astype(BF)
    lane = used - (cols - 128)
    gg = jnp.pad(gg, ((0, 0), (lane, 128 - lane - 3))).reshape(nd, part, 128)
    gsum, asum, usum, esum = scatter_all(
        nt,
        nd,
        gb.reshape(nt, nd, part, cols),
        ga.reshape(nd, part, wa.shape[1]),
        u,
        denc.reshape((nt,) + encoder.shape),
        gg,
        table,
    )
    x = tokens.astype(F32)
    back, _ = norm_back(x, norm_scale(x), g0, usum)
    tokens_grad = grad_one + back
    at = 3 * ff
    ck, cv, cq, co, so = (gsum[:, at + n * hw : at + (n + 1) * hw] for n in range(5))
    return (
        layer_out,
        tokens_grad,
        esum,
        asum[:, :hw],
        asum[:, hw : 2 * hw],
        asum[:, 2 * hw : 3 * hw],
        so.T,
        cq,
        ck,
        cv,
        co.T,
        gsum[:, :ff],
        gsum[:, ff : 2 * ff],
        gsum[:, 2 * ff : 3 * ff].T,
        asum[:heads, 3 * hw : 3 * hw + buckets].T,
        gsum[:, used : used + 3].T,
    )


def solution(mesh):
    rows = P(("dp", "tensor"), None)
    left = P("dp", "tensor")
    right = P("tensor", "dp")
    return jax.shard_map(
        per_device,
        mesh=mesh,
        in_specs=(rows, rows, P("dp", None), P(), rows, left, left, left, right, left, left, left, right, left, left, right)
        + (P(None, "tensor"), P(None, "dp")),
        out_specs=(rows, rows, rows, left, left, left, right, left, left, left, right, left, left, right)
        + (P(None, "tensor"), P(None, "dp")),
        check_vma=False,
    )
```

```python
from functools import partial

import jax
import jax.numpy as jnp
from jax import lax
from jax.experimental import pallas as pl
from jax.experimental.pallas import tpu as pltpu
from jax.sharding import PartitionSpec as P

DK = 64
EPS = 1e-06
MASKED = -1e30
BF = jnp.bfloat16
F32 = jnp.float32
MESH = pl.DeviceIdType.MESH
VMEM = pl.BlockSpec(memory_space=pltpu.VMEM)
ANY = pl.BlockSpec(memory_space=pl.ANY)
LIMIT = 63 * 1024 * 1024
STEP = 256
SPACE = 2
PIECE = 32
TOK0 = 2
TOKR = 1
CORE0 = 3


def dot(a, b):
    return jnp.dot(a, b, preferred_element_type=F32)


def dot_nt(a, b):
    return lax.dot_general(a, b, (((1,), (1,)), ((), ())), preferred_element_type=F32)


def dot_tn(a, b):
    return lax.dot_general(a, b, (((0,), (0,)), ((), ())), preferred_element_type=F32)


def norm_scale(x):
    return lax.rsqrt(jnp.mean(x * x, axis=-1, keepdims=True) + EPS)


def norm_back(x, r, g, u):
    w = u * g
    inner = jnp.mean(w * x, axis=-1, keepdims=True)
    return r * w - x * (r * r * r * inner), jnp.sum(u * (x * r), axis=0, keepdims=True)


def flip(index, bit):
    size = 1 << bit
    return index + size - 2 * size * lax.rem(index // size, 2)


def flip_all(index, mask):
    bit = 0
    while mask:
        if mask & 1:
            index = flip(index, bit)
        mask >>= 1
        bit += 1
    return index


def subsets(bits):
    out = [0]
    for b in bits:
        out = out + [m | (1 << b) for m in out]
    return out


def bit_orders(count):
    upper = list(range(1, count))
    return [upper + [0], upper[::-1] + [0]]


class Sems:
    def __init__(self, ref):
        self.ref = ref
        self.used = 0

    def take(self):
        self.used += 1
        return self.ref.at[self.used - 1]

    def many(self, count):
        base = self.used
        self.used += count
        return lambda n: self.ref.at[base + n]


def wait_bytes(ref, sem):
    pltpu.make_async_copy(ref, ref, sem).wait()


def row_loop(shape, body):
    size = 32 if shape[1] <= 256 else 16
    if shape[0] % size:
        body(slice(0, shape[0]))
        return

    def step(n, carry):
        body(pl.ds(pl.multiple_of(n * size, size), size))
        return carry

    lax.fori_loop(0, shape[0] // size, step, 0)


def add_into(ref, got):
    if len(ref.shape) == 2:

        def body(at):
            ref[at, :] = ref[at, :] + got[at, :]

        row_loop(ref.shape, body)
    else:

        def step(t, carry):
            ref[t] = ref[t] + got[t]
            return carry

        lax.fori_loop(0, ref.shape[0], step, 0)


def enter(nt, nd, all_tensor=False):
    me_t, me_d = lax.axis_index("tensor"), lax.axis_index("dp")
    bar = pltpu.get_barrier_semaphore()
    bits = nd.bit_length() - 1
    for b in range(bits):
        pl.semaphore_signal(bar, 1, device_id={"dp": flip(me_d, b)}, device_id_type=MESH)
    if all_tensor:
        for k in range(1, nt):
            pl.semaphore_signal(bar, 1, device_id={"tensor": lax.rem(me_t + k, nt)}, device_id_type=MESH)
        pl.semaphore_wait(bar, bits + nt - 1)
        return me_t, me_d

    @pl.when(me_t > 0)
    def _():
        pl.semaphore_signal(bar, 1, device_id={"tensor": me_t - 1}, device_id_type=MESH)

    @pl.when(me_t < nt - 1)
    def _():
        pl.semaphore_signal(bar, 1, device_id={"tensor": me_t + 1}, device_id_type=MESH)

    pl.semaphore_wait(bar, bits + (me_t + nt - 1) // nt + (2 * nt - 2 - me_t) // nt)
    return me_t, me_d


def run_jobs(jobs, after):
    events = []
    for number, (start, stages, ticks) in enumerate(jobs):
        for tick, stage in zip(ticks, stages, strict=True):
            events.append((start + tick, start, number, stage))
    for event in sorted(events, key=lambda e: e[:3]):
        event[3]()
    for fn in after:
        fn()


def line_gather(nt, me, own, slot, sends, recvs, after):
    sem = {(s, j): (sends.take(), recvs.take()) for s in (1, -1) for j in range(1, nt)}

    def send(side, j):
        block = me - side * (j - 1)
        target = me + side
        ok = (block >= 0) & (block < nt) & (target >= 0) & (target < nt)
        src = own if j == 1 else slot(jnp.clip(block, 0, nt - 1))
        dst = slot(jnp.clip(block, 0, nt - 1))
        ss, rs = sem[side, j]

        @pl.when(ok)
        def _():
            pltpu.make_async_remote_copy(
                src, dst, ss, rs, device_id={"tensor": target}, device_id_type=MESH
            ).start()

        def done():
            @pl.when(ok)
            def _():
                wait_bytes(own, ss)

        after.append(done)

    def arrive(side, j):
        block = me - side * j

        @pl.when((block >= 0) & (block < nt))
        def _():
            wait_bytes(own, sem[side, j][1])

    def stage(j):
        def run():
            for side in (1, -1):
                if j > 0:
                    arrive(side, j)
                if j < nt - 1:
                    send(side, j + 1)

        return run

    return [stage(j) for j in range(nt)]


def cube_gather(nd, me, order, own, slot, slots, sends, recvs, after):
    count = len(order)
    sem = [(sends.take(), recvs.take()) for _ in range(count)]

    def start(k):
        bit = order[k]
        for m in subsets(order[:k]):
            block = flip_all(me, m)
            src = own if (m == 0 and own is not None) else slot(block)
            pltpu.make_async_remote_copy(
                src, slot(block), sem[k][0], sem[k][1], device_id={"dp": flip(me, bit)}, device_id_type=MESH
            ).start()

        def done():
            wait_bytes(slots(1 << k), sem[k][0])

        after.append(done)

    def stage(k):
        def run():
            if k > 0:
                wait_bytes(slots(1 << (k - 1)), sem[k - 1][1])
            if k < count:
                start(k)

        return run

    return [stage(k) for k in range(count + 1)]


def gather_kernel(
    nt, nd, tok_ref, enc_ref, wa_ref, wb_ref, tok_out, enc_out, wa_out, wb_out, ssem, rsem, lsem
):
    me_t, me_d = enter(nt, nd)
    bits = nd.bit_length() - 1
    sends, recvs, after = Sems(ssem), Sems(rsem), []
    locals_ = [
        (tok_ref, tok_out.at[me_t]),
        (enc_ref, enc_out.at[me_t]),
        (wa_ref, wa_out.at[me_d]),
        (wb_ref, wb_out.at[me_t, me_d]),
    ]
    for n, (src, dst) in enumerate(locals_):
        pltpu.make_async_copy(src, dst, lsem.at[n]).start()
    orders = bit_orders(bits)
    cols = wb_ref.shape[1]
    chunks = cols // STEP
    half = STEP // 2
    jobs = []
    jobs.append(
        (
            0,
            cube_gather(nd, me_d, orders[0], wa_ref, lambda d: wa_out.at[d], lambda n: wa_out.at[pl.ds(0, n)], sends, recvs, after),
            [SPACE * k for k in range(bits + 1)],
        )
    )

    def chunk_job(c):
        first = c * STEP
        z = line_gather(
            nt,
            me_t,
            wb_ref.at[:, pl.ds(first, STEP)],
            lambda t: wb_out.at[t, me_d, :, pl.ds(first, STEP)],
            sends,
            recvs,
            after,
        )
        cubes = []
        for n in range(2):
            at = first + n * half
            cubes.append(
                cube_gather(
                    nd,
                    me_d,
                    orders[n],
                    None,
                    lambda d, at=at: wb_out.at[:, d, :, pl.ds(at, half)],
                    lambda k, at=at: wb_out.at[:, pl.ds(0, k), :, pl.ds(at, half)],
                    sends,
                    recvs,
                    after,
                )
            )

        def meet():
            z[-1]()
            for q in cubes:
                q[0]()

        def both(k):
            def run():
                for q in cubes:
                    q[k]()

            return run

        return z[:-1] + [meet] + [both(k) for k in range(1, bits + 1)]


    def row_job(ref, out, n):
        at = pl.ds(n * PIECE, PIECE)
        return line_gather(nt, me_t, ref.at[at], lambda t: out.at[t, at], sends, recvs, after)

    ticks = list(range(nt)) + [nt - 1 + SPACE * k for k in range(1, bits + 1)]
    for c in range(chunks):
        jobs.append((c, chunk_job(c), ticks))
    number = TOK0
    for ref, out in ((tok_ref, tok_out), (enc_ref, enc_out)):
        for n in range(ref.shape[0] // PIECE):
            jobs.append((number // TOKR, row_job(ref, out, n), list(range(nt))))
            number += 1
    pltpu.make_async_copy(wb_ref, wb_out.at[me_t, me_d], lsem.at[3]).wait()
    for n in range(3):
        src, dst = locals_[n]
        after.append(lambda n=n, src=src, dst=dst: pltpu.make_async_copy(src, dst, lsem.at[n]).wait())
    run_jobs(jobs, after)


def gather_all(nt, nd, tok, enc, wa, wb):
    bits = nd.bit_length() - 1
    chunks = wb.shape[1] // STEP
    lines = chunks + (tok.shape[0] + enc.shape[0]) // PIECE
    total = lines * 2 * (nt - 1) + (2 * chunks + 1) * bits
    return pl.pallas_call(
        partial(gather_kernel, nt, nd),
        out_shape=(
            jax.ShapeDtypeStruct((nt,) + tok.shape, BF),
            jax.ShapeDtypeStruct((nt,) + enc.shape, BF),
            jax.ShapeDtypeStruct((nd,) + wa.shape, BF),
            jax.ShapeDtypeStruct((nt, nd) + wb.shape, BF),
        ),
        in_specs=[VMEM] * 4,
        out_specs=(ANY,) * 4,
        scratch_shapes=[
            pltpu.SemaphoreType.DMA((total,)),
            pltpu.SemaphoreType.DMA((total,)),
            pltpu.SemaphoreType.DMA((4,)),
        ],
        compiler_params=pltpu.CompilerParams(collective_id=0, has_side_effects=True),
        name="gather_all",
    )(tok, enc, wa, wb)


def exchange_kernel(nt, x_ref, o_ref, ssem, rsem, lsem):
    me = lax.axis_index("tensor")
    bar = pltpu.get_barrier_semaphore()
    for k in range(1, nt):
        pl.semaphore_signal(bar, 1, device_id={"tensor": lax.rem(me + k, nt)}, device_id_type=MESH)
    pl.semaphore_wait(bar, nt - 1)
    local = pltpu.make_async_copy(x_ref.at[me], o_ref.at[me], lsem)
    local.start()
    copies = []
    for k in range(1, nt):
        peer = lax.rem(me + k, nt)
        copy = pltpu.make_async_remote_copy(
            x_ref.at[peer], o_ref.at[me], ssem.at[k], rsem.at[k], device_id={"tensor": peer}, device_id_type=MESH
        )
        copy.start()
        copies.append(copy)
    local.wait()
    for copy in copies:
        copy.wait()


def exchange(nt, x, ident):
    return pl.pallas_call(
        partial(exchange_kernel, nt),
        out_shape=jax.ShapeDtypeStruct(x.shape, x.dtype),
        in_specs=[VMEM],
        out_specs=VMEM,
        scratch_shapes=[
            pltpu.SemaphoreType.DMA((nt,)),
            pltpu.SemaphoreType.DMA((nt,)),
            pltpu.SemaphoreType.DMA,
        ],
        compiler_params=pltpu.CompilerParams(collective_id=ident, has_side_effects=True),
        name="exchange",
    )(x)


def cube_scatter(nd, me, order, value, recv, sends, recvs, after):
    count = len(order)
    sem = [(sends.take(), recvs.take()) for _ in range(count)]

    def start(k):
        bit = order[k]
        peer = flip(me, bit)
        for j, m in enumerate(subsets(order[k + 1 :])):
            pltpu.make_async_remote_copy(
                value(flip_all(peer, m)),
                recv[k].at[j],
                sem[k][0],
                sem[k][1],
                device_id={"dp": peer},
                device_id_type=MESH,
            ).start()

        def done():
            wait_bytes(recv[k], sem[k][0])

        after.append(done)

    def land(k):
        wait_bytes(recv[k], sem[k][1])
        for j, m in enumerate(subsets(order[k + 1 :])):
            add_into(value(flip_all(me, m)), recv[k].at[j])

    def stage(k):
        def run():
            if k > 0:
                land(k - 1)
            if k < count:
                start(k)

        return run

    return [stage(k) for k in range(count + 1)]


def line_scatter(nt, me, value, recv, out, sends, recvs, after):
    ssem, rsem = sends.many(2 * nt), recvs.many(2 * nt)

    def land(side, b):
        return recv.at[b + 1 - side]

    def hop(z):
        def run():
            for side, here in ((0, z), (1, nt - 1 - z)):
                goal = here + 1 if side == 0 else here - 1
                blocks = range(here + 1, nt) if side == 0 else range(here - 1, -1, -1)

                @pl.when(me == here)
                def _(side=side, goal=goal, blocks=blocks):
                    for b in blocks:
                        ref = value(b)
                        if z > 0:
                            got = land(side, b)
                            wait_bytes(got, rsem(side * nt + b))
                            add_into(ref, got)
                        pltpu.make_async_remote_copy(
                            ref,
                            land(side, b),
                            ssem(side * nt + b),
                            rsem(side * nt + b),
                            device_id={"tensor": goal},
                            device_id_type=MESH,
                        ).start()

        return run

    def last():
        own = value(me)

        def first(at):
            out[at, :] = own[at, :].astype(F32)

        row_loop(out.shape, first)
        for side, some in ((0, me > 0), (1, me < nt - 1)):

            @pl.when(some)
            def _(side=side):
                got = land(side, me)
                wait_bytes(got, rsem(side * nt + me))

                def more(at):
                    out[at, :] = out[at, :] + got[at, :].astype(F32)

                row_loop(out.shape, more)

    def done():
        for here in range(nt):

            @pl.when(me == here)
            def _(here=here):
                for b in range(here + 1, nt):
                    wait_bytes(land(0, b), ssem(b))
                for b in range(here):
                    wait_bytes(land(1, b), ssem(nt + b))

    after.append(done)
    return [hop(z) for z in range(nt - 1)] + [last]


def backward_kernel(
    nt,
    nd,
    heads,
    g_used,
    g_ref,
    e_ref,
    gain_in,
    dmine_ref,
    tok_ref,
    wa_ref,
    g0_ref,
    segr_ref,
    bl_ref,
    tab_ref,
    qkv_ref,
    attn_ref,
    lse_ref,
    g_out,
    a_out,
    u_out,
    e_out,
    *scratch,
):
    bits = nd.bit_length() - 1
    gv, uz, ez, gz = scratch[:4]
    arecv = scratch[4 : 4 + bits]
    grecv = scratch[4 + bits : 4 + 2 * bits]
    a_ref, u_ref, da_ref, strips, ks, vs, dkt, dvt, dqkv, lines, gain0 = scratch[4 + 2 * bits : 15 + 2 * bits]
    ssem, rsem, lsem = scratch[15 + 2 * bits :]
    cols = g_ref.shape[3]
    chunks = cols // STEP
    half = STEP // 2
    block = tok_ref.shape[1]
    hw = heads * DK
    width = strips.shape[1]
    strip, dstrip = strips.at[pl.ds(0, block)], strips.at[pl.ds(block, block)]
    gat = strips.at[pl.ds(0, 3 * hw), pl.ds(0, tok_ref.shape[2])]
    for c in range(chunks):
        at = pl.ds(c * STEP, STEP)
        pltpu.make_async_copy(g_ref.at[:, :, :, at], gv.at[:, :, :, at], lsem.at[c]).start()
    me_t, me_d = enter(nt, nd, True)
    sends, recvs, after = Sems(ssem), Sems(rsem), []
    orders = [[0] + o[:-1][::-1] for o in bit_orders(bits)]
    jobs = []

    own = pltpu.make_async_copy(dmine_ref.at[me_t], da_ref.at[me_t], lsem.at[chunks])
    own.start()
    swaps = []
    for k in range(1, nt):
        peer = lax.rem(me_t + k, nt)
        copy = pltpu.make_async_remote_copy(
            dmine_ref.at[peer], da_ref.at[me_t], sends.take(), recvs.take(), device_id={"tensor": peer}, device_id_type=MESH
        )
        copy.start()
        swaps.append(copy)

    def swapped():
        own.wait()
        for copy in swaps:
            copy.wait_recv()

    after.extend(copy.wait_send for copy in swaps)

    line, hot = bias_lines(bl_ref, tab_ref)

    def rows_of(i):
        return slice(i * block, (i + 1) * block)

    def head_start(h):
        build_strip(strip, line[h : h + 1, :])
        dstrip[...] = jnp.zeros_like(dstrip)
        dkt[...] = jnp.zeros_like(dkt)
        dvt[...] = jnp.zeros_like(dvt)
        for i in range(nt):
            ks[rows_of(i), :] = qkv_ref[i, :, hw + h * DK : hw + (h + 1) * DK]
            vs[rows_of(i), :] = qkv_ref[i, :, 2 * hw + h * DK : 2 * hw + (h + 1) * DK]

    def piece(h, i):
        mine = rows_of(i)
        seen = (i + 1) * block
        off = (nt - 1 - i) * block
        part = slice(h * DK, (h + 1) * DK)
        q = qkv_ref[i, :, part]
        da = da_ref[i, :, part]
        delta = jnp.sum(da.astype(F32) * attn_ref[i, :, part].astype(F32), axis=1, keepdims=True)
        s = dot_nt(q, ks[:seen, :])
        s = s + strip[:, off : off + seen]
        s = jnp.where(column(segr_ref[:, mine]) == segr_ref[:, :seen], s, MASKED)
        p = jnp.exp(s - lse_ref[mine, h : h + 1])
        dp = dot_nt(da, vs[:seen, :])
        ds = p * (dp - delta)
        low = ds.astype(BF)
        dqkv[mine, part] = dot(low, ks[:seen, :]).astype(BF)
        dkt[:, :seen] += dot_tn(q, low)
        dvt[:, :seen] += dot_tn(da, p.astype(BF))
        dstrip[:, off : off + seen] += ds

    def head_end(h):
        for i in range(nt):
            dqkv[rows_of(i), hw + h * DK : hw + (h + 1) * DK] = dkt[:, rows_of(i)].T.astype(BF)
            dqkv[rows_of(i), 2 * hw + h * DK : 2 * hw + (h + 1) * DK] = dvt[:, rows_of(i)].T.astype(BF)
        n = block // 2
        while n >= 8:
            dstrip[0:n, :] = dstrip[0:n, :] + pltpu.roll(dstrip[n : 2 * n, :], width - n, 1)
            n //= 2
        x = dstrip[0:8, :]
        row = lax.broadcasted_iota(jnp.int32, x.shape, 0)
        for b in range(3):
            x = jnp.where((row >> b) % 2 == 1, pltpu.roll(x, width - (1 << b), 1), x)
        lines[h : h + 1, :] = jnp.sum(x, axis=0, keepdims=True)

    def rows_end(i):
        mine = rows_of(i)
        x = tok_ref[i].astype(F32)
        hat = x * norm_scale(x)
        more = dot_tn(dqkv[mine, :], (hat * g0_ref[...]).astype(BF))
        gat[...] = more if i == 0 else gat[...] + more
        u = dot_nt(dqkv[mine, :], wa_ref[:, : 3 * hw])
        gain0[...] += jnp.sum(u * hat, axis=0, keepdims=True)
        u_ref[i] = u.astype(BF)

    def finish():
        table = lax.dot_general(
            lines[...],
            hot.astype(F32),
            (((1,), (1,)), ((), ())),
            precision=lax.Precision.HIGHEST,
            preferred_element_type=F32,
        )
        table = jnp.concatenate([table, jnp.zeros((8, 128 - table.shape[1]), F32)], axis=1).astype(BF)
        ga = gat[...].T.astype(BF)
        part = ga.shape[0] // nd
        for d in range(nd):
            a_ref[d, :, : 3 * hw] = ga[d * part : (d + 1) * part]
            a_ref[d, :, 3 * hw :] = jnp.zeros((part, 128), BF)
            a_ref[d, :8, 3 * hw :] = table

    def add_gains():
        at = g_used - (cols - 128)
        row = lax.broadcasted_iota(jnp.int32, (128, gain0.shape[1]), 0)
        gains = jnp.where(row == at, gain0[...], 0.0)
        gains = gains + jnp.where(row == at + 1, gain_in[0:1, :], 0.0) + jnp.where(row == at + 2, gain_in[1:2, :], 0.0)
        gains = gains.T.astype(BF)
        part = gains.shape[0] // nd

        def step(t, carry):
            for d in range(nd):
                gv[t, d, :, cols - 128 :] = gv[t, d, :, cols - 128 :] + gains[d * part : (d + 1) * part]
            return carry

        lax.fori_loop(0, nt, step, 0)

    lines[...] = jnp.zeros_like(lines)
    gain0[...] = jnp.zeros_like(gain0)

    def a_done():
        a_out[...] = a_ref[me_d].astype(F32)

    def chunk_job(c):
        first = c * STEP
        cubes = []
        for n in range(2):
            at = first + n * half
            cubes.append(
                cube_scatter(
                    nd,
                    me_d,
                    orders[n],
                    lambda d, at=at: gv.at[:, d, :, pl.ds(at, half)],
                    [r.at[2 * c + n] for r in grecv],
                    sends,
                    recvs,
                    after,
                )
            )
        z = line_scatter(
            nt,
            me_t,
            lambda b: gv.at[b, me_d, :, pl.ds(first, STEP)],
            gz.at[c],
            g_out.at[:, pl.ds(first, STEP)],
            sends,
            recvs,
            after,
        )

        def begin():
            at = pl.ds(first, STEP)
            pltpu.make_async_copy(g_ref.at[:, :, :, at], gv.at[:, :, :, at], lsem.at[c]).wait()
            if c == chunks - 1:
                add_gains()
            for q in cubes:
                q[0]()

        def both(k):
            def run():
                for q in cubes:
                    q[k]()

            return run

        def meet():
            for q in cubes:
                q[bits]()
            z[0]()

        return [begin] + [both(k) for k in range(1, bits)] + [meet] + z[1:]

    def row_job(ref, recv, out, n):
        at = pl.ds(n * PIECE, PIECE)
        return line_scatter(nt, me_t, lambda b: ref.at[b, at], recv.at[:, at], out.at[at], sends, recvs, after)

    ticks = [SPACE * k for k in range(bits)] + [SPACE * bits + k for k in range(nt)]
    for c in range(chunks):
        jobs.append((min(c, chunks - 1), chunk_job(c), ticks))
    for n in range(e_out.shape[0] // PIECE):
        jobs.append((n, row_job(e_ref, ez, e_out, n), list(range(nt))))
    compute = [(CORE0 - 1, partial(head_start, 0)), (CORE0, swapped)]
    for h in range(heads):
        if h > 0:
            compute.append((CORE0 + h, partial(head_start, h)))
        compute += [(CORE0 + h, partial(piece, h, i)) for i in range(nt)]
        compute.append((CORE0 + h, partial(head_end, h)))
    ready = CORE0 + heads
    compute += [(ready, partial(rows_end, i)) for i in range(nt)]
    compute.append((ready, finish))
    for tick, fn in compute:
        jobs.append((tick, [fn], [0]))
    a_job = cube_scatter(nd, me_d, orders[0], lambda d: a_ref.at[d], arecv, sends, recvs, after) + [a_done]
    jobs.append((ready + 1, a_job, [SPACE * k for k in range(bits + 1)] + [SPACE * bits]))
    for n in range(u_out.shape[0] // PIECE):
        jobs.append((ready + 1 + n, row_job(u_ref, uz, u_out, n), list(range(nt))))
    run_jobs(jobs, after)


def backward_all(nt, nd, heads, used, g, e, gain12, dmine, tok, wa, g0, segr, bl, tab, qkv, attn, lse):
    bits = nd.bit_length() - 1
    rows, cols = g.shape[2:]
    block, width = tok.shape[1:]
    length = nt * block
    wide = wa.shape[1]
    hw = heads * DK
    chunks = cols // STEP
    lines = chunks + (block + e.shape[1]) // PIECE
    total = lines * 2 * nt + (2 * chunks + 1) * bits + nt - 1
    return pl.pallas_call(
        partial(backward_kernel, nt, nd, heads, used),
        out_shape=(
            jax.ShapeDtypeStruct((rows, cols), F32),
            jax.ShapeDtypeStruct((rows, wide), F32),
            jax.ShapeDtypeStruct((block, width), F32),
            jax.ShapeDtypeStruct(e.shape[1:], F32),
        ),
        in_specs=[ANY] + [VMEM] * 12,
        out_specs=(VMEM,) * 4,
        scratch_shapes=[
            pltpu.VMEM((nt, nd, rows, cols), BF),
            pltpu.VMEM((nt + 1, block, width), BF),
            pltpu.VMEM((nt + 1,) + e.shape[1:], BF),
            pltpu.VMEM((chunks, nt + 1, rows, STEP), BF),
        ]
        + [pltpu.VMEM((1 << (bits - 1 - k), rows, wide), BF) for k in range(bits)]
        + [pltpu.VMEM((2 * chunks, 1 << (bits - 1 - k), nt, rows, STEP // 2), BF) for k in range(bits)]
        + [
            pltpu.VMEM((nd, rows, wide), BF),
            pltpu.VMEM((nt, block, width), BF),
            pltpu.VMEM((nt, block, hw), BF),
            pltpu.VMEM((max(2 * block, 3 * hw), length + block), F32),
            pltpu.VMEM((length, DK), BF),
            pltpu.VMEM((length, DK), BF),
            pltpu.VMEM((DK, length), F32),
            pltpu.VMEM((DK, length), F32),
            pltpu.VMEM((length, 3 * hw), BF),
            pltpu.VMEM((8, length + block), F32),
            pltpu.VMEM((1, width), F32),
            pltpu.SemaphoreType.DMA((total,)),
            pltpu.SemaphoreType.DMA((total,)),
            pltpu.SemaphoreType.DMA((chunks + 1,)),
        ],
        compiler_params=pltpu.CompilerParams(collective_id=1, has_side_effects=True, vmem_limit_bytes=LIMIT),
        name="backward_all",
    )(g, e, gain12, dmine, tok, wa, g0, segr, bl, tab, qkv, attn, lse)


def column(row):
    return jnp.broadcast_to(row, (8, row.shape[1])).T[:, 0:1]


def build_strip(strip, x):
    block, width = strip.shape
    row = lax.broadcasted_iota(jnp.int32, (8, width), 0)
    x = jnp.broadcast_to(x, (8, width))
    for b in range(3):
        x = jnp.where((row >> b) % 2 == 1, pltpu.roll(x, 1 << b, 1), x)
    strip[0:8, :] = x
    n = 8
    while n < block:
        strip[n : 2 * n, :] = pltpu.roll(strip[0:n, :], n, 1)
        n *= 2


def bias_lines(bl_ref, tab_ref):
    width = bl_ref.shape[1]
    buckets = tab_ref.shape[1]
    hot = bl_ref[...] == lax.broadcasted_iota(jnp.int32, (buckets, width), 0)
    line = dot(tab_ref[...], hot.astype(F32).astype(BF))
    return jnp.where(bl_ref[...] >= 0, line, MASKED), hot


def self_forward_kernel(
    heads, tok_ref, wa_ref, g_ref, segr_ref, bl_ref, tab_ref, qkv_ref, attn_ref, lse_ref, strip, qs, ks, vs, os, lses
):
    nt, block = tok_ref.shape[:2]
    hw = heads * DK
    line, _ = bias_lines(bl_ref, tab_ref)
    for h in range(heads):
        build_strip(strip.at[h], line[h : h + 1, :])
    for i in range(nt):
        x = tok_ref[i].astype(F32)
        n = (x * norm_scale(x) * g_ref[...]).astype(BF)
        y = dot(n, wa_ref[:, : 3 * hw]).astype(BF)
        qkv_ref[i] = y
        for h in range(heads):
            for which, ref in enumerate((qs, ks, vs)):
                at = which * hw + h * DK
                ref[h, i * block : (i + 1) * block, :] = y[:, at : at + DK]

    def head(h, carry):
        for i in range(nt):
            mine = slice(i * block, (i + 1) * block)
            seen = (i + 1) * block
            s = dot_nt(qs[h, mine, :], ks[h, :seen, :])
            s = s + strip[h, :, (nt - 1 - i) * block : (nt - 1 - i) * block + seen]
            s = jnp.where(column(segr_ref[:, mine]) == segr_ref[:, :seen], s, MASKED)
            top = jnp.max(s, axis=-1, keepdims=True)
            p = jnp.exp(s - top)
            total = jnp.sum(p, axis=-1, keepdims=True)
            o = dot(p.astype(BF), vs[h, :seen, :]) / total
            os[h, mine, :] = o
            lses[h, mine, :] = top + jnp.log(total)
        return carry

    lax.fori_loop(0, heads, head, 0)
    for i in range(nt):
        mine = slice(i * block, (i + 1) * block)
        attn_ref[i] = jnp.concatenate([os[h, mine, :] for h in range(heads)], axis=1).astype(BF)
        for h in range(heads):
            lse_ref[mine, h : h + 1] = lses[h, mine, :]


def self_forward(heads, tok, wa, g, segr, bl, tab):
    nt, block, width = tok.shape
    length = nt * block
    hw = heads * DK
    return pl.pallas_call(
        partial(self_forward_kernel, heads),
        out_shape=(
            jax.ShapeDtypeStruct((nt, block, 3 * hw), BF),
            jax.ShapeDtypeStruct((nt, block, hw), BF),
            jax.ShapeDtypeStruct((length, 8), F32),
        ),
        in_specs=[VMEM] * 6,
        out_specs=(VMEM,) * 3,
        scratch_shapes=[pltpu.VMEM((heads, block, length + block), F32)]
        + [pltpu.VMEM((heads, length, DK), BF)] * 3
        + [pltpu.VMEM((heads, length, DK), F32), pltpu.VMEM((heads, length, 1), F32)],
        compiler_params=pltpu.CompilerParams(vmem_limit_bytes=LIMIT),
        name="self_forward",
    )(tok, wa, g, segr, bl, tab)


def middle_kernel(
    heads,
    ff,
    tok_ref,
    enc_ref,
    attn_ref,
    og_ref,
    gains_ref,
    w_hbm,
    layer_ref,
    one_ref,
    denc_ref,
    gain_ref,
    dattn_ref,
    g_hbm,
    w,
    g,
    h1_ref,
    h2_ref,
    n1_ref,
    n2_ref,
    acc_ref,
    dn_ref,
    g2_ref,
    denc,
    qc,
    kv,
    ac,
    oc,
    lse,
    dkv,
    insem,
    outsem,
):
    nt = w.shape[0]
    hw = heads * DK
    cols = w.shape[2]
    f0, f1, f2 = 0, ff, 2 * ff
    kv0 = 3 * ff
    q0 = kv0 + 2 * hw
    c0 = q0 + hw
    s0 = c0 + hw
    end = s0 + hw
    ffn = pl.ds(0, 3 * ff)
    att = pl.ds(3 * ff, cols - 3 * ff)
    loads = [pltpu.make_async_copy(w_hbm.at[t, :, att], w.at[t, :, att], insem.at[0, t]) for t in range(nt)]
    loads += [pltpu.make_async_copy(w_hbm.at[t, :, ffn], w.at[t, :, ffn], insem.at[1, t]) for t in range(nt)]
    for copy in loads:
        copy.start()

    def load_wait(which, t):
        at = att if which == 0 else ffn
        pltpu.make_async_copy(w_hbm.at[t, :, at], w.at[t, :, at], insem.at[which, t]).wait()

    def store(which, t):
        at = att if which == 0 else ffn
        return pltpu.make_async_copy(g.at[t, :, at], g_hbm.at[t, :, at], outsem.at[which, t])

    acc_ref[...] = tok_ref[...].astype(F32)

    def self_out(t, carry):
        load_wait(0, t)
        acc_ref[...] += dot_nt(attn_ref[t], w[t, :, s0:end])
        return carry

    lax.fori_loop(0, nt, self_out, 0)
    h1 = acc_ref[...]
    h1_ref[...] = h1
    n1_ref[...] = (h1 * norm_scale(h1) * gains_ref[1:2, :]).astype(BF)

    def cross(t, carry):
        q = dot(n1_ref[...], w[t, :, q0:c0]).astype(BF)
        both = dot(enc_ref[...], w[t, :, kv0:q0]).astype(BF)
        qc[t] = q
        kv[t] = both
        outs = []
        for h in range(heads):
            part = slice(h * DK, (h + 1) * DK)
            s = dot_nt(q[:, part], both[:, part])
            top = jnp.max(s, axis=-1, keepdims=True)
            p = jnp.exp(s - top)
            total = jnp.sum(p, axis=-1, keepdims=True)
            lse[t, h] = top + jnp.log(total)
            outs.append(dot(p.astype(BF), both[:, hw + h * DK : hw + (h + 1) * DK]) / total)
        a = jnp.concatenate(outs, axis=1).astype(BF)
        ac[t] = a
        acc_ref[...] += dot_nt(a, w[t, :, c0:s0])
        return carry

    lax.fori_loop(0, nt, cross, 0)
    h2 = acc_ref[...]
    h2_ref[...] = h2
    n2_ref[...] = (h2 * norm_scale(h2) * gains_ref[2:3, :]).astype(BF)
    dn_ref[...] = jnp.zeros_like(dn_ref)

    def units(t, carry):
        load_wait(1, t)
        n2 = n2_ref[...]
        og = og_ref[...]
        gate = dot(n2, w[t, :, f0:f1])
        up = dot(n2, w[t, :, f1:f2])
        dinner = dot(og, w[t, :, f2 : 3 * ff])
        sq = gate * gate
        th = jnp.tanh(0.7978845608028654 * (gate + 0.044715 * (gate * sq)))
        cdf = 0.5 * (1.0 + th)
        act = gate * cdf
        slope = cdf + gate * (0.5 * (1.0 - th * th)) * (0.7978845608028654 * (1.0 + 0.134145 * sq))
        inner = (act * up).astype(BF)
        dgate = (dinner * up * slope).astype(BF)
        dup = (dinner * act).astype(BF)
        acc_ref[...] += dot_nt(inner, w[t, :, f2 : 3 * ff])
        dn_ref[...] += dot_nt(dgate, w[t, :, f0:f1]) + dot_nt(dup, w[t, :, f1:f2])
        g[t, :, f0:f1] = dot_tn(n2, dgate).astype(BF)
        g[t, :, f1:f2] = dot_tn(n2, dup).astype(BF)
        g[t, :, f2 : 3 * ff] = dot_tn(og, inner).astype(BF)
        store(1, t).start()
        return carry

    lax.fori_loop(0, nt, units, 0)
    layer_ref[...] = acc_ref[...].astype(BF)
    h2 = h2_ref[...]
    back, gain2 = norm_back(h2, norm_scale(h2), gains_ref[2:3, :], dn_ref[...])
    g2 = og_ref[...].astype(F32) + back
    acc_ref[...] = g2
    g2_ref[...] = g2.astype(BF)
    dn_ref[...] = jnp.zeros_like(dn_ref)
    denc[...] = jnp.zeros_like(denc)

    def cross_back(t, carry):
        g2 = g2_ref[...]
        a = ac[t]
        da = dot(g2, w[t, :, c0:s0]).astype(BF)
        g[t, :, c0:s0] = dot_tn(g2, a).astype(BF)
        prod = da.astype(F32) * a.astype(F32)
        q = qc[t]
        both = kv[t]
        dqs = []
        for h in range(heads):
            part = slice(h * DK, (h + 1) * DK)
            qh, kh = q[:, part], both[:, part]
            vh, dah = both[:, hw + h * DK : hw + (h + 1) * DK], da[:, part]
            p = jnp.exp(dot_nt(qh, kh) - lse[t, h])
            delta = jnp.sum(prod[:, part], axis=1, keepdims=True)
            ds = (p * (dot_nt(dah, vh) - delta)).astype(BF)
            dqs.append(dot(ds, kh))
            dkv[h * DK : (h + 1) * DK, :] = dot_tn(qh, ds)
            dkv[hw + h * DK : hw + (h + 1) * DK, :] = dot_tn(dah, p.astype(BF))
        dq = jnp.concatenate(dqs, axis=1).astype(BF)
        dboth = dkv[...].astype(BF)
        g[t, :, q0:c0] = dot_tn(n1_ref[...], dq).astype(BF)
        g[t, :, kv0:q0] = lax.dot_general(
            enc_ref[...], dboth, (((0,), (1,)), ((), ())), preferred_element_type=F32
        ).astype(BF)
        dn_ref[...] += dot_nt(dq, w[t, :, q0:c0])
        denc[...] += lax.dot_general(
            dboth, w[t, :, kv0:q0], (((0,), (1,)), ((), ())), preferred_element_type=F32
        )
        return carry

    lax.fori_loop(0, nt, cross_back, 0)
    denc_ref[...] = denc[...].astype(BF)
    h1 = h1_ref[...]
    back, gain1 = norm_back(h1, norm_scale(h1), gains_ref[1:2, :], dn_ref[...])
    g1 = acc_ref[...] + back
    one_ref[...] = g1
    g2_ref[...] = g1.astype(BF)
    gain_ref[...] = jnp.concatenate([gain1, gain2, jnp.zeros((6, gain1.shape[1]), F32)], axis=0)

    def self_out_back(t, carry):
        low = g2_ref[...]
        dattn_ref[t] = dot(low, w[t, :, s0:end]).astype(BF)
        tail = dot_tn(low, attn_ref[t])
        g[t, :, s0:cols] = jnp.concatenate([tail, jnp.zeros((tail.shape[0], cols - end), F32)], axis=1).astype(BF)
        store(0, t).start()
        return carry

    lax.fori_loop(0, nt, self_out_back, 0)
    for t in range(nt):
        store(1, t).wait()
        store(0, t).wait()


def middle(heads, ff, tok, enc, attn, og, gains, w):
    nt, _, cols = w.shape
    rows, width = tok.shape
    states = enc.shape[0]
    hw = heads * DK
    return pl.pallas_call(
        partial(middle_kernel, heads, ff),
        out_shape=(
            jax.ShapeDtypeStruct((rows, width), BF),
            jax.ShapeDtypeStruct((rows, width), F32),
            jax.ShapeDtypeStruct((states, width), BF),
            jax.ShapeDtypeStruct((8, width), F32),
            jax.ShapeDtypeStruct((nt, rows, hw), BF),
            jax.ShapeDtypeStruct(w.shape, BF),
        ),
        in_specs=[VMEM] * 5 + [ANY],
        out_specs=(VMEM,) * 5 + (ANY,),
        scratch_shapes=[
            pltpu.VMEM(w.shape, BF),
            pltpu.VMEM(w.shape, BF),
            pltpu.VMEM((rows, width), F32),
            pltpu.VMEM((rows, width), F32),
            pltpu.VMEM((rows, width), BF),
            pltpu.VMEM((rows, width), BF),
            pltpu.VMEM((rows, width), F32),
            pltpu.VMEM((rows, width), F32),
            pltpu.VMEM((rows, width), BF),
            pltpu.VMEM((states, width), F32),
            pltpu.VMEM((nt, rows, hw), BF),
            pltpu.VMEM((nt, states, 2 * hw), BF),
            pltpu.VMEM((nt, rows, hw), BF),
            pltpu.VMEM((8, 128), F32),
            pltpu.VMEM((nt, heads, rows, 1), F32),
            pltpu.VMEM((2 * hw, states), F32),
            pltpu.SemaphoreType.DMA((2, nt)),
            pltpu.SemaphoreType.DMA((2, nt)),
        ],
        compiler_params=pltpu.CompilerParams(vmem_limit_bytes=LIMIT),
        name="middle",
    )(tok, enc, attn, og, gains, w)


def per_device(
    tokens,
    encoder,
    segments,
    rel_bucket,
    out_grad,
    self_q,
    self_k,
    self_v,
    self_o,
    cross_q,
    cross_k,
    cross_v,
    cross_o,
    ffn_gate,
    ffn_up,
    ffn_down,
    bias_table,
    norm_gains,
):
    nt, nd = lax.axis_size("tensor"), lax.axis_size("dp")
    part, hw = self_q.shape
    ff = ffn_gate.shape[1]
    heads = hw // DK
    rows, width = tokens.shape
    length = rows * nt
    buckets = bias_table.shape[0]
    wa = jnp.concatenate([self_q, self_k, self_v, jnp.pad(norm_gains.T, ((0, 0), (0, 128 - norm_gains.shape[0])))], axis=1)
    wb = jnp.concatenate([ffn_gate, ffn_up, ffn_down.T, cross_k, cross_v, cross_q, cross_o.T, self_o.T], axis=1)
    used = wb.shape[1]
    cols = -(-(used + 3) // STEP) * STEP
    wb = jnp.pad(wb, ((0, 0), (0, cols - used)))
    tok_all, enc_all, wa_all, wb_all = gather_all(nt, nd, tokens, encoder, wa, wb)
    wa_full = wa_all.reshape(nd * part, wa.shape[1])
    wb_full = wb_all.reshape(nt, nd * part, cols)
    gains = jnp.pad(wa_full[:, 3 * hw : 3 * hw + 3].T.astype(F32), ((0, 5), (0, 0)))
    top = (nt - 1) * rows
    blank = jnp.full((length - 1 - top,), -1, jnp.int32)
    bl = jnp.concatenate(
        [rel_bucket[: top + 1][::-1], blank, jnp.full((1,), -1, jnp.int32), rel_bucket[top + 1 : length][::-1]]
    )[None, :]
    tab = jnp.pad(bias_table.T, ((0, 8 - heads), (0, 0)))
    segr = segments
    g0 = gains[0:1]
    qkv, attn, lse = self_forward(heads, tok_all, wa_full, g0, segr, bl, tab)
    mine = exchange(nt, attn, 2)
    layer_out, grad_one, denc, gain12, dmine, gb = middle(
        heads, ff, tokens, enc_all.reshape(nt * encoder.shape[0], width), mine, out_grad, gains, wb_full
    )
    gsum, asum, usum, esum = backward_all(
        nt,
        nd,
        heads,
        used,
        gb.reshape(nt, nd, part, cols),
        denc.reshape((nt,) + encoder.shape),
        gain12,
        dmine,
        tok_all,
        wa_full,
        g0,
        segr,
        bl,
        tab,
        qkv,
        attn,
        lse,
    )
    x = tokens.astype(F32)
    back, _ = norm_back(x, norm_scale(x), g0, usum)
    tokens_grad = grad_one + back
    at = 3 * ff
    ck, cv, cq, co, so = (gsum[:, at + n * hw : at + (n + 1) * hw] for n in range(5))
    return (
        layer_out,
        tokens_grad,
        esum,
        asum[:, :hw],
        asum[:, hw : 2 * hw],
        asum[:, 2 * hw : 3 * hw],
        so.T,
        cq,
        ck,
        cv,
        co.T,
        gsum[:, :ff],
        gsum[:, ff : 2 * ff],
        gsum[:, 2 * ff : 3 * ff].T,
        asum[:heads, 3 * hw : 3 * hw + buckets].T,
        gsum[:, used : used + 3].T,
    )


def solution(mesh):
    rows = P(("dp", "tensor"), None)
    left = P("dp", "tensor")
    right = P("tensor", "dp")
    return jax.shard_map(
        per_device,
        mesh=mesh,
        in_specs=(rows, rows, P("dp", None), P(), rows, left, left, left, right, left, left, left, right, left, left, right)
        + (P(None, "tensor"), P(None, "dp")),
        out_specs=(rows, rows, rows, left, left, left, right, left, left, left, right, left, left, right)
        + (P(None, "tensor"), P(None, "dp")),
        check_vma=False,
    )
```

```python
from functools import partial

import jax
import jax.numpy as jnp
from jax import lax
from jax.experimental import pallas as pl
from jax.experimental.pallas import tpu as pltpu
from jax.sharding import PartitionSpec as P

DK = 64
EPS = 1e-06
MASKED = -1e30
BF = jnp.bfloat16
F32 = jnp.float32
MESH = pl.DeviceIdType.MESH
VMEM = pl.BlockSpec(memory_space=pltpu.VMEM)
ANY = pl.BlockSpec(memory_space=pl.ANY)
LIMIT = 63 * 1024 * 1024
STEP = 256
SPACE = 2
PIECE = 32
TOK0 = 2
TOKR = 1
CORE0 = 3
CORE1 = 13


def dot(a, b):
    return jnp.dot(a, b, preferred_element_type=F32)


def dot_nt(a, b):
    return lax.dot_general(a, b, (((1,), (1,)), ((), ())), preferred_element_type=F32)


def dot_tn(a, b):
    return lax.dot_general(a, b, (((0,), (0,)), ((), ())), preferred_element_type=F32)


def norm_scale(x):
    return lax.rsqrt(jnp.mean(x * x, axis=-1, keepdims=True) + EPS)


def norm_back(x, r, g, u):
    w = u * g
    inner = jnp.mean(w * x, axis=-1, keepdims=True)
    return r * w - x * (r * r * r * inner), jnp.sum(u * (x * r), axis=0, keepdims=True)


def flip(index, bit):
    size = 1 << bit
    return index + size - 2 * size * lax.rem(index // size, 2)


def flip_all(index, mask):
    bit = 0
    while mask:
        if mask & 1:
            index = flip(index, bit)
        mask >>= 1
        bit += 1
    return index


def subsets(bits):
    out = [0]
    for b in bits:
        out = out + [m | (1 << b) for m in out]
    return out


def bit_orders(count):
    upper = list(range(1, count))
    return [upper + [0], upper[::-1] + [0]]


class Sems:
    def __init__(self, ref):
        self.ref = ref
        self.used = 0

    def take(self):
        self.used += 1
        return self.ref.at[self.used - 1]

    def many(self, count):
        base = self.used
        self.used += count
        return lambda n: self.ref.at[base + n]


def wait_bytes(ref, sem):
    pltpu.make_async_copy(ref, ref, sem).wait()


def row_loop(shape, body):
    size = 32 if shape[1] <= 256 else 16
    if shape[0] % size:
        body(slice(0, shape[0]))
        return

    def step(n, carry):
        body(pl.ds(pl.multiple_of(n * size, size), size))
        return carry

    lax.fori_loop(0, shape[0] // size, step, 0)


def add_into(ref, got):
    if len(ref.shape) == 2:

        def body(at):
            ref[at, :] = ref[at, :] + got[at, :]

        row_loop(ref.shape, body)
    else:

        def step(t, carry):
            ref[t] = ref[t] + got[t]
            return carry

        lax.fori_loop(0, ref.shape[0], step, 0)


def enter(nt, nd, all_tensor=False):
    me_t, me_d = lax.axis_index("tensor"), lax.axis_index("dp")
    bar = pltpu.get_barrier_semaphore()
    bits = nd.bit_length() - 1
    for b in range(bits):
        pl.semaphore_signal(bar, 1, device_id={"dp": flip(me_d, b)}, device_id_type=MESH)
    if all_tensor:
        for k in range(1, nt):
            pl.semaphore_signal(bar, 1, device_id={"tensor": lax.rem(me_t + k, nt)}, device_id_type=MESH)
        pl.semaphore_wait(bar, bits + nt - 1)
        return me_t, me_d

    @pl.when(me_t > 0)
    def _():
        pl.semaphore_signal(bar, 1, device_id={"tensor": me_t - 1}, device_id_type=MESH)

    @pl.when(me_t < nt - 1)
    def _():
        pl.semaphore_signal(bar, 1, device_id={"tensor": me_t + 1}, device_id_type=MESH)

    pl.semaphore_wait(bar, bits + (me_t + nt - 1) // nt + (2 * nt - 2 - me_t) // nt)
    return me_t, me_d


def run_jobs(jobs, after):
    events = []
    for number, (start, stages, ticks) in enumerate(jobs):
        for tick, stage in zip(ticks, stages, strict=True):
            events.append((start + tick, start, number, stage))
    for event in sorted(events, key=lambda e: e[:3]):
        event[3]()
    for fn in after:
        fn()


def line_gather(nt, me, own, slot, sends, recvs, after):
    sem = {(s, j): (sends.take(), recvs.take()) for s in (1, -1) for j in range(1, nt)}

    def send(side, j):
        block = me - side * (j - 1)
        target = me + side
        ok = (block >= 0) & (block < nt) & (target >= 0) & (target < nt)
        src = own if j == 1 else slot(jnp.clip(block, 0, nt - 1))
        dst = slot(jnp.clip(block, 0, nt - 1))
        ss, rs = sem[side, j]

        @pl.when(ok)
        def _():
            pltpu.make_async_remote_copy(
                src, dst, ss, rs, device_id={"tensor": target}, device_id_type=MESH
            ).start()

        def done():
            @pl.when(ok)
            def _():
                wait_bytes(own, ss)

        after.append(done)

    def arrive(side, j):
        block = me - side * j

        @pl.when((block >= 0) & (block < nt))
        def _():
            wait_bytes(own, sem[side, j][1])

    def stage(j):
        def run():
            for side in (1, -1):
                if j > 0:
                    arrive(side, j)
                if j < nt - 1:
                    send(side, j + 1)

        return run

    return [stage(j) for j in range(nt)]


def cube_gather(nd, me, order, own, slot, slots, sends, recvs, after):
    count = len(order)
    sem = [(sends.take(), recvs.take()) for _ in range(count)]

    def start(k):
        bit = order[k]
        for m in subsets(order[:k]):
            block = flip_all(me, m)
            src = own if (m == 0 and own is not None) else slot(block)
            pltpu.make_async_remote_copy(
                src, slot(block), sem[k][0], sem[k][1], device_id={"dp": flip(me, bit)}, device_id_type=MESH
            ).start()

        def done():
            wait_bytes(slots(1 << k), sem[k][0])

        after.append(done)

    def stage(k):
        def run():
            if k > 0:
                wait_bytes(slots(1 << (k - 1)), sem[k - 1][1])
            if k < count:
                start(k)

        return run

    return [stage(k) for k in range(count + 1)]


def forward_kernel(
    nt,
    nd,
    heads,
    tok_ref,
    enc_ref,
    wa_ref,
    wb_ref,
    segr_ref,
    bl_ref,
    tab_ref,
    tok_out,
    enc_out,
    wb_out,
    wa_full,
    gain_ref,
    qkv_ref,
    lse_ref,
    attn_ref,
    mine_ref,
    wa_out,
    strip,
    ks,
    vs,
    ssem,
    rsem,
    lsem,
):
    me_t, me_d = enter(nt, nd, True)
    bits = nd.bit_length() - 1
    sends, recvs, after = Sems(ssem), Sems(rsem), []
    locals_ = [
        (tok_ref, tok_out.at[me_t]),
        (enc_ref, enc_out.at[me_t]),
        (wa_ref, wa_out.at[me_d]),
        (wb_ref, wb_out.at[me_t, me_d]),
    ]
    for n, (src, dst) in enumerate(locals_):
        pltpu.make_async_copy(src, dst, lsem.at[n]).start()
    orders = bit_orders(bits)
    cols = wb_ref.shape[1]
    chunks = cols // STEP
    half = STEP // 2
    jobs = []
    jobs.append(
        (
            0,
            cube_gather(nd, me_d, orders[0], wa_ref, lambda d: wa_out.at[d], lambda n: wa_out.at[pl.ds(0, n)], sends, recvs, after),
            [SPACE * k for k in range(bits + 1)],
        )
    )

    def chunk_job(c):
        first = c * STEP
        z = line_gather(
            nt,
            me_t,
            wb_ref.at[:, pl.ds(first, STEP)],
            lambda t: wb_out.at[t, me_d, :, pl.ds(first, STEP)],
            sends,
            recvs,
            after,
        )
        cubes = []
        for n in range(2):
            at = first + n * half
            cubes.append(
                cube_gather(
                    nd,
                    me_d,
                    orders[n],
                    None,
                    lambda d, at=at: wb_out.at[:, d, :, pl.ds(at, half)],
                    lambda k, at=at: wb_out.at[:, pl.ds(0, k), :, pl.ds(at, half)],
                    sends,
                    recvs,
                    after,
                )
            )

        def meet():
            z[-1]()
            for q in cubes:
                q[0]()

        def both(k):
            def run():
                for q in cubes:
                    q[k]()

            return run

        return z[:-1] + [meet] + [both(k) for k in range(1, bits + 1)]


    def row_job(ref, out, n):
        at = pl.ds(n * PIECE, PIECE)
        return line_gather(nt, me_t, ref.at[at], lambda t: out.at[t, at], sends, recvs, after)

    ticks = list(range(nt)) + [nt - 1 + SPACE * k for k in range(1, bits + 1)]
    for c in range(chunks):
        jobs.append((c, chunk_job(c), ticks))
    number = TOK0
    for ref, out in ((tok_ref, tok_out), (enc_ref, enc_out)):
        for n in range(ref.shape[0] // PIECE):
            jobs.append((number // TOKR, row_job(ref, out, n), list(range(nt))))
            number += 1
    pltpu.make_async_copy(wb_ref, wb_out.at[me_t, me_d], lsem.at[3]).wait()
    after.append(lambda: pltpu.make_async_copy(enc_ref, enc_out.at[me_t], lsem.at[1]).wait())

    block = tok_ref.shape[0]
    part = wa_ref.shape[0]
    hw = heads * DK
    line, _ = bias_lines(bl_ref, tab_ref)

    def rows_of(i):
        return slice(i * block, (i + 1) * block)

    def weights():
        for n in (0, 2):
            src, dst = locals_[n]
            pltpu.make_async_copy(src, dst, lsem.at[n]).wait()
        for d in range(nd):
            wa_full[d * part : (d + 1) * part, :] = wa_out[d]
        gain_ref[...] = wa_full[:, 3 * hw :].astype(F32).T[0:8]

    def rows_start(i):
        x = tok_out[i].astype(F32)
        n = (x * norm_scale(x) * gain_ref[0:1, :]).astype(BF)
        qkv_ref[i] = dot(n, wa_full[:, : 3 * hw]).astype(BF)

    def head_start(h):
        build_strip(strip, line[h : h + 1, :])
        for i in range(nt):
            ks[rows_of(i), :] = qkv_ref[i, :, hw + h * DK : hw + (h + 1) * DK]
            vs[rows_of(i), :] = qkv_ref[i, :, 2 * hw + h * DK : 2 * hw + (h + 1) * DK]

    def piece(h, i):
        mine = rows_of(i)
        seen = (i + 1) * block
        off = (nt - 1 - i) * block
        cols_h = slice(h * DK, (h + 1) * DK)
        s = dot_nt(qkv_ref[i, :, cols_h], ks[:seen, :])
        s = s + strip[:, off : off + seen]
        s = jnp.where(column(segr_ref[:, mine]) == segr_ref[:, :seen], s, MASKED)
        top = jnp.max(s, axis=-1, keepdims=True)
        p = jnp.exp(s - top)
        total = jnp.sum(p, axis=-1, keepdims=True)
        attn_ref[i, :, cols_h] = (dot(p.astype(BF), vs[:seen, :]) / total).astype(BF)
        lse_ref[mine, h : h + 1] = top + jnp.log(total)

    own = pltpu.make_async_copy(attn_ref.at[me_t], mine_ref.at[me_t], lsem.at[4])
    swaps = []
    for k in range(1, nt):
        peer = lax.rem(me_t + k, nt)
        swaps.append(
            pltpu.make_async_remote_copy(
                attn_ref.at[peer],
                mine_ref.at[me_t],
                sends.take(),
                recvs.take(),
                device_id={"tensor": peer},
                device_id_type=MESH,
            )
        )

    def swap():
        for copy in swaps + [own]:
            copy.start()

    after.extend(copy.wait for copy in swaps + [own])
    compute = [(CORE1, weights)] + [(CORE1, partial(rows_start, i)) for i in range(nt)]
    for h in range(heads):
        compute.append((CORE1 + 1 + h, partial(head_start, h)))
        compute += [(CORE1 + 1 + h, partial(piece, h, i)) for i in range(nt)]
    compute.append((CORE1 + heads, swap))
    for tick, fn in compute:
        jobs.append((tick, [fn], [0]))
    run_jobs(jobs, after)


def forward_all(nt, nd, heads, tok, enc, wa, wb, segr, bl, tab):
    bits = nd.bit_length() - 1
    chunks = wb.shape[1] // STEP
    lines = chunks + (tok.shape[0] + enc.shape[0]) // PIECE
    total = lines * 2 * (nt - 1) + (2 * chunks + 1) * bits + nt - 1
    block, width = tok.shape
    length = nt * block
    hw = heads * DK
    return pl.pallas_call(
        partial(forward_kernel, nt, nd, heads),
        out_shape=(
            jax.ShapeDtypeStruct((nt,) + tok.shape, BF),
            jax.ShapeDtypeStruct((nt,) + enc.shape, BF),
            jax.ShapeDtypeStruct((nt, nd) + wb.shape, BF),
            jax.ShapeDtypeStruct((width, wa.shape[1]), BF),
            jax.ShapeDtypeStruct((8, width), F32),
            jax.ShapeDtypeStruct((nt, block, 3 * hw), BF),
            jax.ShapeDtypeStruct((length, 8), F32),
            jax.ShapeDtypeStruct((nt, block, hw), BF),
            jax.ShapeDtypeStruct((nt, block, hw), BF),
        ),
        in_specs=[VMEM] * 7,
        out_specs=(VMEM, ANY, ANY) + (VMEM,) * 6,
        scratch_shapes=[
            pltpu.VMEM((nd,) + wa.shape, BF),
            pltpu.VMEM((block, length + block), F32),
            pltpu.VMEM((length, DK), BF),
            pltpu.VMEM((length, DK), BF),
            pltpu.SemaphoreType.DMA((total,)),
            pltpu.SemaphoreType.DMA((total,)),
            pltpu.SemaphoreType.DMA((5,)),
        ],
        compiler_params=pltpu.CompilerParams(collective_id=0, has_side_effects=True, vmem_limit_bytes=LIMIT),
        name="forward_all",
    )(tok, enc, wa, wb, segr, bl, tab)


def cube_scatter(nd, me, order, value, recv, sends, recvs, after):
    count = len(order)
    sem = [(sends.take(), recvs.take()) for _ in range(count)]

    def start(k):
        bit = order[k]
        peer = flip(me, bit)
        for j, m in enumerate(subsets(order[k + 1 :])):
            pltpu.make_async_remote_copy(
                value(flip_all(peer, m)),
                recv[k].at[j],
                sem[k][0],
                sem[k][1],
                device_id={"dp": peer},
                device_id_type=MESH,
            ).start()

        def done():
            wait_bytes(recv[k], sem[k][0])

        after.append(done)

    def land(k):
        wait_bytes(recv[k], sem[k][1])
        for j, m in enumerate(subsets(order[k + 1 :])):
            add_into(value(flip_all(me, m)), recv[k].at[j])

    def stage(k):
        def run():
            if k > 0:
                land(k - 1)
            if k < count:
                start(k)

        return run

    return [stage(k) for k in range(count + 1)]


def line_scatter(nt, me, value, recv, out, sends, recvs, after):
    ssem, rsem = sends.many(2 * nt), recvs.many(2 * nt)

    def land(side, b):
        return recv.at[b + 1 - side]

    def hop(z):
        def run():
            for side, here in ((0, z), (1, nt - 1 - z)):
                goal = here + 1 if side == 0 else here - 1
                blocks = range(here + 1, nt) if side == 0 else range(here - 1, -1, -1)

                @pl.when(me == here)
                def _(side=side, goal=goal, blocks=blocks):
                    for b in blocks:
                        ref = value(b)
                        if z > 0:
                            got = land(side, b)
                            wait_bytes(got, rsem(side * nt + b))
                            add_into(ref, got)
                        pltpu.make_async_remote_copy(
                            ref,
                            land(side, b),
                            ssem(side * nt + b),
                            rsem(side * nt + b),
                            device_id={"tensor": goal},
                            device_id_type=MESH,
                        ).start()

        return run

    def last():
        own = value(me)

        def first(at):
            out[at, :] = own[at, :].astype(F32)

        row_loop(out.shape, first)
        for side, some in ((0, me > 0), (1, me < nt - 1)):

            @pl.when(some)
            def _(side=side):
                got = land(side, me)
                wait_bytes(got, rsem(side * nt + me))

                def more(at):
                    out[at, :] = out[at, :] + got[at, :].astype(F32)

                row_loop(out.shape, more)

    def done():
        for here in range(nt):

            @pl.when(me == here)
            def _(here=here):
                for b in range(here + 1, nt):
                    wait_bytes(land(0, b), ssem(b))
                for b in range(here):
                    wait_bytes(land(1, b), ssem(nt + b))

    after.append(done)
    return [hop(z) for z in range(nt - 1)] + [last]


def backward_kernel(
    nt,
    nd,
    heads,
    g_used,
    g_ref,
    e_ref,
    gain_in,
    dmine_ref,
    tok_ref,
    wa_ref,
    g0_ref,
    segr_ref,
    bl_ref,
    tab_ref,
    qkv_ref,
    attn_ref,
    lse_ref,
    g_out,
    a_out,
    u_out,
    e_out,
    *scratch,
):
    bits = nd.bit_length() - 1
    gv, uz, ez, gz = scratch[:4]
    arecv = scratch[4 : 4 + bits]
    grecv = scratch[4 + bits : 4 + 2 * bits]
    a_ref, u_ref, da_ref, strips, ks, vs, dkt, dvt, dqkv, lines, gain0 = scratch[4 + 2 * bits : 15 + 2 * bits]
    ssem, rsem, lsem = scratch[15 + 2 * bits :]
    cols = g_ref.shape[3]
    chunks = cols // STEP
    half = STEP // 2
    block = tok_ref.shape[1]
    hw = heads * DK
    width = strips.shape[1]
    strip, dstrip = strips.at[pl.ds(0, block)], strips.at[pl.ds(block, block)]
    gat = strips.at[pl.ds(0, 3 * hw), pl.ds(0, tok_ref.shape[2])]
    for c in range(chunks):
        at = pl.ds(c * STEP, STEP)
        pltpu.make_async_copy(g_ref.at[:, :, :, at], gv.at[:, :, :, at], lsem.at[c]).start()
    me_t, me_d = enter(nt, nd, True)
    sends, recvs, after = Sems(ssem), Sems(rsem), []
    orders = [[0] + o[:-1][::-1] for o in bit_orders(bits)]
    jobs = []

    own = pltpu.make_async_copy(dmine_ref.at[me_t], da_ref.at[me_t], lsem.at[chunks])
    own.start()
    swaps = []
    for k in range(1, nt):
        peer = lax.rem(me_t + k, nt)
        copy = pltpu.make_async_remote_copy(
            dmine_ref.at[peer], da_ref.at[me_t], sends.take(), recvs.take(), device_id={"tensor": peer}, device_id_type=MESH
        )
        copy.start()
        swaps.append(copy)

    def swapped():
        own.wait()
        for copy in swaps:
            copy.wait_recv()

    after.extend(copy.wait_send for copy in swaps)

    line, hot = bias_lines(bl_ref, tab_ref)

    def rows_of(i):
        return slice(i * block, (i + 1) * block)

    def head_start(h):
        build_strip(strip, line[h : h + 1, :])
        dstrip[...] = jnp.zeros_like(dstrip)
        dkt[...] = jnp.zeros_like(dkt)
        dvt[...] = jnp.zeros_like(dvt)
        for i in range(nt):
            ks[rows_of(i), :] = qkv_ref[i, :, hw + h * DK : hw + (h + 1) * DK]
            vs[rows_of(i), :] = qkv_ref[i, :, 2 * hw + h * DK : 2 * hw + (h + 1) * DK]

    def piece(h, i):
        mine = rows_of(i)
        seen = (i + 1) * block
        off = (nt - 1 - i) * block
        part = slice(h * DK, (h + 1) * DK)
        q = qkv_ref[i, :, part]
        da = da_ref[i, :, part]
        delta = jnp.sum(da.astype(F32) * attn_ref[i, :, part].astype(F32), axis=1, keepdims=True)
        s = dot_nt(q, ks[:seen, :])
        s = s + strip[:, off : off + seen]
        s = jnp.where(column(segr_ref[:, mine]) == segr_ref[:, :seen], s, MASKED)
        p = jnp.exp(s - lse_ref[mine, h : h + 1])
        dp = dot_nt(da, vs[:seen, :])
        ds = p * (dp - delta)
        low = ds.astype(BF)
        dqkv[mine, part] = dot(low, ks[:seen, :]).astype(BF)
        dkt[:, :seen] += dot_tn(q, low)
        dvt[:, :seen] += dot_tn(da, p.astype(BF))
        dstrip[:, off : off + seen] += ds

    def head_end(h):
        for i in range(nt):
            dqkv[rows_of(i), hw + h * DK : hw + (h + 1) * DK] = dkt[:, rows_of(i)].T.astype(BF)
            dqkv[rows_of(i), 2 * hw + h * DK : 2 * hw + (h + 1) * DK] = dvt[:, rows_of(i)].T.astype(BF)
        n = block // 2
        while n >= 8:
            dstrip[0:n, :] = dstrip[0:n, :] + pltpu.roll(dstrip[n : 2 * n, :], width - n, 1)
            n //= 2
        x = dstrip[0:8, :]
        row = lax.broadcasted_iota(jnp.int32, x.shape, 0)
        for b in range(3):
            x = jnp.where((row >> b) % 2 == 1, pltpu.roll(x, width - (1 << b), 1), x)
        lines[h : h + 1, :] = jnp.sum(x, axis=0, keepdims=True)

    def rows_end(i):
        mine = rows_of(i)
        x = tok_ref[i].astype(F32)
        hat = x * norm_scale(x)
        more = dot_tn(dqkv[mine, :], (hat * g0_ref[...]).astype(BF))
        gat[...] = more if i == 0 else gat[...] + more
        u = dot_nt(dqkv[mine, :], wa_ref[:, : 3 * hw])
        gain0[...] += jnp.sum(u * hat, axis=0, keepdims=True)
        u_ref[i] = u.astype(BF)

    def finish():
        table = lax.dot_general(
            lines[...],
            hot.astype(F32),
            (((1,), (1,)), ((), ())),
            precision=lax.Precision.HIGHEST,
            preferred_element_type=F32,
        )
        table = jnp.concatenate([table, jnp.zeros((8, 128 - table.shape[1]), F32)], axis=1).astype(BF)
        ga = gat[...].T.astype(BF)
        part = ga.shape[0] // nd
        for d in range(nd):
            a_ref[d, :, : 3 * hw] = ga[d * part : (d + 1) * part]
            a_ref[d, :, 3 * hw :] = jnp.zeros((part, 128), BF)
            a_ref[d, :8, 3 * hw :] = table

    def add_gains():
        at = g_used - (cols - 128)
        row = lax.broadcasted_iota(jnp.int32, (128, gain0.shape[1]), 0)
        gains = jnp.where(row == at, gain0[...], 0.0)
        gains = gains + jnp.where(row == at + 1, gain_in[0:1, :], 0.0) + jnp.where(row == at + 2, gain_in[1:2, :], 0.0)
        gains = gains.T.astype(BF)
        part = gains.shape[0] // nd

        def step(t, carry):
            for d in range(nd):
                gv[t, d, :, cols - 128 :] = gv[t, d, :, cols - 128 :] + gains[d * part : (d + 1) * part]
            return carry

        lax.fori_loop(0, nt, step, 0)

    lines[...] = jnp.zeros_like(lines)
    gain0[...] = jnp.zeros_like(gain0)

    def a_done():
        a_out[...] = a_ref[me_d].astype(F32)

    def chunk_job(c):
        first = c * STEP
        cubes = []
        for n in range(2):
            at = first + n * half
            cubes.append(
                cube_scatter(
                    nd,
                    me_d,
                    orders[n],
                    lambda d, at=at: gv.at[:, d, :, pl.ds(at, half)],
                    [r.at[2 * c + n] for r in grecv],
                    sends,
                    recvs,
                    after,
                )
            )
        z = line_scatter(
            nt,
            me_t,
            lambda b: gv.at[b, me_d, :, pl.ds(first, STEP)],
            gz.at[c],
            g_out.at[:, pl.ds(first, STEP)],
            sends,
            recvs,
            after,
        )

        def begin():
            at = pl.ds(first, STEP)
            pltpu.make_async_copy(g_ref.at[:, :, :, at], gv.at[:, :, :, at], lsem.at[c]).wait()
            if c == chunks - 1:
                add_gains()
            for q in cubes:
                q[0]()

        def both(k):
            def run():
                for q in cubes:
                    q[k]()

            return run

        def meet():
            for q in cubes:
                q[bits]()
            z[0]()

        return [begin] + [both(k) for k in range(1, bits)] + [meet] + z[1:]

    def row_job(ref, recv, out, n):
        at = pl.ds(n * PIECE, PIECE)
        return line_scatter(nt, me_t, lambda b: ref.at[b, at], recv.at[:, at], out.at[at], sends, recvs, after)

    ticks = [SPACE * k for k in range(bits)] + [SPACE * bits + k for k in range(nt)]
    for c in range(chunks):
        jobs.append((min(c, chunks - 1), chunk_job(c), ticks))
    for n in range(e_out.shape[0] // PIECE):
        jobs.append((n, row_job(e_ref, ez, e_out, n), list(range(nt))))
    compute = [(CORE0 - 1, partial(head_start, 0)), (CORE0, swapped)]
    for h in range(heads):
        if h > 0:
            compute.append((CORE0 + h, partial(head_start, h)))
        compute += [(CORE0 + h, partial(piece, h, i)) for i in range(nt)]
        compute.append((CORE0 + h, partial(head_end, h)))
    ready = CORE0 + heads
    compute += [(ready, partial(rows_end, i)) for i in range(nt)]
    compute.append((ready, finish))
    for tick, fn in compute:
        jobs.append((tick, [fn], [0]))
    a_job = cube_scatter(nd, me_d, orders[0], lambda d: a_ref.at[d], arecv, sends, recvs, after) + [a_done]
    jobs.append((ready + 1, a_job, [SPACE * k for k in range(bits + 1)] + [SPACE * bits]))
    for n in range(u_out.shape[0] // PIECE):
        jobs.append((ready + 1 + n, row_job(u_ref, uz, u_out, n), list(range(nt))))
    run_jobs(jobs, after)


def backward_all(nt, nd, heads, used, g, e, gain12, dmine, tok, wa, g0, segr, bl, tab, qkv, attn, lse):
    bits = nd.bit_length() - 1
    rows, cols = g.shape[2:]
    block, width = tok.shape[1:]
    length = nt * block
    wide = wa.shape[1]
    hw = heads * DK
    chunks = cols // STEP
    lines = chunks + (block + e.shape[1]) // PIECE
    total = lines * 2 * nt + (2 * chunks + 1) * bits + nt - 1
    return pl.pallas_call(
        partial(backward_kernel, nt, nd, heads, used),
        out_shape=(
            jax.ShapeDtypeStruct((rows, cols), F32),
            jax.ShapeDtypeStruct((rows, wide), F32),
            jax.ShapeDtypeStruct((block, width), F32),
            jax.ShapeDtypeStruct(e.shape[1:], F32),
        ),
        in_specs=[ANY] + [VMEM] * 12,
        out_specs=(VMEM,) * 4,
        scratch_shapes=[
            pltpu.VMEM((nt, nd, rows, cols), BF),
            pltpu.VMEM((nt + 1, block, width), BF),
            pltpu.VMEM((nt + 1,) + e.shape[1:], BF),
            pltpu.VMEM((chunks, nt + 1, rows, STEP), BF),
        ]
        + [pltpu.VMEM((1 << (bits - 1 - k), rows, wide), BF) for k in range(bits)]
        + [pltpu.VMEM((2 * chunks, 1 << (bits - 1 - k), nt, rows, STEP // 2), BF) for k in range(bits)]
        + [
            pltpu.VMEM((nd, rows, wide), BF),
            pltpu.VMEM((nt, block, width), BF),
            pltpu.VMEM((nt, block, hw), BF),
            pltpu.VMEM((max(2 * block, 3 * hw), length + block), F32),
            pltpu.VMEM((length, DK), BF),
            pltpu.VMEM((length, DK), BF),
            pltpu.VMEM((DK, length), F32),
            pltpu.VMEM((DK, length), F32),
            pltpu.VMEM((length, 3 * hw), BF),
            pltpu.VMEM((8, length + block), F32),
            pltpu.VMEM((1, width), F32),
            pltpu.SemaphoreType.DMA((total,)),
            pltpu.SemaphoreType.DMA((total,)),
            pltpu.SemaphoreType.DMA((chunks + 1,)),
        ],
        compiler_params=pltpu.CompilerParams(collective_id=1, has_side_effects=True, vmem_limit_bytes=LIMIT),
        name="backward_all",
    )(g, e, gain12, dmine, tok, wa, g0, segr, bl, tab, qkv, attn, lse)


def column(row):
    return jnp.broadcast_to(row, (8, row.shape[1])).T[:, 0:1]


def build_strip(strip, x):
    block, width = strip.shape
    row = lax.broadcasted_iota(jnp.int32, (8, width), 0)
    x = jnp.broadcast_to(x, (8, width))
    for b in range(3):
        x = jnp.where((row >> b) % 2 == 1, pltpu.roll(x, 1 << b, 1), x)
    strip[0:8, :] = x
    n = 8
    while n < block:
        strip[n : 2 * n, :] = pltpu.roll(strip[0:n, :], n, 1)
        n *= 2


def bias_lines(bl_ref, tab_ref):
    width = bl_ref.shape[1]
    buckets = tab_ref.shape[1]
    hot = bl_ref[...] == lax.broadcasted_iota(jnp.int32, (buckets, width), 0)
    line = dot(tab_ref[...], hot.astype(F32).astype(BF))
    return jnp.where(bl_ref[...] >= 0, line, MASKED), hot


def middle_kernel(
    heads,
    ff,
    tok_ref,
    enc_ref,
    attn_ref,
    og_ref,
    gains_ref,
    w_hbm,
    layer_ref,
    one_ref,
    denc_ref,
    gain_ref,
    dattn_ref,
    g_hbm,
    w,
    g,
    h1_ref,
    h2_ref,
    n1_ref,
    n2_ref,
    acc_ref,
    dn_ref,
    g2_ref,
    denc,
    qc,
    kv,
    ac,
    oc,
    lse,
    dkv,
    insem,
    outsem,
):
    nt = w.shape[0]
    hw = heads * DK
    cols = w.shape[2]
    f0, f1, f2 = 0, ff, 2 * ff
    kv0 = 3 * ff
    q0 = kv0 + 2 * hw
    c0 = q0 + hw
    s0 = c0 + hw
    end = s0 + hw
    ffn = pl.ds(0, 3 * ff)
    att = pl.ds(3 * ff, cols - 3 * ff)
    loads = [pltpu.make_async_copy(w_hbm.at[t, :, att], w.at[t, :, att], insem.at[0, t]) for t in range(nt)]
    loads += [pltpu.make_async_copy(w_hbm.at[t, :, ffn], w.at[t, :, ffn], insem.at[1, t]) for t in range(nt)]
    for copy in loads:
        copy.start()

    def load_wait(which, t):
        at = att if which == 0 else ffn
        pltpu.make_async_copy(w_hbm.at[t, :, at], w.at[t, :, at], insem.at[which, t]).wait()

    def store(which, t):
        at = att if which == 0 else ffn
        return pltpu.make_async_copy(g.at[t, :, at], g_hbm.at[t, :, at], outsem.at[which, t])

    acc_ref[...] = tok_ref[...].astype(F32)

    def self_out(t, carry):
        load_wait(0, t)
        acc_ref[...] += dot_nt(attn_ref[t], w[t, :, s0:end])
        return carry

    lax.fori_loop(0, nt, self_out, 0)
    h1 = acc_ref[...]
    h1_ref[...] = h1
    n1_ref[...] = (h1 * norm_scale(h1) * gains_ref[1:2, :]).astype(BF)

    def cross(t, carry):
        q = dot(n1_ref[...], w[t, :, q0:c0]).astype(BF)
        both = dot(enc_ref[...], w[t, :, kv0:q0]).astype(BF)
        qc[t] = q
        kv[t] = both
        outs = []
        for h in range(heads):
            part = slice(h * DK, (h + 1) * DK)
            s = dot_nt(q[:, part], both[:, part])
            top = jnp.max(s, axis=-1, keepdims=True)
            p = jnp.exp(s - top)
            total = jnp.sum(p, axis=-1, keepdims=True)
            lse[t, h] = top + jnp.log(total)
            outs.append(dot(p.astype(BF), both[:, hw + h * DK : hw + (h + 1) * DK]) / total)
        a = jnp.concatenate(outs, axis=1).astype(BF)
        ac[t] = a
        acc_ref[...] += dot_nt(a, w[t, :, c0:s0])
        return carry

    lax.fori_loop(0, nt, cross, 0)
    h2 = acc_ref[...]
    h2_ref[...] = h2
    n2_ref[...] = (h2 * norm_scale(h2) * gains_ref[2:3, :]).astype(BF)
    dn_ref[...] = jnp.zeros_like(dn_ref)

    def units(t, carry):
        load_wait(1, t)
        n2 = n2_ref[...]
        og = og_ref[...]
        gate = dot(n2, w[t, :, f0:f1])
        up = dot(n2, w[t, :, f1:f2])
        dinner = dot(og, w[t, :, f2 : 3 * ff])
        sq = gate * gate
        th = jnp.tanh(0.7978845608028654 * (gate + 0.044715 * (gate * sq)))
        cdf = 0.5 * (1.0 + th)
        act = gate * cdf
        slope = cdf + gate * (0.5 * (1.0 - th * th)) * (0.7978845608028654 * (1.0 + 0.134145 * sq))
        inner = (act * up).astype(BF)
        dgate = (dinner * up * slope).astype(BF)
        dup = (dinner * act).astype(BF)
        acc_ref[...] += dot_nt(inner, w[t, :, f2 : 3 * ff])
        dn_ref[...] += dot_nt(dgate, w[t, :, f0:f1]) + dot_nt(dup, w[t, :, f1:f2])
        g[t, :, f0:f1] = dot_tn(n2, dgate).astype(BF)
        g[t, :, f1:f2] = dot_tn(n2, dup).astype(BF)
        g[t, :, f2 : 3 * ff] = dot_tn(og, inner).astype(BF)
        store(1, t).start()
        return carry

    lax.fori_loop(0, nt, units, 0)
    layer_ref[...] = acc_ref[...].astype(BF)
    h2 = h2_ref[...]
    back, gain2 = norm_back(h2, norm_scale(h2), gains_ref[2:3, :], dn_ref[...])
    g2 = og_ref[...].astype(F32) + back
    acc_ref[...] = g2
    g2_ref[...] = g2.astype(BF)
    dn_ref[...] = jnp.zeros_like(dn_ref)
    denc[...] = jnp.zeros_like(denc)

    def cross_back(t, carry):
        g2 = g2_ref[...]
        a = ac[t]
        da = dot(g2, w[t, :, c0:s0]).astype(BF)
        g[t, :, c0:s0] = dot_tn(g2, a).astype(BF)
        prod = da.astype(F32) * a.astype(F32)
        q = qc[t]
        both = kv[t]
        dqs = []
        for h in range(heads):
            part = slice(h * DK, (h + 1) * DK)
            qh, kh = q[:, part], both[:, part]
            vh, dah = both[:, hw + h * DK : hw + (h + 1) * DK], da[:, part]
            p = jnp.exp(dot_nt(qh, kh) - lse[t, h])
            delta = jnp.sum(prod[:, part], axis=1, keepdims=True)
            ds = (p * (dot_nt(dah, vh) - delta)).astype(BF)
            dqs.append(dot(ds, kh))
            dkv[h * DK : (h + 1) * DK, :] = dot_tn(qh, ds)
            dkv[hw + h * DK : hw + (h + 1) * DK, :] = dot_tn(dah, p.astype(BF))
        dq = jnp.concatenate(dqs, axis=1).astype(BF)
        dboth = dkv[...].astype(BF)
        g[t, :, q0:c0] = dot_tn(n1_ref[...], dq).astype(BF)
        g[t, :, kv0:q0] = lax.dot_general(
            enc_ref[...], dboth, (((0,), (1,)), ((), ())), preferred_element_type=F32
        ).astype(BF)
        dn_ref[...] += dot_nt(dq, w[t, :, q0:c0])
        denc[...] += lax.dot_general(
            dboth, w[t, :, kv0:q0], (((0,), (1,)), ((), ())), preferred_element_type=F32
        )
        return carry

    lax.fori_loop(0, nt, cross_back, 0)
    denc_ref[...] = denc[...].astype(BF)
    h1 = h1_ref[...]
    back, gain1 = norm_back(h1, norm_scale(h1), gains_ref[1:2, :], dn_ref[...])
    g1 = acc_ref[...] + back
    one_ref[...] = g1
    g2_ref[...] = g1.astype(BF)
    gain_ref[...] = jnp.concatenate([gain1, gain2, jnp.zeros((6, gain1.shape[1]), F32)], axis=0)

    def self_out_back(t, carry):
        low = g2_ref[...]
        dattn_ref[t] = dot(low, w[t, :, s0:end]).astype(BF)
        tail = dot_tn(low, attn_ref[t])
        g[t, :, s0:cols] = jnp.concatenate([tail, jnp.zeros((tail.shape[0], cols - end), F32)], axis=1).astype(BF)
        store(0, t).start()
        return carry

    lax.fori_loop(0, nt, self_out_back, 0)
    for t in range(nt):
        store(1, t).wait()
        store(0, t).wait()


def middle(heads, ff, tok, enc, attn, og, gains, w):
    nt, _, cols = w.shape
    rows, width = tok.shape
    states = enc.shape[0]
    hw = heads * DK
    return pl.pallas_call(
        partial(middle_kernel, heads, ff),
        out_shape=(
            jax.ShapeDtypeStruct((rows, width), BF),
            jax.ShapeDtypeStruct((rows, width), F32),
            jax.ShapeDtypeStruct((states, width), BF),
            jax.ShapeDtypeStruct((8, width), F32),
            jax.ShapeDtypeStruct((nt, rows, hw), BF),
            jax.ShapeDtypeStruct(w.shape, BF),
        ),
        in_specs=[VMEM] * 5 + [ANY],
        out_specs=(VMEM,) * 5 + (ANY,),
        scratch_shapes=[
            pltpu.VMEM(w.shape, BF),
            pltpu.VMEM(w.shape, BF),
            pltpu.VMEM((rows, width), F32),
            pltpu.VMEM((rows, width), F32),
            pltpu.VMEM((rows, width), BF),
            pltpu.VMEM((rows, width), BF),
            pltpu.VMEM((rows, width), F32),
            pltpu.VMEM((rows, width), F32),
            pltpu.VMEM((rows, width), BF),
            pltpu.VMEM((states, width), F32),
            pltpu.VMEM((nt, rows, hw), BF),
            pltpu.VMEM((nt, states, 2 * hw), BF),
            pltpu.VMEM((nt, rows, hw), BF),
            pltpu.VMEM((8, 128), F32),
            pltpu.VMEM((nt, heads, rows, 1), F32),
            pltpu.VMEM((2 * hw, states), F32),
            pltpu.SemaphoreType.DMA((2, nt)),
            pltpu.SemaphoreType.DMA((2, nt)),
        ],
        compiler_params=pltpu.CompilerParams(vmem_limit_bytes=LIMIT),
        name="middle",
    )(tok, enc, attn, og, gains, w)


def per_device(
    tokens,
    encoder,
    segments,
    rel_bucket,
    out_grad,
    self_q,
    self_k,
    self_v,
    self_o,
    cross_q,
    cross_k,
    cross_v,
    cross_o,
    ffn_gate,
    ffn_up,
    ffn_down,
    bias_table,
    norm_gains,
):
    nt, nd = lax.axis_size("tensor"), lax.axis_size("dp")
    part, hw = self_q.shape
    ff = ffn_gate.shape[1]
    heads = hw // DK
    rows, width = tokens.shape
    length = rows * nt
    buckets = bias_table.shape[0]
    wa = jnp.concatenate([self_q, self_k, self_v, jnp.pad(norm_gains.T, ((0, 0), (0, 128 - norm_gains.shape[0])))], axis=1)
    wb = jnp.concatenate([ffn_gate, ffn_up, ffn_down.T, cross_k, cross_v, cross_q, cross_o.T, self_o.T], axis=1)
    used = wb.shape[1]
    cols = -(-(used + 3) // STEP) * STEP
    wb = jnp.pad(wb, ((0, 0), (0, cols - used)))
    top = (nt - 1) * rows
    blank = jnp.full((length - 1 - top,), -1, jnp.int32)
    bl = jnp.concatenate(
        [rel_bucket[: top + 1][::-1], blank, jnp.full((1,), -1, jnp.int32), rel_bucket[top + 1 : length][::-1]]
    )[None, :]
    tab = jnp.pad(bias_table.T, ((0, 8 - heads), (0, 0)))
    segr = segments
    tok_all, enc_all, wb_all, wa_full, gains, qkv, lse, attn, mine = forward_all(
        nt, nd, heads, tokens, encoder, wa, wb, segr, bl, tab
    )
    wb_full = wb_all.reshape(nt, nd * part, cols)
    g0 = gains[0:1]
    layer_out, grad_one, denc, gain12, dmine, gb = middle(
        heads, ff, tokens, enc_all.reshape(nt * encoder.shape[0], width), mine, out_grad, gains, wb_full
    )
    gsum, asum, usum, esum = backward_all(
        nt,
        nd,
        heads,
        used,
        gb.reshape(nt, nd, part, cols),
        denc.reshape((nt,) + encoder.shape),
        gain12,
        dmine,
        tok_all,
        wa_full,
        g0,
        segr,
        bl,
        tab,
        qkv,
        attn,
        lse,
    )
    x = tokens.astype(F32)
    back, _ = norm_back(x, norm_scale(x), g0, usum)
    tokens_grad = grad_one + back
    at = 3 * ff
    ck, cv, cq, co, so = (gsum[:, at + n * hw : at + (n + 1) * hw] for n in range(5))
    return (
        layer_out,
        tokens_grad,
        esum,
        asum[:, :hw],
        asum[:, hw : 2 * hw],
        asum[:, 2 * hw : 3 * hw],
        so.T,
        cq,
        ck,
        cv,
        co.T,
        gsum[:, :ff],
        gsum[:, ff : 2 * ff],
        gsum[:, 2 * ff : 3 * ff].T,
        asum[:heads, 3 * hw : 3 * hw + buckets].T,
        gsum[:, used : used + 3].T,
    )


def solution(mesh):
    rows = P(("dp", "tensor"), None)
    left = P("dp", "tensor")
    right = P("tensor", "dp")
    return jax.shard_map(
        per_device,
        mesh=mesh,
        in_specs=(rows, rows, P("dp", None), P(), rows, left, left, left, right, left, left, left, right, left, left, right)
        + (P(None, "tensor"), P(None, "dp")),
        out_specs=(rows, rows, rows, left, left, left, right, left, left, left, right, left, left, right)
        + (P(None, "tensor"), P(None, "dp")),
        check_vma=False,
    )
```

```python
from functools import partial

import jax
import jax.numpy as jnp
from jax import lax
from jax.experimental import pallas as pl
from jax.experimental.pallas import tpu as pltpu
from jax.sharding import PartitionSpec as P

DK = 64
EPS = 1e-06
MASKED = -1e30
BF = jnp.bfloat16
F32 = jnp.float32
MESH = pl.DeviceIdType.MESH
VMEM = pl.BlockSpec(memory_space=pltpu.VMEM)
ANY = pl.BlockSpec(memory_space=pl.ANY)
LIMIT = 510 * 128 * 1024
STEP = 256
SPACE = 2
PIECE = 32
TOK0 = 2
TOKR = 1
CORE0 = 4
CORE1 = 13


def dot(a, b):
    return jnp.dot(a, b, preferred_element_type=F32)


def dot_nt(a, b):
    return lax.dot_general(a, b, (((1,), (1,)), ((), ())), preferred_element_type=F32)


def dot_tn(a, b):
    return lax.dot_general(a, b, (((0,), (0,)), ((), ())), preferred_element_type=F32)


def norm_scale(x):
    return lax.rsqrt(jnp.mean(x * x, axis=-1, keepdims=True) + EPS)


def norm_back(x, r, g, u):
    w = u * g
    inner = jnp.mean(w * x, axis=-1, keepdims=True)
    return r * w - x * (r * r * r * inner), jnp.sum(u * (x * r), axis=0, keepdims=True)


def flip(index, bit):
    size = 1 << bit
    return index + size - 2 * size * lax.rem(index // size, 2)


def flip_all(index, mask):
    bit = 0
    while mask:
        if mask & 1:
            index = flip(index, bit)
        mask >>= 1
        bit += 1
    return index


def subsets(bits):
    out = [0]
    for b in bits:
        out = out + [m | (1 << b) for m in out]
    return out


def bit_orders(count):
    upper = list(range(1, count))
    return [upper + [0], upper[::-1] + [0]]


class Sems:
    def __init__(self, ref):
        self.ref = ref
        self.used = 0

    def take(self):
        self.used += 1
        return self.ref.at[self.used - 1]

    def many(self, count):
        base = self.used
        self.used += count
        return lambda n: self.ref.at[base + n]


def wait_bytes(ref, sem):
    pltpu.make_async_copy(ref, ref, sem).wait()


def row_loop(shape, body):
    size = 32 if shape[1] <= 256 else 16
    if shape[0] % size:
        body(slice(0, shape[0]))
        return

    def step(n, carry):
        body(pl.ds(pl.multiple_of(n * size, size), size))
        return carry

    lax.fori_loop(0, shape[0] // size, step, 0)


def add_into(ref, got):
    if len(ref.shape) == 2:

        def body(at):
            ref[at, :] = ref[at, :] + got[at, :]

        row_loop(ref.shape, body)
    else:

        def step(t, carry):
            ref[t] = ref[t] + got[t]
            return carry

        lax.fori_loop(0, ref.shape[0], step, 0)


def enter(nt, nd, all_tensor=False):
    me_t, me_d = lax.axis_index("tensor"), lax.axis_index("dp")
    bar = pltpu.get_barrier_semaphore()
    bits = nd.bit_length() - 1
    for b in range(bits):
        pl.semaphore_signal(bar, 1, device_id={"dp": flip(me_d, b)}, device_id_type=MESH)
    if all_tensor:
        for k in range(1, nt):
            pl.semaphore_signal(bar, 1, device_id={"tensor": lax.rem(me_t + k, nt)}, device_id_type=MESH)
        pl.semaphore_wait(bar, bits + nt - 1)
        return me_t, me_d

    @pl.when(me_t > 0)
    def _():
        pl.semaphore_signal(bar, 1, device_id={"tensor": me_t - 1}, device_id_type=MESH)

    @pl.when(me_t < nt - 1)
    def _():
        pl.semaphore_signal(bar, 1, device_id={"tensor": me_t + 1}, device_id_type=MESH)

    pl.semaphore_wait(bar, bits + (me_t + nt - 1) // nt + (2 * nt - 2 - me_t) // nt)
    return me_t, me_d


def run_jobs(jobs, after):
    events = []
    for number, (start, stages, ticks) in enumerate(jobs):
        for tick, stage in zip(ticks, stages, strict=True):
            events.append((start + tick, start, number, stage))
    for event in sorted(events, key=lambda e: e[:3]):
        event[3]()
    for fn in after:
        fn()


def line_gather(nt, me, own, slot, sends, recvs, after):
    sem = {(s, j): (sends.take(), recvs.take()) for s in (1, -1) for j in range(1, nt)}

    def send(side, j):
        block = me - side * (j - 1)
        target = me + side
        ok = (block >= 0) & (block < nt) & (target >= 0) & (target < nt)
        src = own if j == 1 else slot(jnp.clip(block, 0, nt - 1))
        dst = slot(jnp.clip(block, 0, nt - 1))
        ss, rs = sem[side, j]

        @pl.when(ok)
        def _():
            pltpu.make_async_remote_copy(
                src, dst, ss, rs, device_id={"tensor": target}, device_id_type=MESH
            ).start()

        def done():
            @pl.when(ok)
            def _():
                wait_bytes(own, ss)

        after.append(done)

    def arrive(side, j):
        block = me - side * j

        @pl.when((block >= 0) & (block < nt))
        def _():
            wait_bytes(own, sem[side, j][1])

    def stage(j):
        def run():
            for side in (1, -1):
                if j > 0:
                    arrive(side, j)
                if j < nt - 1:
                    send(side, j + 1)

        return run

    return [stage(j) for j in range(nt)]


def cube_gather(nd, me, order, own, slot, slots, sends, recvs, after):
    count = len(order)
    sem = [(sends.take(), recvs.take()) for _ in range(count)]

    def start(k):
        bit = order[k]
        for m in subsets(order[:k]):
            block = flip_all(me, m)
            src = own if (m == 0 and own is not None) else slot(block)
            pltpu.make_async_remote_copy(
                src, slot(block), sem[k][0], sem[k][1], device_id={"dp": flip(me, bit)}, device_id_type=MESH
            ).start()

        def done():
            wait_bytes(slots(1 << k), sem[k][0])

        after.append(done)

    def stage(k):
        def run():
            if k > 0:
                wait_bytes(slots(1 << (k - 1)), sem[k - 1][1])
            if k < count:
                start(k)

        return run

    return [stage(k) for k in range(count + 1)]


def forward_kernel(
    nt,
    nd,
    heads,
    tok_ref,
    enc_ref,
    wa_ref,
    wb_ref,
    segr_ref,
    bl_ref,
    tab_ref,
    tok_out,
    enc_out,
    wb_out,
    wa_full,
    gain_ref,
    qkv_ref,
    lse_ref,
    attn_ref,
    mine_ref,
    wa_out,
    strip,
    bias,
    qs,
    ks,
    vs,
    os,
    lses,
    ssem,
    rsem,
    lsem,
):
    me_t, me_d = enter(nt, nd, True)
    bits = nd.bit_length() - 1
    sends, recvs, after = Sems(ssem), Sems(rsem), []
    locals_ = [
        (tok_ref, tok_out.at[me_t]),
        (enc_ref, enc_out.at[me_t]),
        (wa_ref, wa_out.at[me_d]),
        (wb_ref, wb_out.at[me_t, me_d]),
    ]
    for n, (src, dst) in enumerate(locals_):
        pltpu.make_async_copy(src, dst, lsem.at[n]).start()
    orders = bit_orders(bits)
    cols = wb_ref.shape[1]
    chunks = cols // STEP
    half = STEP // 2
    jobs = []
    jobs.append(
        (
            0,
            cube_gather(nd, me_d, orders[0], wa_ref, lambda d: wa_out.at[d], lambda n: wa_out.at[pl.ds(0, n)], sends, recvs, after),
            [SPACE * k for k in range(bits + 1)],
        )
    )

    def chunk_job(c):
        first = c * STEP
        z = line_gather(
            nt,
            me_t,
            wb_ref.at[:, pl.ds(first, STEP)],
            lambda t: wb_out.at[t, me_d, :, pl.ds(first, STEP)],
            sends,
            recvs,
            after,
        )
        cubes = []
        for n in range(2):
            at = first + n * half
            cubes.append(
                cube_gather(
                    nd,
                    me_d,
                    orders[n],
                    None,
                    lambda d, at=at: wb_out.at[:, d, :, pl.ds(at, half)],
                    lambda k, at=at: wb_out.at[:, pl.ds(0, k), :, pl.ds(at, half)],
                    sends,
                    recvs,
                    after,
                )
            )

        def meet():
            z[-1]()
            for q in cubes:
                q[0]()

        def both(k):
            def run():
                for q in cubes:
                    q[k]()

            return run

        return z[:-1] + [meet] + [both(k) for k in range(1, bits + 1)]


    def row_job(ref, out, n):
        at = pl.ds(n * PIECE, PIECE)
        return line_gather(nt, me_t, ref.at[at], lambda t: out.at[t, at], sends, recvs, after)

    ticks = list(range(nt)) + [nt - 1 + SPACE * k for k in range(1, bits + 1)]
    for c in range(chunks):
        jobs.append((c, chunk_job(c), ticks))
    number = TOK0
    for ref, out in ((tok_ref, tok_out), (enc_ref, enc_out)):
        for n in range(ref.shape[0] // PIECE):
            jobs.append((number // TOKR, row_job(ref, out, n), list(range(nt))))
            number += 1
    pltpu.make_async_copy(wb_ref, wb_out.at[me_t, me_d], lsem.at[3]).wait()
    after.append(lambda: pltpu.make_async_copy(enc_ref, enc_out.at[me_t], lsem.at[1]).wait())

    block = tok_ref.shape[0]
    part = wa_ref.shape[0]
    hw = heads * DK
    bias[...] = bias_lines(bl_ref, tab_ref)[0]

    def rows_of(i):
        return slice(i * block, (i + 1) * block)

    def weights():
        for n in (0, 2):
            src, dst = locals_[n]
            pltpu.make_async_copy(src, dst, lsem.at[n]).wait()
        for d in range(nd):
            wa_full[d * part : (d + 1) * part, :] = wa_out[d]
        gain_ref[...] = wa_full[:, 3 * hw :].astype(F32).T[0:8]

    def rows_start(i):
        x = tok_out[i].astype(F32)
        n = (x * norm_scale(x) * gain_ref[0:1, :]).astype(BF)
        y = dot(n, wa_full[:, : 3 * hw]).astype(BF)
        qkv_ref[i] = y
        for h in range(heads):
            for which, ref in enumerate((qs, ks, vs)):
                at = which * hw + h * DK
                ref[h, rows_of(i), :] = y[:, at : at + DK]

    def head(h, carry):
        build_strip(strip, bias[pl.ds(h, 1), :])
        for i in range(nt):
            piece(h, i)
        return carry

    def piece(h, i):
        mine = rows_of(i)
        seen = (i + 1) * block
        off = (nt - 1 - i) * block
        s = dot_nt(qs[h, mine, :], ks[h, :seen, :])
        s = s + strip[:, off : off + seen]
        s = jnp.where(column(segr_ref[:, mine]) == segr_ref[:, :seen], s, MASKED)
        top = jnp.max(s, axis=-1, keepdims=True)
        p = jnp.exp(s - top)
        total = jnp.sum(p, axis=-1, keepdims=True)
        os[h, mine, :] = (dot(p.astype(BF), vs[h, :seen, :]) / total).astype(BF)
        lses[h, mine, :] = top + jnp.log(total)

    def collect():
        for i in range(nt):
            for h in range(heads):
                attn_ref[i, :, h * DK : (h + 1) * DK] = os[h, rows_of(i), :]
                lse_ref[rows_of(i), h : h + 1] = lses[h, rows_of(i), :]

    own = pltpu.make_async_copy(attn_ref.at[me_t], mine_ref.at[me_t], lsem.at[4])
    swaps = []
    for k in range(1, nt):
        peer = lax.rem(me_t + k, nt)
        swaps.append(
            pltpu.make_async_remote_copy(
                attn_ref.at[peer],
                mine_ref.at[me_t],
                sends.take(),
                recvs.take(),
                device_id={"tensor": peer},
                device_id_type=MESH,
            )
        )

    def swap():
        for copy in swaps + [own]:
            copy.start()

    after.extend(copy.wait for copy in swaps + [own])
    compute = [(CORE1, weights)] + [(CORE1, partial(rows_start, i)) for i in range(nt)]
    compute.append((CORE1 + 1, lambda: lax.fori_loop(0, heads, head, 0)))
    compute += [(CORE1 + 1, collect), (CORE1 + 1, swap)]
    for tick, fn in compute:
        jobs.append((tick, [fn], [0]))
    run_jobs(jobs, after)


def forward_all(nt, nd, heads, tok, enc, wa, wb, segr, bl, tab):
    bits = nd.bit_length() - 1
    chunks = wb.shape[1] // STEP
    lines = chunks + (tok.shape[0] + enc.shape[0]) // PIECE
    total = lines * 2 * (nt - 1) + (2 * chunks + 1) * bits + nt - 1
    block, width = tok.shape
    length = nt * block
    hw = heads * DK
    return pl.pallas_call(
        partial(forward_kernel, nt, nd, heads),
        out_shape=(
            jax.ShapeDtypeStruct((nt,) + tok.shape, BF),
            jax.ShapeDtypeStruct((nt,) + enc.shape, BF),
            jax.ShapeDtypeStruct((nt, nd) + wb.shape, BF),
            jax.ShapeDtypeStruct((width, wa.shape[1]), BF),
            jax.ShapeDtypeStruct((8, width), F32),
            jax.ShapeDtypeStruct((nt, block, 3 * hw), BF),
            jax.ShapeDtypeStruct((length, 8), F32),
            jax.ShapeDtypeStruct((nt, block, hw), BF),
            jax.ShapeDtypeStruct((nt, block, hw), BF),
        ),
        in_specs=[VMEM] * 7,
        out_specs=(VMEM, ANY, ANY) + (VMEM,) * 6,
        scratch_shapes=[
            pltpu.VMEM((nd,) + wa.shape, BF),
            pltpu.VMEM((block, length + block), F32),
            pltpu.VMEM((8, length + block), F32),
        ]
        + [pltpu.VMEM((heads, length, DK), BF)] * 4
        + [
            pltpu.VMEM((heads, length, 1), F32),
            pltpu.SemaphoreType.DMA((total,)),
            pltpu.SemaphoreType.DMA((total,)),
            pltpu.SemaphoreType.DMA((5,)),
        ],
        compiler_params=pltpu.CompilerParams(collective_id=0, has_side_effects=True, vmem_limit_bytes=LIMIT),
        name="forward_all",
    )(tok, enc, wa, wb, segr, bl, tab)


def cube_scatter(nd, me, order, value, recv, sends, recvs, after):
    count = len(order)
    sem = [(sends.take(), recvs.take()) for _ in range(count)]

    def start(k):
        bit = order[k]
        peer = flip(me, bit)
        for j, m in enumerate(subsets(order[k + 1 :])):
            pltpu.make_async_remote_copy(
                value(flip_all(peer, m)),
                recv[k].at[j],
                sem[k][0],
                sem[k][1],
                device_id={"dp": peer},
                device_id_type=MESH,
            ).start()

        def done():
            wait_bytes(recv[k], sem[k][0])

        after.append(done)

    def land(k):
        wait_bytes(recv[k], sem[k][1])
        for j, m in enumerate(subsets(order[k + 1 :])):
            add_into(value(flip_all(me, m)), recv[k].at[j])

    def stage(k):
        def run():
            if k > 0:
                land(k - 1)
            if k < count:
                start(k)

        return run

    return [stage(k) for k in range(count + 1)]


def line_scatter(nt, me, value, recv, out, sends, recvs, after):
    ssem, rsem = sends.many(2 * nt), recvs.many(2 * nt)

    def land(side, b):
        return recv.at[b + 1 - side]

    def hop(z):
        def run():
            for side, here in ((0, z), (1, nt - 1 - z)):
                goal = here + 1 if side == 0 else here - 1
                blocks = range(here + 1, nt) if side == 0 else range(here - 1, -1, -1)

                @pl.when(me == here)
                def _(side=side, goal=goal, blocks=blocks):
                    for b in blocks:
                        ref = value(b)
                        if z > 0:
                            got = land(side, b)
                            wait_bytes(got, rsem(side * nt + b))
                            add_into(ref, got)
                        pltpu.make_async_remote_copy(
                            ref,
                            land(side, b),
                            ssem(side * nt + b),
                            rsem(side * nt + b),
                            device_id={"tensor": goal},
                            device_id_type=MESH,
                        ).start()

        return run

    def last():
        own = value(me)

        def first(at):
            out[at, :] = own[at, :].astype(F32)

        row_loop(out.shape, first)
        for side, some in ((0, me > 0), (1, me < nt - 1)):

            @pl.when(some)
            def _(side=side):
                got = land(side, me)
                wait_bytes(got, rsem(side * nt + me))

                def more(at):
                    out[at, :] = out[at, :] + got[at, :].astype(F32)

                row_loop(out.shape, more)

    def done():
        for here in range(nt):

            @pl.when(me == here)
            def _(here=here):
                for b in range(here + 1, nt):
                    wait_bytes(land(0, b), ssem(b))
                for b in range(here):
                    wait_bytes(land(1, b), ssem(nt + b))

    after.append(done)
    return [hop(z) for z in range(nt - 1)] + [last]


def backward_kernel(
    nt,
    nd,
    heads,
    g_used,
    g_ref,
    e_ref,
    gain_in,
    dmine_ref,
    tok_ref,
    wa_ref,
    g0_ref,
    segr_ref,
    bl_ref,
    tab_ref,
    qkv_ref,
    lse_ref,
    g_out,
    a_out,
    u_out,
    e_out,
    *scratch,
):
    bits = nd.bit_length() - 1
    gv, uz, ez, gz = scratch[:4]
    arecv = scratch[4 : 4 + bits]
    grecv = scratch[4 + bits : 4 + 2 * bits]
    a_ref, u_ref, da_ref, strips, qs, ks, vs, das, dkt, dvt, dqkv, lines, bias, gain0 = scratch[4 + 2 * bits : 18 + 2 * bits]
    ssem, rsem, lsem = scratch[18 + 2 * bits :]
    cols = g_ref.shape[3]
    chunks = cols // STEP
    half = STEP // 2
    block = tok_ref.shape[1]
    hw = heads * DK
    width = strips.shape[1]
    strip, dstrip = strips.at[pl.ds(0, block)], strips.at[pl.ds(block, block)]
    gat = strips.at[pl.ds(0, 3 * hw), pl.ds(0, tok_ref.shape[2])]
    for c in range(chunks):
        at = pl.ds(c * STEP, STEP)
        pltpu.make_async_copy(g_ref.at[:, :, :, at], gv.at[:, :, :, at], lsem.at[c]).start()
    me_t, me_d = enter(nt, nd, True)
    sends, recvs, after = Sems(ssem), Sems(rsem), []
    orders = [[0] + o[:-1][::-1] for o in bit_orders(bits)]
    jobs = []

    own = pltpu.make_async_copy(dmine_ref.at[me_t], da_ref.at[me_t], lsem.at[chunks])
    own.start()
    swaps = []
    for k in range(1, nt):
        peer = lax.rem(me_t + k, nt)
        copy = pltpu.make_async_remote_copy(
            dmine_ref.at[peer], da_ref.at[me_t], sends.take(), recvs.take(), device_id={"tensor": peer}, device_id_type=MESH
        )
        copy.start()
        swaps.append(copy)

    def swapped():
        own.wait()
        for copy in swaps:
            copy.wait_recv()

    after.extend(copy.wait_send for copy in swaps)

    line, hot = bias_lines(bl_ref, tab_ref)

    def rows_of(i):
        return slice(i * block, (i + 1) * block)

    bias[...] = line

    def piece(h, i):
        mine = rows_of(i)
        seen = (i + 1) * block
        off = (nt - 1 - i) * block
        q = qs[mine, :]
        da = das[mine, :]
        s = dot_nt(q, ks[:seen, :])
        s = s + strip[:, off : off + seen]
        s = jnp.where(column(segr_ref[:, mine]) == segr_ref[:, :seen], s, MASKED)
        at = lax.broadcasted_iota(jnp.int32, (block, lse_ref.shape[1]), 1) == h
        lse = jnp.sum(jnp.where(at, lse_ref[mine, :], 0.0), axis=1, keepdims=True)
        p = jnp.exp(s - lse)
        dp = dot_nt(da, vs[:seen, :])
        ds = p * (dp - jnp.sum(p * dp, axis=1, keepdims=True))
        low = ds.astype(BF)
        dkt[:, :seen] += dot_tn(q, low)
        dvt[:, :seen] += dot_tn(da, p.astype(BF))
        dstrip[:, off : off + seen] += ds
        qs[mine, :] = dot(low, ks[:seen, :]).astype(BF)

    def head(h, carry):
        build_strip(strip, bias[pl.ds(h, 1), :])
        for k in range(heads):

            @pl.when(h == k)
            def _(k=k):
                for i in range(nt):
                    for which, ref in enumerate((qs, ks, vs)):
                        at = which * hw + k * DK
                        ref[rows_of(i), :] = qkv_ref[i, :, at : at + DK]
                    das[rows_of(i), :] = da_ref[i, :, k * DK : (k + 1) * DK]

        dstrip[...] = jnp.zeros_like(dstrip)
        dkt[...] = jnp.zeros_like(dkt)
        dvt[...] = jnp.zeros_like(dvt)
        for i in range(nt):
            piece(h, i)
        for i in range(nt):
            ks[rows_of(i), :] = dkt[:, rows_of(i)].T.astype(BF)
            vs[rows_of(i), :] = dvt[:, rows_of(i)].T.astype(BF)
        for k in range(heads):

            @pl.when(h == k)
            def _(k=k):
                for which, ref in enumerate((qs, ks, vs)):
                    at = which * hw + k * DK
                    dqkv[:, at : at + DK] = ref[...]

        n = block // 2
        while n >= 8:
            dstrip[0:n, :] = dstrip[0:n, :] + pltpu.roll(dstrip[n : 2 * n, :], width - n, 1)
            n //= 2
        x = dstrip[0:8, :]
        row = lax.broadcasted_iota(jnp.int32, x.shape, 0)
        for b in range(3):
            x = jnp.where((row >> b) % 2 == 1, pltpu.roll(x, width - (1 << b), 1), x)
        lines[pl.ds(h, 1), :] = jnp.sum(x, axis=0, keepdims=True)
        return carry

    def rows_end(i):
        mine = rows_of(i)
        x = tok_ref[i].astype(F32)
        hat = x * norm_scale(x)
        more = dot_tn(dqkv[mine, :], (hat * g0_ref[...]).astype(BF))
        gat[...] = more if i == 0 else gat[...] + more
        u = dot_nt(dqkv[mine, :], wa_ref[:, : 3 * hw])
        gain0[...] += jnp.sum(u * hat, axis=0, keepdims=True)
        u_ref[i] = u.astype(BF)

    def finish():
        table = lax.dot_general(
            lines[...],
            hot.astype(F32),
            (((1,), (1,)), ((), ())),
            precision=lax.Precision.HIGHEST,
            preferred_element_type=F32,
        )
        table = jnp.concatenate([table, jnp.zeros((8, 128 - table.shape[1]), F32)], axis=1).astype(BF)
        ga = gat[...].T.astype(BF)
        part = ga.shape[0] // nd
        for d in range(nd):
            a_ref[d, :, : 3 * hw] = ga[d * part : (d + 1) * part]
            a_ref[d, :, 3 * hw :] = jnp.zeros((part, 128), BF)
            a_ref[d, :8, 3 * hw :] = table

    def add_gains():
        at = g_used - (cols - 128)
        row = lax.broadcasted_iota(jnp.int32, (128, gain0.shape[1]), 0)
        gains = jnp.where(row == at, gain0[...], 0.0)
        gains = gains + jnp.where(row == at + 1, gain_in[0:1, :], 0.0) + jnp.where(row == at + 2, gain_in[1:2, :], 0.0)
        gains = gains.T.astype(BF)
        part = gains.shape[0] // nd

        def step(t, carry):
            for d in range(nd):
                gv[t, d, :, cols - 128 :] = gv[t, d, :, cols - 128 :] + gains[d * part : (d + 1) * part]
            return carry

        lax.fori_loop(0, nt, step, 0)

    lines[...] = jnp.zeros_like(lines)
    gain0[...] = jnp.zeros_like(gain0)

    def a_done():
        a_out[...] = a_ref[me_d].astype(F32)

    def chunk_job(c):
        first = c * STEP
        cubes = []
        for n in range(2):
            at = first + n * half
            cubes.append(
                cube_scatter(
                    nd,
                    me_d,
                    orders[n],
                    lambda d, at=at: gv.at[:, d, :, pl.ds(at, half)],
                    [r.at[2 * c + n] for r in grecv],
                    sends,
                    recvs,
                    after,
                )
            )
        z = line_scatter(
            nt,
            me_t,
            lambda b: gv.at[b, me_d, :, pl.ds(first, STEP)],
            gz.at[c],
            g_out.at[:, pl.ds(first, STEP)],
            sends,
            recvs,
            after,
        )

        def begin():
            at = pl.ds(first, STEP)
            pltpu.make_async_copy(g_ref.at[:, :, :, at], gv.at[:, :, :, at], lsem.at[c]).wait()
            if c == chunks - 1:
                add_gains()
            for q in cubes:
                q[0]()

        def both(k):
            def run():
                for q in cubes:
                    q[k]()

            return run

        def meet():
            for q in cubes:
                q[bits]()
            z[0]()

        return [begin] + [both(k) for k in range(1, bits)] + [meet] + z[1:]

    def row_job(ref, recv, out, n):
        at = pl.ds(n * PIECE, PIECE)
        return line_scatter(nt, me_t, lambda b: ref.at[b, at], recv.at[:, at], out.at[at], sends, recvs, after)

    ticks = [SPACE * k for k in range(bits)] + [SPACE * bits + k for k in range(nt)]
    for c in range(chunks):
        jobs.append((min(c, chunks - 1), chunk_job(c), ticks))
    for n in range(e_out.shape[0] // PIECE):
        jobs.append((n, row_job(e_ref, ez, e_out, n), list(range(nt))))
    compute = [(CORE0, swapped), (CORE0, lambda: lax.fori_loop(0, heads, head, 0))]
    ready = CORE0 + 1
    compute += [(ready, partial(rows_end, i)) for i in range(nt)]
    compute.append((ready, finish))
    for tick, fn in compute:
        jobs.append((tick, [fn], [0]))
    a_job = cube_scatter(nd, me_d, orders[0], lambda d: a_ref.at[d], arecv, sends, recvs, after) + [a_done]
    jobs.append((ready + 1, a_job, [SPACE * k for k in range(bits + 1)] + [SPACE * bits]))
    for n in range(u_out.shape[0] // PIECE):
        jobs.append((ready + 1 + n, row_job(u_ref, uz, u_out, n), list(range(nt))))
    run_jobs(jobs, after)


def backward_all(nt, nd, heads, used, g, e, gain12, dmine, tok, wa, g0, segr, bl, tab, qkv, lse):
    bits = nd.bit_length() - 1
    rows, cols = g.shape[2:]
    block, width = tok.shape[1:]
    length = nt * block
    wide = wa.shape[1]
    hw = heads * DK
    chunks = cols // STEP
    lines = chunks + (block + e.shape[1]) // PIECE
    total = lines * 2 * nt + (2 * chunks + 1) * bits + nt - 1
    return pl.pallas_call(
        partial(backward_kernel, nt, nd, heads, used),
        out_shape=(
            jax.ShapeDtypeStruct((rows, cols), F32),
            jax.ShapeDtypeStruct((rows, wide), F32),
            jax.ShapeDtypeStruct((block, width), F32),
            jax.ShapeDtypeStruct(e.shape[1:], F32),
        ),
        in_specs=[ANY] + [VMEM] * 11,
        out_specs=(VMEM,) * 4,
        scratch_shapes=[
            pltpu.VMEM((nt, nd, rows, cols), BF),
            pltpu.VMEM((nt + 1, block, width), BF),
            pltpu.VMEM((nt + 1,) + e.shape[1:], BF),
            pltpu.VMEM((chunks, nt + 1, rows, STEP), BF),
        ]
        + [pltpu.VMEM((1 << (bits - 1 - k), rows, wide), BF) for k in range(bits)]
        + [pltpu.VMEM((2 * chunks, 1 << (bits - 1 - k), nt, rows, STEP // 2), BF) for k in range(bits)]
        + [
            pltpu.VMEM((nd, rows, wide), BF),
            pltpu.VMEM((nt, block, width), BF),
            pltpu.VMEM((nt, block, hw), BF),
            pltpu.VMEM((max(2 * block, 3 * hw), length + block), F32),
            pltpu.VMEM((length, DK), BF),
            pltpu.VMEM((length, DK), BF),
            pltpu.VMEM((length, DK), BF),
            pltpu.VMEM((length, DK), BF),
            pltpu.VMEM((DK, length), F32),
            pltpu.VMEM((DK, length), F32),
            pltpu.VMEM((length, 3 * hw), BF),
            pltpu.VMEM((8, length + block), F32),
            pltpu.VMEM((8, length + block), F32),
            pltpu.VMEM((1, width), F32),
            pltpu.SemaphoreType.DMA((total,)),
            pltpu.SemaphoreType.DMA((total,)),
            pltpu.SemaphoreType.DMA((chunks + 1,)),
        ],
        compiler_params=pltpu.CompilerParams(collective_id=1, has_side_effects=True, vmem_limit_bytes=LIMIT),
        name="backward_all",
    )(g, e, gain12, dmine, tok, wa, g0, segr, bl, tab, qkv, lse)


def column(row):
    return jnp.broadcast_to(row, (8, row.shape[1])).T[:, 0:1]


def build_strip(strip, x):
    block, width = strip.shape
    row = lax.broadcasted_iota(jnp.int32, (8, width), 0)
    x = jnp.broadcast_to(x, (8, width))
    for b in range(3):
        x = jnp.where((row >> b) % 2 == 1, pltpu.roll(x, 1 << b, 1), x)
    strip[0:8, :] = x
    n = 8
    while n < block:
        strip[n : 2 * n, :] = pltpu.roll(strip[0:n, :], n, 1)
        n *= 2


def bias_lines(bl_ref, tab_ref):
    width = bl_ref.shape[1]
    buckets = tab_ref.shape[1]
    hot = bl_ref[...] == lax.broadcasted_iota(jnp.int32, (buckets, width), 0)
    line = dot(tab_ref[...], hot.astype(F32).astype(BF))
    return jnp.where(bl_ref[...] >= 0, line, MASKED), hot


def middle_kernel(
    heads,
    ff,
    tok_ref,
    enc_ref,
    attn_ref,
    og_ref,
    gains_ref,
    w_hbm,
    layer_ref,
    one_ref,
    denc_ref,
    gain_ref,
    dattn_ref,
    g_hbm,
    w,
    g,
    h1_ref,
    h2_ref,
    n1_ref,
    n2_ref,
    acc_ref,
    dn_ref,
    g2_ref,
    denc,
    qc,
    kv,
    ac,
    oc,
    lse,
    dkv,
    insem,
    outsem,
):
    nt = w.shape[0]
    hw = heads * DK
    cols = w.shape[2]
    f0, f1, f2 = 0, ff, 2 * ff
    kv0 = 3 * ff
    q0 = kv0 + 2 * hw
    c0 = q0 + hw
    s0 = c0 + hw
    end = s0 + hw
    ffn = pl.ds(0, 3 * ff)
    att = pl.ds(3 * ff, cols - 3 * ff)
    loads = [pltpu.make_async_copy(w_hbm.at[t, :, att], w.at[t, :, att], insem.at[0, t]) for t in range(nt)]
    loads += [pltpu.make_async_copy(w_hbm.at[t, :, ffn], w.at[t, :, ffn], insem.at[1, t]) for t in range(nt)]
    for copy in loads:
        copy.start()

    def load_wait(which, t):
        at = att if which == 0 else ffn
        pltpu.make_async_copy(w_hbm.at[t, :, at], w.at[t, :, at], insem.at[which, t]).wait()

    def store(which, t):
        at = att if which == 0 else ffn
        return pltpu.make_async_copy(g.at[t, :, at], g_hbm.at[t, :, at], outsem.at[which, t])

    acc_ref[...] = tok_ref[...].astype(F32)

    def self_out(t, carry):
        load_wait(0, t)
        acc_ref[...] += dot_nt(attn_ref[t], w[t, :, s0:end])
        return carry

    lax.fori_loop(0, nt, self_out, 0)
    h1 = acc_ref[...]
    h1_ref[...] = h1
    n1_ref[...] = (h1 * norm_scale(h1) * gains_ref[1:2, :]).astype(BF)

    def cross(t, carry):
        q = dot(n1_ref[...], w[t, :, q0:c0]).astype(BF)
        both = dot(enc_ref[...], w[t, :, kv0:q0]).astype(BF)
        qc[t] = q
        kv[t] = both
        outs = []
        for h in range(heads):
            part = slice(h * DK, (h + 1) * DK)
            s = dot_nt(q[:, part], both[:, part])
            top = jnp.max(s, axis=-1, keepdims=True)
            p = jnp.exp(s - top)
            total = jnp.sum(p, axis=-1, keepdims=True)
            lse[t, h] = top + jnp.log(total)
            outs.append(dot(p.astype(BF), both[:, hw + h * DK : hw + (h + 1) * DK]) / total)
        a = jnp.concatenate(outs, axis=1).astype(BF)
        ac[t] = a
        acc_ref[...] += dot_nt(a, w[t, :, c0:s0])
        return carry

    lax.fori_loop(0, nt, cross, 0)
    h2 = acc_ref[...]
    h2_ref[...] = h2
    n2_ref[...] = (h2 * norm_scale(h2) * gains_ref[2:3, :]).astype(BF)
    dn_ref[...] = jnp.zeros_like(dn_ref)

    def units(t, carry):
        load_wait(1, t)
        n2 = n2_ref[...]
        og = og_ref[...]
        gate = dot(n2, w[t, :, f0:f1])
        up = dot(n2, w[t, :, f1:f2])
        dinner = dot(og, w[t, :, f2 : 3 * ff])
        sq = gate * gate
        th = jnp.tanh(0.7978845608028654 * (gate + 0.044715 * (gate * sq)))
        cdf = 0.5 * (1.0 + th)
        act = gate * cdf
        slope = cdf + gate * (0.5 * (1.0 - th * th)) * (0.7978845608028654 * (1.0 + 0.134145 * sq))
        inner = (act * up).astype(BF)
        dgate = (dinner * up * slope).astype(BF)
        dup = (dinner * act).astype(BF)
        acc_ref[...] += dot_nt(inner, w[t, :, f2 : 3 * ff])
        dn_ref[...] += dot_nt(dgate, w[t, :, f0:f1]) + dot_nt(dup, w[t, :, f1:f2])
        g[t, :, f0:f1] = dot_tn(n2, dgate).astype(BF)
        g[t, :, f1:f2] = dot_tn(n2, dup).astype(BF)
        g[t, :, f2 : 3 * ff] = dot_tn(og, inner).astype(BF)
        store(1, t).start()
        return carry

    lax.fori_loop(0, nt, units, 0)
    layer_ref[...] = acc_ref[...].astype(BF)
    h2 = h2_ref[...]
    back, gain2 = norm_back(h2, norm_scale(h2), gains_ref[2:3, :], dn_ref[...])
    g2 = og_ref[...].astype(F32) + back
    acc_ref[...] = g2
    g2_ref[...] = g2.astype(BF)
    dn_ref[...] = jnp.zeros_like(dn_ref)
    denc[...] = jnp.zeros_like(denc)

    def cross_back(t, carry):
        g2 = g2_ref[...]
        a = ac[t]
        da = dot(g2, w[t, :, c0:s0]).astype(BF)
        g[t, :, c0:s0] = dot_tn(g2, a).astype(BF)
        prod = da.astype(F32) * a.astype(F32)
        q = qc[t]
        both = kv[t]
        dqs = []
        for h in range(heads):
            part = slice(h * DK, (h + 1) * DK)
            qh, kh = q[:, part], both[:, part]
            vh, dah = both[:, hw + h * DK : hw + (h + 1) * DK], da[:, part]
            p = jnp.exp(dot_nt(qh, kh) - lse[t, h])
            delta = jnp.sum(prod[:, part], axis=1, keepdims=True)
            ds = (p * (dot_nt(dah, vh) - delta)).astype(BF)
            dqs.append(dot(ds, kh))
            dkv[h * DK : (h + 1) * DK, :] = dot_tn(qh, ds)
            dkv[hw + h * DK : hw + (h + 1) * DK, :] = dot_tn(dah, p.astype(BF))
        dq = jnp.concatenate(dqs, axis=1).astype(BF)
        dboth = dkv[...].astype(BF)
        g[t, :, q0:c0] = dot_tn(n1_ref[...], dq).astype(BF)
        g[t, :, kv0:q0] = lax.dot_general(
            enc_ref[...], dboth, (((0,), (1,)), ((), ())), preferred_element_type=F32
        ).astype(BF)
        dn_ref[...] += dot_nt(dq, w[t, :, q0:c0])
        denc[...] += lax.dot_general(
            dboth, w[t, :, kv0:q0], (((0,), (1,)), ((), ())), preferred_element_type=F32
        )
        return carry

    lax.fori_loop(0, nt, cross_back, 0)
    denc_ref[...] = denc[...].astype(BF)
    h1 = h1_ref[...]
    back, gain1 = norm_back(h1, norm_scale(h1), gains_ref[1:2, :], dn_ref[...])
    g1 = acc_ref[...] + back
    one_ref[...] = g1
    g2_ref[...] = g1.astype(BF)
    gain_ref[...] = jnp.concatenate([gain1, gain2, jnp.zeros((6, gain1.shape[1]), F32)], axis=0)

    def self_out_back(t, carry):
        low = g2_ref[...]
        dattn_ref[t] = dot(low, w[t, :, s0:end]).astype(BF)
        tail = dot_tn(low, attn_ref[t])
        g[t, :, s0:cols] = jnp.concatenate([tail, jnp.zeros((tail.shape[0], cols - end), F32)], axis=1).astype(BF)
        store(0, t).start()
        return carry

    lax.fori_loop(0, nt, self_out_back, 0)
    for t in range(nt):
        store(1, t).wait()
        store(0, t).wait()


def middle(heads, ff, tok, enc, attn, og, gains, w):
    nt, _, cols = w.shape
    rows, width = tok.shape
    states = enc.shape[0]
    hw = heads * DK
    return pl.pallas_call(
        partial(middle_kernel, heads, ff),
        out_shape=(
            jax.ShapeDtypeStruct((rows, width), BF),
            jax.ShapeDtypeStruct((rows, width), F32),
            jax.ShapeDtypeStruct((states, width), BF),
            jax.ShapeDtypeStruct((8, width), F32),
            jax.ShapeDtypeStruct((nt, rows, hw), BF),
            jax.ShapeDtypeStruct(w.shape, BF),
        ),
        in_specs=[VMEM] * 5 + [ANY],
        out_specs=(VMEM,) * 5 + (ANY,),
        scratch_shapes=[
            pltpu.VMEM(w.shape, BF),
            pltpu.VMEM(w.shape, BF),
            pltpu.VMEM((rows, width), F32),
            pltpu.VMEM((rows, width), F32),
            pltpu.VMEM((rows, width), BF),
            pltpu.VMEM((rows, width), BF),
            pltpu.VMEM((rows, width), F32),
            pltpu.VMEM((rows, width), F32),
            pltpu.VMEM((rows, width), BF),
            pltpu.VMEM((states, width), F32),
            pltpu.VMEM((nt, rows, hw), BF),
            pltpu.VMEM((nt, states, 2 * hw), BF),
            pltpu.VMEM((nt, rows, hw), BF),
            pltpu.VMEM((8, 128), F32),
            pltpu.VMEM((nt, heads, rows, 1), F32),
            pltpu.VMEM((2 * hw, states), F32),
            pltpu.SemaphoreType.DMA((2, nt)),
            pltpu.SemaphoreType.DMA((2, nt)),
        ],
        compiler_params=pltpu.CompilerParams(vmem_limit_bytes=LIMIT),
        name="middle",
    )(tok, enc, attn, og, gains, w)


def per_device(
    tokens,
    encoder,
    segments,
    rel_bucket,
    out_grad,
    self_q,
    self_k,
    self_v,
    self_o,
    cross_q,
    cross_k,
    cross_v,
    cross_o,
    ffn_gate,
    ffn_up,
    ffn_down,
    bias_table,
    norm_gains,
):
    nt, nd = lax.axis_size("tensor"), lax.axis_size("dp")
    part, hw = self_q.shape
    ff = ffn_gate.shape[1]
    heads = hw // DK
    rows, width = tokens.shape
    length = rows * nt
    buckets = bias_table.shape[0]
    wa = jnp.concatenate([self_q, self_k, self_v, jnp.pad(norm_gains.T, ((0, 0), (0, 128 - norm_gains.shape[0])))], axis=1)
    wb = jnp.concatenate([ffn_gate, ffn_up, ffn_down.T, cross_k, cross_v, cross_q, cross_o.T, self_o.T], axis=1)
    used = wb.shape[1]
    cols = -(-(used + 3) // STEP) * STEP
    wb = jnp.pad(wb, ((0, 0), (0, cols - used)))
    top = (nt - 1) * rows
    blank = jnp.full((length - 1 - top,), -1, jnp.int32)
    bl = jnp.concatenate(
        [rel_bucket[: top + 1][::-1], blank, jnp.full((1,), -1, jnp.int32), rel_bucket[top + 1 : length][::-1]]
    )[None, :]
    tab = jnp.pad(bias_table.T, ((0, 8 - heads), (0, 0)))
    segr = segments
    tok_all, enc_all, wb_all, wa_full, gains, qkv, lse, attn, mine = forward_all(
        nt, nd, heads, tokens, encoder, wa, wb, segr, bl, tab
    )
    wb_full = wb_all.reshape(nt, nd * part, cols)
    g0 = gains[0:1]
    layer_out, grad_one, denc, gain12, dmine, gb = middle(
        heads, ff, tokens, enc_all.reshape(nt * encoder.shape[0], width), mine, out_grad, gains, wb_full
    )
    gsum, asum, usum, esum = backward_all(
        nt,
        nd,
        heads,
        used,
        gb.reshape(nt, nd, part, cols),
        denc.reshape((nt,) + encoder.shape),
        gain12,
        dmine,
        tok_all,
        wa_full,
        g0,
        segr,
        bl,
        tab,
        qkv,
        lse,
    )
    x = tokens.astype(F32)
    back, _ = norm_back(x, norm_scale(x), g0, usum)
    tokens_grad = grad_one + back
    at = 3 * ff
    ck, cv, cq, co, so = (gsum[:, at + n * hw : at + (n + 1) * hw] for n in range(5))
    return (
        layer_out,
        tokens_grad,
        esum,
        asum[:, :hw],
        asum[:, hw : 2 * hw],
        asum[:, 2 * hw : 3 * hw],
        so.T,
        cq,
        ck,
        cv,
        co.T,
        gsum[:, :ff],
        gsum[:, ff : 2 * ff],
        gsum[:, 2 * ff : 3 * ff].T,
        asum[:heads, 3 * hw : 3 * hw + buckets].T,
        gsum[:, used : used + 3].T,
    )


def solution(mesh):
    rows = P(("dp", "tensor"), None)
    left = P("dp", "tensor")
    right = P("tensor", "dp")
    return jax.shard_map(
        per_device,
        mesh=mesh,
        in_specs=(rows, rows, P("dp", None), P(), rows, left, left, left, right, left, left, left, right, left, left, right)
        + (P(None, "tensor"), P(None, "dp")),
        out_specs=(rows, rows, rows, left, left, left, right, left, left, left, right, left, left, right)
        + (P(None, "tensor"), P(None, "dp")),
        check_vma=False,
    )
```

```python
from functools import partial

import jax
import jax.numpy as jnp
from jax import lax
from jax.experimental import pallas as pl
from jax.experimental.pallas import tpu as pltpu
from jax.sharding import PartitionSpec as P

DK = 64
EPS = 1e-06
MASKED = -1e30
BF = jnp.bfloat16
F32 = jnp.float32
MESH = pl.DeviceIdType.MESH
VMEM = pl.BlockSpec(memory_space=pltpu.VMEM)
ANY = pl.BlockSpec(memory_space=pl.ANY)
LIMIT = 510 * 128 * 1024
STEP = 256
SPACE = 2
PIECE = 32
TOK0 = 2
TOKR = 1
CORE0 = 3
CORE1 = 13


def dot(a, b):
    return jnp.dot(a, b, preferred_element_type=F32)


def dot_nt(a, b):
    return lax.dot_general(a, b, (((1,), (1,)), ((), ())), preferred_element_type=F32)


def dot_tn(a, b):
    return lax.dot_general(a, b, (((0,), (0,)), ((), ())), preferred_element_type=F32)


def norm_scale(x):
    return lax.rsqrt(jnp.mean(x * x, axis=-1, keepdims=True) + EPS)


def norm_back(x, r, g, u):
    w = u * g
    inner = jnp.mean(w * x, axis=-1, keepdims=True)
    return r * w - x * (r * r * r * inner), jnp.sum(u * (x * r), axis=0, keepdims=True)


def flip(index, bit):
    size = 1 << bit
    return index + size - 2 * size * lax.rem(index // size, 2)


def flip_all(index, mask):
    bit = 0
    while mask:
        if mask & 1:
            index = flip(index, bit)
        mask >>= 1
        bit += 1
    return index


def subsets(bits):
    out = [0]
    for b in bits:
        out = out + [m | (1 << b) for m in out]
    return out


def bit_orders(count):
    upper = list(range(1, count))
    return [upper + [0], upper[::-1] + [0]]


class Sems:
    def __init__(self, ref):
        self.ref = ref
        self.used = 0

    def take(self):
        self.used += 1
        return self.ref.at[self.used - 1]

    def many(self, count):
        base = self.used
        self.used += count
        return lambda n: self.ref.at[base + n]


def wait_bytes(ref, sem):
    pltpu.make_async_copy(ref, ref, sem).wait()


def row_loop(shape, body):
    size = 32 if shape[1] <= 256 else 16
    if shape[0] % size:
        body(slice(0, shape[0]))
        return

    def step(n, carry):
        body(pl.ds(pl.multiple_of(n * size, size), size))
        return carry

    lax.fori_loop(0, shape[0] // size, step, 0)


def add_into(ref, got):
    if len(ref.shape) == 2:

        def body(at):
            ref[at, :] = ref[at, :] + got[at, :]

        row_loop(ref.shape, body)
    else:

        def step(t, carry):
            ref[t] = ref[t] + got[t]
            return carry

        lax.fori_loop(0, ref.shape[0], step, 0)


def enter(nt, nd, all_tensor=False):
    me_t, me_d = lax.axis_index("tensor"), lax.axis_index("dp")
    bar = pltpu.get_barrier_semaphore()
    bits = nd.bit_length() - 1
    for b in range(bits):
        pl.semaphore_signal(bar, 1, device_id={"dp": flip(me_d, b)}, device_id_type=MESH)
    if all_tensor:
        for k in range(1, nt):
            pl.semaphore_signal(bar, 1, device_id={"tensor": lax.rem(me_t + k, nt)}, device_id_type=MESH)
        pl.semaphore_wait(bar, bits + nt - 1)
        return me_t, me_d

    @pl.when(me_t > 0)
    def _():
        pl.semaphore_signal(bar, 1, device_id={"tensor": me_t - 1}, device_id_type=MESH)

    @pl.when(me_t < nt - 1)
    def _():
        pl.semaphore_signal(bar, 1, device_id={"tensor": me_t + 1}, device_id_type=MESH)

    pl.semaphore_wait(bar, bits + (me_t + nt - 1) // nt + (2 * nt - 2 - me_t) // nt)
    return me_t, me_d


def run_jobs(jobs, after):
    events = []
    for number, (start, stages, ticks) in enumerate(jobs):
        for tick, stage in zip(ticks, stages, strict=True):
            events.append((start + tick, start, number, stage))
    for event in sorted(events, key=lambda e: e[:3]):
        event[3]()
    for fn in after:
        fn()


def line_gather(nt, me, own, slot, sends, recvs, after):
    sem = {(s, j): (sends.take(), recvs.take()) for s in (1, -1) for j in range(1, nt)}

    def send(side, j):
        block = me - side * (j - 1)
        target = me + side
        ok = (block >= 0) & (block < nt) & (target >= 0) & (target < nt)
        src = own if j == 1 else slot(jnp.clip(block, 0, nt - 1))
        dst = slot(jnp.clip(block, 0, nt - 1))
        ss, rs = sem[side, j]

        @pl.when(ok)
        def _():
            pltpu.make_async_remote_copy(
                src, dst, ss, rs, device_id={"tensor": target}, device_id_type=MESH
            ).start()

        def done():
            @pl.when(ok)
            def _():
                wait_bytes(own, ss)

        after.append(done)

    def arrive(side, j):
        block = me - side * j

        @pl.when((block >= 0) & (block < nt))
        def _():
            wait_bytes(own, sem[side, j][1])

    def stage(j):
        def run():
            for side in (1, -1):
                if j > 0:
                    arrive(side, j)
                if j < nt - 1:
                    send(side, j + 1)

        return run

    return [stage(j) for j in range(nt)]


def cube_gather(nd, me, order, own, slot, slots, sends, recvs, after):
    count = len(order)
    sem = [(sends.take(), recvs.take()) for _ in range(count)]

    def start(k):
        bit = order[k]
        for m in subsets(order[:k]):
            block = flip_all(me, m)
            src = own if (m == 0 and own is not None) else slot(block)
            pltpu.make_async_remote_copy(
                src, slot(block), sem[k][0], sem[k][1], device_id={"dp": flip(me, bit)}, device_id_type=MESH
            ).start()

        def done():
            wait_bytes(slots(1 << k), sem[k][0])

        after.append(done)

    def stage(k):
        def run():
            if k > 0:
                wait_bytes(slots(1 << (k - 1)), sem[k - 1][1])
            if k < count:
                start(k)

        return run

    return [stage(k) for k in range(count + 1)]


def forward_kernel(
    nt,
    nd,
    heads,
    tok_ref,
    enc_ref,
    wa_ref,
    wb_ref,
    segr_ref,
    bl_ref,
    tab_ref,
    tok_out,
    enc_out,
    wb_out,
    wa_full,
    gain_ref,
    qkv_ref,
    lse_ref,
    attn_ref,
    mine_ref,
    wa_out,
    strip,
    bias,
    qs,
    ks,
    vs,
    os,
    lses,
    ssem,
    rsem,
    lsem,
):
    me_t, me_d = enter(nt, nd, True)
    bits = nd.bit_length() - 1
    sends, recvs, after = Sems(ssem), Sems(rsem), []
    locals_ = [
        (tok_ref, tok_out.at[me_t]),
        (enc_ref, enc_out.at[me_t]),
        (wa_ref, wa_out.at[me_d]),
        (wb_ref, wb_out.at[me_t, me_d]),
    ]
    for n, (src, dst) in enumerate(locals_):
        pltpu.make_async_copy(src, dst, lsem.at[n]).start()
    orders = bit_orders(bits)
    cols = wb_ref.shape[1]
    chunks = cols // STEP
    half = STEP // 2
    jobs = []
    jobs.append(
        (
            0,
            cube_gather(nd, me_d, orders[0], wa_ref, lambda d: wa_out.at[d], lambda n: wa_out.at[pl.ds(0, n)], sends, recvs, after),
            [SPACE * k for k in range(bits + 1)],
        )
    )

    def chunk_job(c):
        first = c * STEP
        z = line_gather(
            nt,
            me_t,
            wb_ref.at[:, pl.ds(first, STEP)],
            lambda t: wb_out.at[t, me_d, :, pl.ds(first, STEP)],
            sends,
            recvs,
            after,
        )
        cubes = []
        for n in range(2):
            at = first + n * half
            cubes.append(
                cube_gather(
                    nd,
                    me_d,
                    orders[n],
                    None,
                    lambda d, at=at: wb_out.at[:, d, :, pl.ds(at, half)],
                    lambda k, at=at: wb_out.at[:, pl.ds(0, k), :, pl.ds(at, half)],
                    sends,
                    recvs,
                    after,
                )
            )

        def meet():
            z[-1]()
            for q in cubes:
                q[0]()

        def both(k):
            def run():
                for q in cubes:
                    q[k]()

            return run

        return z[:-1] + [meet] + [both(k) for k in range(1, bits + 1)]


    def row_job(ref, out, n):
        at = pl.ds(n * PIECE, PIECE)
        return line_gather(nt, me_t, ref.at[at], lambda t: out.at[t, at], sends, recvs, after)

    ticks = list(range(nt)) + [nt - 1 + SPACE * k for k in range(1, bits + 1)]
    for c in range(chunks):
        jobs.append((c, chunk_job(c), ticks))
    number = TOK0
    for ref, out in ((tok_ref, tok_out), (enc_ref, enc_out)):
        for n in range(ref.shape[0] // PIECE):
            jobs.append((number // TOKR, row_job(ref, out, n), list(range(nt))))
            number += 1
    pltpu.make_async_copy(wb_ref, wb_out.at[me_t, me_d], lsem.at[3]).wait()
    after.append(lambda: pltpu.make_async_copy(enc_ref, enc_out.at[me_t], lsem.at[1]).wait())

    block = tok_ref.shape[0]
    part = wa_ref.shape[0]
    hw = heads * DK
    bias[...] = bias_lines(bl_ref, tab_ref)[0]

    def rows_of(i):
        return slice(i * block, (i + 1) * block)

    def weights():
        for n in (0, 2):
            src, dst = locals_[n]
            pltpu.make_async_copy(src, dst, lsem.at[n]).wait()
        for d in range(nd):
            wa_full[d * part : (d + 1) * part, :] = wa_out[d]
        gain_ref[...] = wa_full[:, 3 * hw :].astype(F32).T[0:8]

    def rows_start(i):
        x = tok_out[i].astype(F32)
        n = (x * norm_scale(x) * gain_ref[0:1, :]).astype(BF)
        y = dot(n, wa_full[:, : 3 * hw]).astype(BF)
        qkv_ref[i] = y
        for h in range(heads):
            for which, ref in enumerate((qs, ks, vs)):
                at = which * hw + h * DK
                ref[h, rows_of(i), :] = y[:, at : at + DK]

    def head(h, carry):
        build_strip(strip, bias[pl.ds(h, 1), :])
        for i in range(nt):
            piece(h, i)
        return carry

    def piece(h, i):
        mine = rows_of(i)
        seen = (i + 1) * block
        off = (nt - 1 - i) * block
        s = dot_nt(qs[h, mine, :], ks[h, :seen, :])
        s = s + strip[:, off : off + seen]
        s = jnp.where(column(segr_ref[:, mine]) == segr_ref[:, :seen], s, MASKED)
        top = jnp.max(s, axis=-1, keepdims=True)
        p = jnp.exp(s - top)
        total = jnp.sum(p, axis=-1, keepdims=True)
        os[h, mine, :] = (dot(p.astype(BF), vs[h, :seen, :]) / total).astype(BF)
        lses[h, mine, :] = top + jnp.log(total)

    def collect():
        for i in range(nt):
            for h in range(heads):
                attn_ref[i, :, h * DK : (h + 1) * DK] = os[h, rows_of(i), :]
                lse_ref[rows_of(i), h : h + 1] = lses[h, rows_of(i), :]

    own = pltpu.make_async_copy(attn_ref.at[me_t], mine_ref.at[me_t], lsem.at[4])
    swaps = []
    for k in range(1, nt):
        peer = lax.rem(me_t + k, nt)
        swaps.append(
            pltpu.make_async_remote_copy(
                attn_ref.at[peer],
                mine_ref.at[me_t],
                sends.take(),
                recvs.take(),
                device_id={"tensor": peer},
                device_id_type=MESH,
            )
        )

    def swap():
        for copy in swaps + [own]:
            copy.start()

    after.extend(copy.wait for copy in swaps + [own])
    compute = [(CORE1, weights)] + [(CORE1, partial(rows_start, i)) for i in range(nt)]
    compute.append((CORE1 + 1, lambda: lax.fori_loop(0, heads, head, 0)))
    compute += [(CORE1 + 1, collect), (CORE1 + 1, swap)]
    for tick, fn in compute:
        jobs.append((tick, [fn], [0]))
    run_jobs(jobs, after)


def forward_all(nt, nd, heads, tok, enc, wa, wb, segr, bl, tab):
    bits = nd.bit_length() - 1
    chunks = wb.shape[1] // STEP
    lines = chunks + (tok.shape[0] + enc.shape[0]) // PIECE
    total = lines * 2 * (nt - 1) + (2 * chunks + 1) * bits + nt - 1
    block, width = tok.shape
    length = nt * block
    hw = heads * DK
    return pl.pallas_call(
        partial(forward_kernel, nt, nd, heads),
        out_shape=(
            jax.ShapeDtypeStruct((nt,) + tok.shape, BF),
            jax.ShapeDtypeStruct((nt,) + enc.shape, BF),
            jax.ShapeDtypeStruct((nt, nd) + wb.shape, BF),
            jax.ShapeDtypeStruct((width, wa.shape[1]), BF),
            jax.ShapeDtypeStruct((8, width), F32),
            jax.ShapeDtypeStruct((nt, block, 3 * hw), BF),
            jax.ShapeDtypeStruct((length, 8), F32),
            jax.ShapeDtypeStruct((nt, block, hw), BF),
            jax.ShapeDtypeStruct((nt, block, hw), BF),
        ),
        in_specs=[VMEM] * 7,
        out_specs=(VMEM, ANY, ANY) + (VMEM,) * 6,
        scratch_shapes=[
            pltpu.VMEM((nd,) + wa.shape, BF),
            pltpu.VMEM((block, length + block), F32),
            pltpu.VMEM((8, length + block), F32),
        ]
        + [pltpu.VMEM((heads, length, DK), BF)] * 4
        + [
            pltpu.VMEM((heads, length, 1), F32),
            pltpu.SemaphoreType.DMA((total,)),
            pltpu.SemaphoreType.DMA((total,)),
            pltpu.SemaphoreType.DMA((5,)),
        ],
        compiler_params=pltpu.CompilerParams(collective_id=0, has_side_effects=True, vmem_limit_bytes=LIMIT),
        name="forward_all",
    )(tok, enc, wa, wb, segr, bl, tab)


def cube_scatter(nd, me, order, value, recv, sends, recvs, after):
    count = len(order)
    sem = [(sends.take(), recvs.take()) for _ in range(count)]

    def start(k):
        bit = order[k]
        peer = flip(me, bit)
        for j, m in enumerate(subsets(order[k + 1 :])):
            pltpu.make_async_remote_copy(
                value(flip_all(peer, m)),
                recv[k].at[j],
                sem[k][0],
                sem[k][1],
                device_id={"dp": peer},
                device_id_type=MESH,
            ).start()

        def done():
            wait_bytes(recv[k], sem[k][0])

        after.append(done)

    def land(k):
        wait_bytes(recv[k], sem[k][1])
        for j, m in enumerate(subsets(order[k + 1 :])):
            add_into(value(flip_all(me, m)), recv[k].at[j])

    def stage(k):
        def run():
            if k > 0:
                land(k - 1)
            if k < count:
                start(k)

        return run

    return [stage(k) for k in range(count + 1)]


def line_scatter(nt, me, value, recv, out, sends, recvs, after):
    ssem, rsem = sends.many(2 * nt), recvs.many(2 * nt)

    def land(side, b):
        return recv.at[b + 1 - side]

    def hop(z):
        def run():
            for side, here in ((0, z), (1, nt - 1 - z)):
                goal = here + 1 if side == 0 else here - 1
                blocks = range(here + 1, nt) if side == 0 else range(here - 1, -1, -1)

                @pl.when(me == here)
                def _(side=side, goal=goal, blocks=blocks):
                    for b in blocks:
                        ref = value(b)
                        if z > 0:
                            got = land(side, b)
                            wait_bytes(got, rsem(side * nt + b))
                            add_into(ref, got)
                        pltpu.make_async_remote_copy(
                            ref,
                            land(side, b),
                            ssem(side * nt + b),
                            rsem(side * nt + b),
                            device_id={"tensor": goal},
                            device_id_type=MESH,
                        ).start()

        return run

    def last():
        own = value(me)

        def first(at):
            out[at, :] = own[at, :].astype(F32)

        row_loop(out.shape, first)
        for side, some in ((0, me > 0), (1, me < nt - 1)):

            @pl.when(some)
            def _(side=side):
                got = land(side, me)
                wait_bytes(got, rsem(side * nt + me))

                def more(at):
                    out[at, :] = out[at, :] + got[at, :].astype(F32)

                row_loop(out.shape, more)

    def done():
        for here in range(nt):

            @pl.when(me == here)
            def _(here=here):
                for b in range(here + 1, nt):
                    wait_bytes(land(0, b), ssem(b))
                for b in range(here):
                    wait_bytes(land(1, b), ssem(nt + b))

    after.append(done)
    return [hop(z) for z in range(nt - 1)] + [last]


def backward_kernel(
    nt,
    nd,
    heads,
    g_used,
    g_ref,
    e_ref,
    gain_in,
    dmine_ref,
    tok_ref,
    wa_ref,
    g0_ref,
    segr_ref,
    bl_ref,
    tab_ref,
    qkv_ref,
    lse_ref,
    g_out,
    a_out,
    u_out,
    e_out,
    *scratch,
):
    bits = nd.bit_length() - 1
    gv, uz, ez, gz = scratch[:4]
    arecv = scratch[4 : 4 + bits]
    grecv = scratch[4 + bits : 4 + 2 * bits]
    a_ref, u_ref, da_ref, strips, qs, ks, vs, das, dkt, dvt, dqkv, lines, bias, gain0 = scratch[4 + 2 * bits : 18 + 2 * bits]
    ssem, rsem, lsem = scratch[18 + 2 * bits :]
    cols = g_ref.shape[3]
    chunks = cols // STEP
    half = STEP // 2
    block = tok_ref.shape[1]
    hw = heads * DK
    width = strips.shape[1]
    strip, dstrip = strips.at[pl.ds(0, block)], strips.at[pl.ds(block, block)]
    gat = strips.at[pl.ds(0, 3 * hw), pl.ds(0, tok_ref.shape[2])]
    for c in range(chunks):
        at = pl.ds(c * STEP, STEP)
        pltpu.make_async_copy(g_ref.at[:, :, :, at], gv.at[:, :, :, at], lsem.at[c]).start()
    me_t, me_d = enter(nt, nd, True)
    sends, recvs, after = Sems(ssem), Sems(rsem), []
    orders = [[0] + o[:-1][::-1] for o in bit_orders(bits)]
    jobs = []

    own = pltpu.make_async_copy(dmine_ref.at[me_t], da_ref.at[me_t], lsem.at[chunks])
    own.start()
    swaps = []
    for k in range(1, nt):
        peer = lax.rem(me_t + k, nt)
        copy = pltpu.make_async_remote_copy(
            dmine_ref.at[peer], da_ref.at[me_t], sends.take(), recvs.take(), device_id={"tensor": peer}, device_id_type=MESH
        )
        copy.start()
        swaps.append(copy)

    def swapped():
        own.wait()
        for copy in swaps:
            copy.wait_recv()

    after.extend(copy.wait_send for copy in swaps)

    line, hot = bias_lines(bl_ref, tab_ref)

    def rows_of(i):
        return slice(i * block, (i + 1) * block)

    bias[...] = line

    def piece(h, i):
        mine = rows_of(i)
        seen = (i + 1) * block
        off = (nt - 1 - i) * block
        q = qs[mine, :]
        da = das[mine, :]
        s = dot_nt(q, ks[:seen, :])
        s = s + strip[:, off : off + seen]
        s = jnp.where(column(segr_ref[:, mine]) == segr_ref[:, :seen], s, MASKED)
        at = lax.broadcasted_iota(jnp.int32, (block, lse_ref.shape[1]), 1) == h
        lse = jnp.sum(jnp.where(at, lse_ref[mine, :], 0.0), axis=1, keepdims=True)
        p = jnp.exp(s - lse)
        dp = dot_nt(da, vs[:seen, :])
        ds = p * (dp - jnp.sum(p * dp, axis=1, keepdims=True))
        low = ds.astype(BF)
        dkt[:, :seen] += dot_tn(q, low)
        dvt[:, :seen] += dot_tn(da, p.astype(BF))
        dstrip[:, off : off + seen] += ds
        qs[mine, :] = dot(low, ks[:seen, :]).astype(BF)

    def head(h, carry):
        build_strip(strip, bias[pl.ds(h, 1), :])
        for k in range(heads):

            @pl.when(h == k)
            def _(k=k):
                for i in range(nt):
                    for which, ref in enumerate((qs, ks, vs)):
                        at = which * hw + k * DK
                        ref[rows_of(i), :] = qkv_ref[i, :, at : at + DK]
                    das[rows_of(i), :] = da_ref[i, :, k * DK : (k + 1) * DK]

        dstrip[...] = jnp.zeros_like(dstrip)
        dkt[...] = jnp.zeros_like(dkt)
        dvt[...] = jnp.zeros_like(dvt)
        for i in range(nt):
            piece(h, i)
        for i in range(nt):
            ks[rows_of(i), :] = dkt[:, rows_of(i)].T.astype(BF)
            vs[rows_of(i), :] = dvt[:, rows_of(i)].T.astype(BF)
        for k in range(heads):

            @pl.when(h == k)
            def _(k=k):
                for which, ref in enumerate((qs, ks, vs)):
                    at = which * hw + k * DK
                    dqkv[:, at : at + DK] = ref[...]

        n = block // 2
        while n >= 8:
            dstrip[0:n, :] = dstrip[0:n, :] + pltpu.roll(dstrip[n : 2 * n, :], width - n, 1)
            n //= 2
        x = dstrip[0:8, :]
        row = lax.broadcasted_iota(jnp.int32, x.shape, 0)
        for b in range(3):
            x = jnp.where((row >> b) % 2 == 1, pltpu.roll(x, width - (1 << b), 1), x)
        lines[pl.ds(h, 1), :] = jnp.sum(x, axis=0, keepdims=True)
        return carry

    def rows_end(i):
        mine = rows_of(i)
        x = tok_ref[i].astype(F32)
        hat = x * norm_scale(x)
        more = dot_tn(dqkv[mine, :], (hat * g0_ref[...]).astype(BF))
        gat[...] = more if i == 0 else gat[...] + more
        u = dot_nt(dqkv[mine, :], wa_ref[:, : 3 * hw])
        gain0[...] += jnp.sum(u * hat, axis=0, keepdims=True)
        u_ref[i] = u.astype(BF)

    def finish():
        table = lax.dot_general(
            lines[...],
            hot.astype(F32),
            (((1,), (1,)), ((), ())),
            precision=lax.Precision.HIGHEST,
            preferred_element_type=F32,
        )
        table = jnp.concatenate([table, jnp.zeros((8, 128 - table.shape[1]), F32)], axis=1).astype(BF)
        ga = gat[...].T.astype(BF)
        part = ga.shape[0] // nd
        for d in range(nd):
            a_ref[d, :, : 3 * hw] = ga[d * part : (d + 1) * part]
            a_ref[d, :, 3 * hw :] = jnp.zeros((part, 128), BF)
            a_ref[d, :8, 3 * hw :] = table

    def add_gains():
        at = g_used - (cols - 128)
        row = lax.broadcasted_iota(jnp.int32, (128, gain0.shape[1]), 0)
        gains = jnp.where(row == at, gain0[...], 0.0)
        gains = gains + jnp.where(row == at + 1, gain_in[0:1, :], 0.0) + jnp.where(row == at + 2, gain_in[1:2, :], 0.0)
        gains = gains.T.astype(BF)
        part = gains.shape[0] // nd

        def step(t, carry):
            for d in range(nd):
                gv[t, d, :, cols - 128 :] = gv[t, d, :, cols - 128 :] + gains[d * part : (d + 1) * part]
            return carry

        lax.fori_loop(0, nt, step, 0)

    lines[...] = jnp.zeros_like(lines)
    gain0[...] = jnp.zeros_like(gain0)

    def a_done():
        a_out[...] = a_ref[me_d].astype(F32)

    def chunk_job(c):
        first = c * STEP
        cubes = []
        for n in range(2):
            at = first + n * half
            cubes.append(
                cube_scatter(
                    nd,
                    me_d,
                    orders[n],
                    lambda d, at=at: gv.at[:, d, :, pl.ds(at, half)],
                    [r.at[2 * c + n] for r in grecv],
                    sends,
                    recvs,
                    after,
                )
            )
        z = line_scatter(
            nt,
            me_t,
            lambda b: gv.at[b, me_d, :, pl.ds(first, STEP)],
            gz.at[c],
            g_out.at[:, pl.ds(first, STEP)],
            sends,
            recvs,
            after,
        )

        def begin():
            at = pl.ds(first, STEP)
            pltpu.make_async_copy(g_ref.at[:, :, :, at], gv.at[:, :, :, at], lsem.at[c]).wait()
            if c == chunks - 1:
                add_gains()
            for q in cubes:
                q[0]()

        def both(k):
            def run():
                for q in cubes:
                    q[k]()

            return run

        def meet():
            for q in cubes:
                q[bits]()
            z[0]()

        return [begin] + [both(k) for k in range(1, bits)] + [meet] + z[1:]

    def row_job(ref, recv, out, n):
        at = pl.ds(n * PIECE, PIECE)
        return line_scatter(nt, me_t, lambda b: ref.at[b, at], recv.at[:, at], out.at[at], sends, recvs, after)

    ticks = [SPACE * k for k in range(bits)] + [SPACE * bits + k for k in range(nt)]
    for c in range(chunks):
        jobs.append((min(c, chunks - 1), chunk_job(c), ticks))
    for n in range(e_out.shape[0] // PIECE):
        jobs.append((n, row_job(e_ref, ez, e_out, n), list(range(nt))))
    compute = [(CORE0, swapped), (CORE0, lambda: lax.fori_loop(0, heads, head, 0))]
    ready = CORE0 + 1
    compute += [(ready, partial(rows_end, i)) for i in range(nt)]
    compute.append((ready, finish))
    for tick, fn in compute:
        jobs.append((tick, [fn], [0]))
    a_job = cube_scatter(nd, me_d, orders[0], lambda d: a_ref.at[d], arecv, sends, recvs, after) + [a_done]
    jobs.append((ready + 1, a_job, [SPACE * k for k in range(bits + 1)] + [SPACE * bits]))
    for n in range(u_out.shape[0] // PIECE):
        jobs.append((ready + 1 + n, row_job(u_ref, uz, u_out, n), list(range(nt))))
    run_jobs(jobs, after)


def backward_all(nt, nd, heads, used, g, e, gain12, dmine, tok, wa, g0, segr, bl, tab, qkv, lse):
    bits = nd.bit_length() - 1
    rows, cols = g.shape[2:]
    block, width = tok.shape[1:]
    length = nt * block
    wide = wa.shape[1]
    hw = heads * DK
    chunks = cols // STEP
    lines = chunks + (block + e.shape[1]) // PIECE
    total = lines * 2 * nt + (2 * chunks + 1) * bits + nt - 1
    return pl.pallas_call(
        partial(backward_kernel, nt, nd, heads, used),
        out_shape=(
            jax.ShapeDtypeStruct((rows, cols), F32),
            jax.ShapeDtypeStruct((rows, wide), F32),
            jax.ShapeDtypeStruct((block, width), F32),
            jax.ShapeDtypeStruct(e.shape[1:], F32),
        ),
        in_specs=[ANY] + [VMEM] * 11,
        out_specs=(VMEM,) * 4,
        scratch_shapes=[
            pltpu.VMEM((nt, nd, rows, cols), BF),
            pltpu.VMEM((nt + 1, block, width), BF),
            pltpu.VMEM((nt + 1,) + e.shape[1:], BF),
            pltpu.VMEM((chunks, nt + 1, rows, STEP), BF),
        ]
        + [pltpu.VMEM((1 << (bits - 1 - k), rows, wide), BF) for k in range(bits)]
        + [pltpu.VMEM((2 * chunks, 1 << (bits - 1 - k), nt, rows, STEP // 2), BF) for k in range(bits)]
        + [
            pltpu.VMEM((nd, rows, wide), BF),
            pltpu.VMEM((nt, block, width), BF),
            pltpu.VMEM((nt, block, hw), BF),
            pltpu.VMEM((max(2 * block, 3 * hw), length + block), F32),
            pltpu.VMEM((length, DK), BF),
            pltpu.VMEM((length, DK), BF),
            pltpu.VMEM((length, DK), BF),
            pltpu.VMEM((length, DK), BF),
            pltpu.VMEM((DK, length), F32),
            pltpu.VMEM((DK, length), F32),
            pltpu.VMEM((length, 3 * hw), BF),
            pltpu.VMEM((8, length + block), F32),
            pltpu.VMEM((8, length + block), F32),
            pltpu.VMEM((1, width), F32),
            pltpu.SemaphoreType.DMA((total,)),
            pltpu.SemaphoreType.DMA((total,)),
            pltpu.SemaphoreType.DMA((chunks + 1,)),
        ],
        compiler_params=pltpu.CompilerParams(collective_id=1, has_side_effects=True, vmem_limit_bytes=LIMIT),
        name="backward_all",
    )(g, e, gain12, dmine, tok, wa, g0, segr, bl, tab, qkv, lse)


def column(row):
    return jnp.broadcast_to(row, (8, row.shape[1])).T[:, 0:1]


def build_strip(strip, x):
    block, width = strip.shape
    row = lax.broadcasted_iota(jnp.int32, (8, width), 0)
    x = jnp.broadcast_to(x, (8, width))
    for b in range(3):
        x = jnp.where((row >> b) % 2 == 1, pltpu.roll(x, 1 << b, 1), x)
    strip[0:8, :] = x
    n = 8
    while n < block:
        strip[n : 2 * n, :] = pltpu.roll(strip[0:n, :], n, 1)
        n *= 2


def bias_lines(bl_ref, tab_ref):
    width = bl_ref.shape[1]
    buckets = tab_ref.shape[1]
    hot = bl_ref[...] == lax.broadcasted_iota(jnp.int32, (buckets, width), 0)
    line = dot(tab_ref[...], hot.astype(F32).astype(BF))
    return jnp.where(bl_ref[...] >= 0, line, MASKED), hot


def middle_kernel(
    heads,
    ff,
    tok_ref,
    enc_ref,
    attn_ref,
    og_ref,
    gains_ref,
    w_hbm,
    layer_ref,
    one_ref,
    denc_ref,
    gain_ref,
    dattn_ref,
    g_hbm,
    w,
    g,
    h1_ref,
    h2_ref,
    n1_ref,
    n2_ref,
    acc_ref,
    dn_ref,
    g2_ref,
    denc,
    qc,
    kv,
    ac,
    oc,
    lse,
    dkv,
    insem,
    outsem,
):
    nt = w.shape[0]
    hw = heads * DK
    cols = w.shape[2]
    f0, f1, f2 = 0, ff, 2 * ff
    kv0 = 3 * ff
    q0 = kv0 + 2 * hw
    c0 = q0 + hw
    s0 = c0 + hw
    end = s0 + hw
    ffn = pl.ds(0, 3 * ff)
    att = pl.ds(3 * ff, cols - 3 * ff)
    loads = [pltpu.make_async_copy(w_hbm.at[t, :, att], w.at[t, :, att], insem.at[0, t]) for t in range(nt)]
    loads += [pltpu.make_async_copy(w_hbm.at[t, :, ffn], w.at[t, :, ffn], insem.at[1, t]) for t in range(nt)]
    for copy in loads:
        copy.start()

    def load_wait(which, t):
        at = att if which == 0 else ffn
        pltpu.make_async_copy(w_hbm.at[t, :, at], w.at[t, :, at], insem.at[which, t]).wait()

    def store(which, t):
        at = att if which == 0 else ffn
        return pltpu.make_async_copy(g.at[t, :, at], g_hbm.at[t, :, at], outsem.at[which, t])

    acc_ref[...] = tok_ref[...].astype(F32)

    def self_out(t, carry):
        load_wait(0, t)
        acc_ref[...] += dot_nt(attn_ref[t], w[t, :, s0:end])
        return carry

    lax.fori_loop(0, nt, self_out, 0)
    h1 = acc_ref[...]
    h1_ref[...] = h1
    n1_ref[...] = (h1 * norm_scale(h1) * gains_ref[1:2, :]).astype(BF)

    def cross(t, carry):
        q = dot(n1_ref[...], w[t, :, q0:c0]).astype(BF)
        both = dot(enc_ref[...], w[t, :, kv0:q0]).astype(BF)
        qc[t] = q
        kv[t] = both
        outs = []
        for h in range(heads):
            part = slice(h * DK, (h + 1) * DK)
            s = dot_nt(q[:, part], both[:, part])
            top = jnp.max(s, axis=-1, keepdims=True)
            p = jnp.exp(s - top)
            total = jnp.sum(p, axis=-1, keepdims=True)
            lse[t, h] = top + jnp.log(total)
            outs.append(dot(p.astype(BF), both[:, hw + h * DK : hw + (h + 1) * DK]) / total)
        a = jnp.concatenate(outs, axis=1).astype(BF)
        ac[t] = a
        acc_ref[...] += dot_nt(a, w[t, :, c0:s0])
        return carry

    lax.fori_loop(0, nt, cross, 0)
    h2 = acc_ref[...]
    h2_ref[...] = h2
    n2_ref[...] = (h2 * norm_scale(h2) * gains_ref[2:3, :]).astype(BF)
    dn_ref[...] = jnp.zeros_like(dn_ref)

    def units(t, carry):
        load_wait(1, t)
        n2 = n2_ref[...]
        og = og_ref[...]
        gate = dot(n2, w[t, :, f0:f1])
        up = dot(n2, w[t, :, f1:f2])
        dinner = dot(og, w[t, :, f2 : 3 * ff])
        sq = gate * gate
        th = jnp.tanh(0.7978845608028654 * (gate + 0.044715 * (gate * sq)))
        cdf = 0.5 * (1.0 + th)
        act = gate * cdf
        slope = cdf + gate * (0.5 * (1.0 - th * th)) * (0.7978845608028654 * (1.0 + 0.134145 * sq))
        inner = (act * up).astype(BF)
        dgate = (dinner * up * slope).astype(BF)
        dup = (dinner * act).astype(BF)
        acc_ref[...] += dot_nt(inner, w[t, :, f2 : 3 * ff])
        dn_ref[...] += dot_nt(dgate, w[t, :, f0:f1]) + dot_nt(dup, w[t, :, f1:f2])
        g[t, :, f0:f1] = dot_tn(n2, dgate).astype(BF)
        g[t, :, f1:f2] = dot_tn(n2, dup).astype(BF)
        g[t, :, f2 : 3 * ff] = dot_tn(og, inner).astype(BF)
        store(1, t).start()
        return carry

    lax.fori_loop(0, nt, units, 0)
    layer_ref[...] = acc_ref[...].astype(BF)
    h2 = h2_ref[...]
    back, gain2 = norm_back(h2, norm_scale(h2), gains_ref[2:3, :], dn_ref[...])
    g2 = og_ref[...].astype(F32) + back
    acc_ref[...] = g2
    g2_ref[...] = g2.astype(BF)
    dn_ref[...] = jnp.zeros_like(dn_ref)
    denc[...] = jnp.zeros_like(denc)

    def cross_back(t, carry):
        g2 = g2_ref[...]
        a = ac[t]
        da = dot(g2, w[t, :, c0:s0]).astype(BF)
        g[t, :, c0:s0] = dot_tn(g2, a).astype(BF)
        prod = da.astype(F32) * a.astype(F32)
        q = qc[t]
        both = kv[t]
        dqs = []
        for h in range(heads):
            part = slice(h * DK, (h + 1) * DK)
            qh, kh = q[:, part], both[:, part]
            vh, dah = both[:, hw + h * DK : hw + (h + 1) * DK], da[:, part]
            p = jnp.exp(dot_nt(qh, kh) - lse[t, h])
            delta = jnp.sum(prod[:, part], axis=1, keepdims=True)
            ds = (p * (dot_nt(dah, vh) - delta)).astype(BF)
            dqs.append(dot(ds, kh))
            dkv[h * DK : (h + 1) * DK, :] = dot_tn(qh, ds)
            dkv[hw + h * DK : hw + (h + 1) * DK, :] = dot_tn(dah, p.astype(BF))
        dq = jnp.concatenate(dqs, axis=1).astype(BF)
        dboth = dkv[...].astype(BF)
        g[t, :, q0:c0] = dot_tn(n1_ref[...], dq).astype(BF)
        g[t, :, kv0:q0] = lax.dot_general(
            enc_ref[...], dboth, (((0,), (1,)), ((), ())), preferred_element_type=F32
        ).astype(BF)
        dn_ref[...] += dot_nt(dq, w[t, :, q0:c0])
        denc[...] += lax.dot_general(
            dboth, w[t, :, kv0:q0], (((0,), (1,)), ((), ())), preferred_element_type=F32
        )
        return carry

    lax.fori_loop(0, nt, cross_back, 0)
    denc_ref[...] = denc[...].astype(BF)
    h1 = h1_ref[...]
    back, gain1 = norm_back(h1, norm_scale(h1), gains_ref[1:2, :], dn_ref[...])
    g1 = acc_ref[...] + back
    one_ref[...] = g1
    g2_ref[...] = g1.astype(BF)
    gain_ref[...] = jnp.concatenate([gain1, gain2, jnp.zeros((6, gain1.shape[1]), F32)], axis=0)

    def self_out_back(t, carry):
        low = g2_ref[...]
        dattn_ref[t] = dot(low, w[t, :, s0:end]).astype(BF)
        tail = dot_tn(low, attn_ref[t])
        g[t, :, s0:cols] = jnp.concatenate([tail, jnp.zeros((tail.shape[0], cols - end), F32)], axis=1).astype(BF)
        store(0, t).start()
        return carry

    lax.fori_loop(0, nt, self_out_back, 0)
    for t in range(nt):
        store(1, t).wait()
        store(0, t).wait()


def middle(heads, ff, tok, enc, attn, og, gains, w):
    nt, _, cols = w.shape
    rows, width = tok.shape
    states = enc.shape[0]
    hw = heads * DK
    return pl.pallas_call(
        partial(middle_kernel, heads, ff),
        out_shape=(
            jax.ShapeDtypeStruct((rows, width), BF),
            jax.ShapeDtypeStruct((rows, width), F32),
            jax.ShapeDtypeStruct((states, width), BF),
            jax.ShapeDtypeStruct((8, width), F32),
            jax.ShapeDtypeStruct((nt, rows, hw), BF),
            jax.ShapeDtypeStruct(w.shape, BF),
        ),
        in_specs=[VMEM] * 5 + [ANY],
        out_specs=(VMEM,) * 5 + (ANY,),
        scratch_shapes=[
            pltpu.VMEM(w.shape, BF),
            pltpu.VMEM(w.shape, BF),
            pltpu.VMEM((rows, width), F32),
            pltpu.VMEM((rows, width), F32),
            pltpu.VMEM((rows, width), BF),
            pltpu.VMEM((rows, width), BF),
            pltpu.VMEM((rows, width), F32),
            pltpu.VMEM((rows, width), F32),
            pltpu.VMEM((rows, width), BF),
            pltpu.VMEM((states, width), F32),
            pltpu.VMEM((nt, rows, hw), BF),
            pltpu.VMEM((nt, states, 2 * hw), BF),
            pltpu.VMEM((nt, rows, hw), BF),
            pltpu.VMEM((8, 128), F32),
            pltpu.VMEM((nt, heads, rows, 1), F32),
            pltpu.VMEM((2 * hw, states), F32),
            pltpu.SemaphoreType.DMA((2, nt)),
            pltpu.SemaphoreType.DMA((2, nt)),
        ],
        compiler_params=pltpu.CompilerParams(vmem_limit_bytes=LIMIT),
        name="middle",
    )(tok, enc, attn, og, gains, w)


def per_device(
    tokens,
    encoder,
    segments,
    rel_bucket,
    out_grad,
    self_q,
    self_k,
    self_v,
    self_o,
    cross_q,
    cross_k,
    cross_v,
    cross_o,
    ffn_gate,
    ffn_up,
    ffn_down,
    bias_table,
    norm_gains,
):
    nt, nd = lax.axis_size("tensor"), lax.axis_size("dp")
    part, hw = self_q.shape
    ff = ffn_gate.shape[1]
    heads = hw // DK
    rows, width = tokens.shape
    length = rows * nt
    buckets = bias_table.shape[0]
    wa = jnp.concatenate([self_q, self_k, self_v, jnp.pad(norm_gains.T, ((0, 0), (0, 128 - norm_gains.shape[0])))], axis=1)
    wb = jnp.concatenate([ffn_gate, ffn_up, ffn_down.T, cross_k, cross_v, cross_q, cross_o.T, self_o.T], axis=1)
    used = wb.shape[1]
    cols = -(-(used + 3) // STEP) * STEP
    wb = jnp.pad(wb, ((0, 0), (0, cols - used)))
    top = (nt - 1) * rows
    blank = jnp.full((length - 1 - top,), -1, jnp.int32)
    bl = jnp.concatenate(
        [rel_bucket[: top + 1][::-1], blank, jnp.full((1,), -1, jnp.int32), rel_bucket[top + 1 : length][::-1]]
    )[None, :]
    tab = jnp.pad(bias_table.T, ((0, 8 - heads), (0, 0)))
    segr = segments
    tok_all, enc_all, wb_all, wa_full, gains, qkv, lse, attn, mine = forward_all(
        nt, nd, heads, tokens, encoder, wa, wb, segr, bl, tab
    )
    wb_full = wb_all.reshape(nt, nd * part, cols)
    g0 = gains[0:1]
    layer_out, grad_one, denc, gain12, dmine, gb = middle(
        heads, ff, tokens, enc_all.reshape(nt * encoder.shape[0], width), mine, out_grad, gains, wb_full
    )
    gsum, asum, usum, esum = backward_all(
        nt,
        nd,
        heads,
        used,
        gb.reshape(nt, nd, part, cols),
        denc.reshape((nt,) + encoder.shape),
        gain12,
        dmine,
        tok_all,
        wa_full,
        g0,
        segr,
        bl,
        tab,
        qkv,
        lse,
    )
    x = tokens.astype(F32)
    back, _ = norm_back(x, norm_scale(x), g0, usum)
    tokens_grad = grad_one + back
    at = 3 * ff
    ck, cv, cq, co, so = (gsum[:, at + n * hw : at + (n + 1) * hw] for n in range(5))
    return (
        layer_out,
        tokens_grad,
        esum,
        asum[:, :hw],
        asum[:, hw : 2 * hw],
        asum[:, 2 * hw : 3 * hw],
        so.T,
        cq,
        ck,
        cv,
        co.T,
        gsum[:, :ff],
        gsum[:, ff : 2 * ff],
        gsum[:, 2 * ff : 3 * ff].T,
        asum[:heads, 3 * hw : 3 * hw + buckets].T,
        gsum[:, used : used + 3].T,
    )


def solution(mesh):
    rows = P(("dp", "tensor"), None)
    left = P("dp", "tensor")
    right = P("tensor", "dp")
    return jax.shard_map(
        per_device,
        mesh=mesh,
        in_specs=(rows, rows, P("dp", None), P(), rows, left, left, left, right, left, left, left, right, left, left, right)
        + (P(None, "tensor"), P(None, "dp")),
        out_specs=(rows, rows, rows, left, left, left, right, left, left, left, right, left, left, right)
        + (P(None, "tensor"), P(None, "dp")),
        check_vma=False,
    )
```
